128 devices in a mesh: row: 16 (over x_hi, z, core), col: 8 (over y, x_lo).
Axes of the slice: x: 4 (x_hi: 2, x_lo: 2; x = x_hi * 2 + x_lo), y: 4, z: 4, core: 2. Of those that a mesh axis runs over, the one named last changes fastest.
Arguments:
- buoy: bfloat16 [512, 512, 384], P('row', 'col'), may hold values from -6 to 6
- vel_w: bfloat16 [512, 512, 384], P('row', 'col'), may hold values from -6 to 6
- strat: float32 [576], P('col'), may hold values from 0.3 to 3
- eig_val: float32 [384], replicated, may hold values from 0.1 to 8
- eig_left: bfloat16 [384, 384], replicated, may hold values from -0.3125 to 0.3125
- eig_right: bfloat16 [384, 384], replicated, may hold values from -0.3125 to 0.3125
Outputs:
- new_buoy: bfloat16 [512, 512, 384], P('row', 'col')
- new_vel: bfloat16 [512, 512, 384], P('row', 'col')
The draws below stay inside these ranges and needn't reach their ends.
All inputs are finite; a program needn't handle non-finite values.
Results may differ from the reference program's by a relative error of at most 0.019.
The reference program's roundings to bfloat16 on the way count: a program that leaves them out, or rounds other values in their place, can miss the bound.
Values may be sent and summed in bfloat16 or wider, within the bound.
A program may use at most 128 MiB of HBM per device.

```python
import math
import jax
import jax.numpy as jnp
from jax import lax

KX = 512
KY = 512
NZ = 384
XG = 768
YG = 768
ZG = 576


def shard_levels(own_key, extent, split, smallest, high):
    factor_of, own = 1.0, jax.random.fold_in(own_key, 6)
    for position, parts in split:
        steps = jnp.exp(jax.random.uniform(jax.random.fold_in(own, position), (parts,), jnp.float32, smallest / len(split), high / len(split)))
        factor_of = factor_of * jnp.repeat(steps, extent[position] // parts).reshape([-1 if axis == position else 1 for axis in range(len(extent))])
    return factor_of


def bell_draw(rng, dims, scale, reach, split=(), kind=jnp.bfloat16):
    values = scale * jax.random.normal(rng, dims, jnp.float32)
    if split:
        values = values * shard_levels(rng, dims, split, -0.22, 0.18)
    return jnp.clip(values, -reach, reach).astype(kind)


def setup_inputs(seed: int = 0) -> dict:
    key_list = jax.random.split(jax.random.key(seed), 7)
    buoy = bell_draw(key_list[0], (KX, KY, NZ), 1.0, 6.0, ((0, 16), (1, 8)))
    vel_w = bell_draw(key_list[1], (KX, KY, NZ), 1.0, 6.0, ((0, 16), (1, 8)))
    strat = jnp.clip(jnp.exp(math.log(3.0) - 2.3025851 * jax.random.uniform(key_list[2], (ZG,), jnp.float32) ** shard_levels(key_list[2], (ZG,), ((0, 8),), -0.2, 0.2)), 0.3, 3.0)
    eig_val = jnp.clip(jnp.exp(jax.random.uniform(key_list[3], (NZ,), jnp.float32, math.log(0.1), math.log(8.0))), 0.1, 8.0)
    eig_left = bell_draw(key_list[4], (NZ, NZ), NZ ** -0.5, 0.3125)
    eig_right = bell_draw(key_list[5], (NZ, NZ), NZ ** -0.5, 0.3125)
    return dict(buoy=buoy, vel_w=vel_w, strat=strat, eig_val=eig_val, eig_left=eig_left, eig_right=eig_right)


explicit_step = 0.5
diffuse_buoy = 0.5
diffuse_vel = 0.25
couple_buoy = 0.7
couple_vel = 0.7

def rounded(values):
    return lax.optimization_barrier(values.astype(jnp.bfloat16)).astype(jnp.float32)

def fourier_trig(modes, points):
    order = jnp.arange(modes, dtype=jnp.int32)
    freq = ((order + 1) // 2).astype(jnp.float32)
    place = jnp.arange(points, dtype=jnp.float32)
    angle = 2.0 * math.pi / points * freq[:, None] * place[None, :]
    return (order, jnp.where((order % 2 == 0)[:, None], jnp.cos(angle), jnp.sin(angle)))

def fourier_eval(modes, points):
    order, values = fourier_trig(modes, points)
    return (values * math.sqrt(2.0 / modes)).astype(jnp.bfloat16)

def fourier_proj(modes, points):
    order, values = fourier_trig(modes, points)
    weight = jnp.where(order == 0, 1.0 / points, 2.0 / points).astype(jnp.float32)
    return jnp.transpose(values * weight[:, None] * math.sqrt(modes / 2.0)).astype(jnp.bfloat16)

def cheb_tables(degree, points):
    order = jnp.arange(degree, dtype=jnp.float32)
    theta = math.pi * (jnp.arange(points, dtype=jnp.float32) + 0.5) / points
    angle = order[:, None] * theta[None, :]
    norm = math.sqrt(2.0 / degree)
    levels = jnp.cos(angle) * norm
    slopes = -(order[:, None] / degree) * jnp.sin(angle) * norm
    weight = jnp.where(order == 0, 1.0 / points, 2.0 / points).astype(jnp.float32)
    projector = jnp.transpose(jnp.cos(angle) * weight[:, None] * math.sqrt(degree / 2.0))
    return (levels.astype(jnp.bfloat16), slopes.astype(jnp.bfloat16), projector.astype(jnp.bfloat16))

def wave_squares(modes):
    order = jnp.arange(modes, dtype=jnp.int32)
    freq = ((order + 1) // 2).astype(jnp.float32) * (2.0 / modes)
    return freq * freq

def mult(form, left, right):
    return jnp.einsum(form, left, right, precision=lax.Precision.HIGHEST)

def reference(buoy, vel_w, strat, eig_val, eig_left, eig_right):
    levels, slopes, projector = cheb_tables(NZ, ZG)
    along_y = fourier_eval(KY, YG).astype(jnp.float32)
    along_x = fourier_eval(KX, XG).astype(jnp.float32)
    back_x = fourier_proj(KX, XG).astype(jnp.float32)
    back_y = fourier_proj(KY, YG).astype(jnp.float32)
    vel_full = vel_w.astype(jnp.float32)
    buoy_full = buoy.astype(jnp.float32)
    depth = ZG // 8

    def slab(carry, block):
        start = (block * depth).astype(jnp.int32)
        level_part = lax.dynamic_slice_in_dim(levels, start, depth, 1).astype(jnp.float32)
        slope_part = lax.dynamic_slice_in_dim(slopes, start, depth, 1).astype(jnp.float32)
        proj_part = lax.dynamic_slice_in_dim(projector, start, depth, 0).astype(jnp.float32)
        strata = lax.dynamic_slice_in_dim(strat, start, depth, 0)
        field_list = []
        for coeffs, lookup in ((vel_full, level_part), (buoy_full, slope_part)):
            upper = rounded(mult('xyn,nz->xyz', coeffs, lookup))
            middle = rounded(mult('xkz,ky->xyz', upper, along_y))
            field_list.append(rounded(mult('kyz,kx->xyz', middle, along_x)))
        vel_grid, slope_grid = field_list
        flux_buoy = rounded(-(vel_grid * slope_grid) - strata[None, None, :] * vel_grid)
        flux_vel = rounded(-(vel_grid * jnp.abs(vel_grid)))
        totals = []
        for flux, total in ((flux_buoy, carry[0]), (flux_vel, carry[1])):
            partial_x = rounded(mult('xyz,xk->kyz', flux, back_x))
            partial_y = rounded(mult('kyz,yl->klz', partial_x, back_y))
            totals.append(total + mult('klz,zn->kln', partial_y, proj_part))
        return ((totals[0], totals[1]), None)
    zeros = jnp.zeros((KX, KY, NZ), jnp.float32)
    (tend_buoy, tend_vel), _ = lax.scan(slab, (zeros, zeros), jnp.arange(ZG // depth, dtype=jnp.int32))
    rhs_buoy = rounded(buoy_full + explicit_step * tend_buoy)
    rhs_vel = rounded(vel_full + explicit_step * tend_vel)
    left_matrix = eig_left.astype(jnp.float32)
    modal_buoy = mult('xyn,nj->xyj', rhs_buoy, left_matrix)
    modal_vel = mult('xyn,nj->xyj', rhs_vel, left_matrix)
    lapl = 4.0 * (wave_squares(KX)[:, None, None] + wave_squares(KY)[None, :, None]) + eig_val[None, None, :]
    diag_buoy = 1.0 + diffuse_buoy * lapl
    diag_vel = 1.0 + diffuse_vel * lapl
    determ = diag_buoy * diag_vel + couple_buoy * couple_vel
    solved_buoy = rounded((diag_vel * modal_buoy - couple_buoy * modal_vel) / determ)
    solved_vel = rounded((diag_buoy * modal_vel + couple_vel * modal_buoy) / determ)
    right_matrix = eig_right.astype(jnp.float32)
    new_buoy = mult('xyj,jn->xyn', solved_buoy, right_matrix).astype(jnp.bfloat16)
    new_vel = mult('xyj,jn->xyn', solved_vel, right_matrix).astype(jnp.bfloat16)
    return (new_buoy, new_vel)
```

```python
import functools
import math

import jax
import jax.numpy as jnp
import numpy as np
from jax import lax
from jax.experimental import pallas as pl
from jax.experimental.pallas import tpu as pltpu
from jax.sharding import PartitionSpec as P

KX = 512
KY = 512
NZ = 384
XG = 768
YG = 768
ZG = 576

explicit_step = 0.5
diffuse_buoy = 0.5
diffuse_vel = 0.25
couple_buoy = 0.7
couple_vel = 0.7

ROWS = 16
COLS = 8
A = KX // ROWS
K = KY // COLS
PAIRS = A // 2
LANES = 2 * K
G = 3
ZPART = ZG // COLS
ZC = ZPART // G
ZI = 3
YH = YG // 2
BF = jnp.bfloat16
F32 = jnp.float32
MESH = pl.DeviceIdType.MESH
VMEM_LIMIT = 66_500_000


def trig(modes, points):
    order = np.arange(modes)
    freq = ((order + 1) // 2).astype(np.float32)
    step = np.float32(2.0 * math.pi / points)
    angle = (step * freq)[:, None] * np.arange(points, dtype=np.float32)[None, :]
    angle = angle.astype(np.float64)
    values = np.where((order % 2 == 0)[:, None], np.cos(angle), np.sin(angle))
    return order, values.astype(np.float32)


def fourier_eval(modes, points):
    _, values = trig(modes, points)
    return (values * np.float32(math.sqrt(2.0 / modes))).astype(BF)


def fourier_proj(modes, points):
    order, values = trig(modes, points)
    weight = np.where(order == 0, 1.0 / points, 2.0 / points).astype(np.float32)
    return (values * weight[:, None] * np.float32(math.sqrt(modes / 2.0))).T.astype(BF)


def cheb_tables(degree, points):
    order = np.arange(degree, dtype=np.float32)
    theta = np.float32(math.pi) * (np.arange(points, dtype=np.float32) + np.float32(0.5))
    theta = theta / np.float32(points)
    angle = (order[:, None] * theta[None, :]).astype(np.float64)
    cos, sin = np.cos(angle).astype(np.float32), np.sin(angle).astype(np.float32)
    norm = np.float32(math.sqrt(2.0 / degree))
    weight = np.where(order == 0, 1.0 / points, 2.0 / points).astype(np.float32)
    levels = cos * norm
    slopes = -(order[:, None] / np.float32(degree)) * sin * norm
    projector = (cos * weight[:, None] * np.float32(math.sqrt(degree / 2.0))).T
    return levels.astype(BF), slopes.astype(BF), projector.astype(BF)


def tables():
    levels, slopes, projector = cheb_tables(NZ, ZG)

    def by_chunk(rows):
        parts = np.asarray(rows).reshape(COLS, G, ZC, NZ).transpose(1, 0, 2, 3)
        return np.ascontiguousarray(parts)

    lift = by_chunk(levels.T).reshape(G, COLS * ZC, NZ)
    slope = by_chunk(slopes.T).reshape(G, COLS * ZC, NZ)
    drop = by_chunk(projector).reshape(ZG, NZ)
    place = np.arange(KX).reshape(ROWS, PAIRS, 2).transpose(0, 2, 1).reshape(-1)
    eval_y = np.asarray(fourier_eval(KY, YG))
    proj_y = np.asarray(fourier_proj(KY, YG))
    eval_x = np.ascontiguousarray(np.asarray(fourier_eval(KX, XG)).T[:, place])
    proj_x = np.ascontiguousarray(np.asarray(fourier_proj(KX, XG)).T[place, :])
    return lift, slope, drop, eval_y, proj_y, eval_x, proj_x


def mm(left, right, dims=((1,), (0,))):
    return lax.dot_general(left, right, (dims, ((), ())), preferred_element_type=F32)


def kernel(
    vel, buoy, lift, slope, drop, eval_y, proj_y, eval_x, proj_x, strata, eig_val, eig_left, eig_right,
    out_buoy, out_vel,
    lifted, arrived, spread, grid, returned, folded, tall, wide_eval, wide_proj, flux, strata_all,
    colf_s, colf_r, rowf_s, rowf_r, rowb_s, rowb_r, colb_s, colb_r, strat_s, strat_r,
):
    row, col = lax.axis_index("row"), lax.axis_index("col")
    high = row // (ROWS // 2)
    base, low = (col // 2) * 2, col % 2
    part = base + (low + high) % 2

    def col_of(q):
        return (row, (q // 2) * 2 + (q % 2 + high) % 2)

    def row_of(t):
        return (t, base + (low + high + t // (ROWS // 2)) % 2)

    barrier = pltpu.get_barrier_semaphore()

    @pl.loop(1, COLS)
    def _(i):
        pl.semaphore_signal(barrier, inc=1, device_id=col_of((part + i) % COLS), device_id_type=MESH)

    @pl.loop(1, ROWS)
    def _(i):
        pl.semaphore_signal(barrier, inc=1, device_id=row_of((row + i) % ROWS), device_id_type=MESH)

    pl.semaphore_wait(barrier, COLS + ROWS - 2)

    def remote(src, dst, send, recv, device):
        return pltpu.make_async_remote_copy(
            src_ref=src, dst_ref=dst, send_sem=send, recv_sem=recv, device_id=device, device_id_type=MESH
        )

    swap = remote(strata, strata_all.at[1], strat_s, strat_r, (row, base + 1 - low))
    swap.start()
    strata_all[0] = strata[...]

    def col_fwd(g, q):
        return remote(lifted.at[g, q], arrived.at[g, col], colf_s.at[g, q], colf_r.at[g, col], col_of(q))

    def col_fwd_in(g, s):
        block = arrived.at[g, s]
        return remote(block, block, colf_s.at[g, s], colf_r.at[g, s], col_of(0))

    def col_fwd_own(g):
        return pltpu.make_async_copy(lifted.at[g, part], arrived.at[g, col], colf_r.at[g, col])

    def row_fwd(g, t):
        mine = pl.ds(pl.multiple_of(row * A, A), A)
        return remote(spread.at[g, t], grid.at[g, :, :, mine, :], rowf_s.at[g, t], rowf_r.at[g, row], row_of(t))

    def row_fwd_in(g, t):
        block = grid.at[g, :, :, pl.ds(pl.multiple_of(t * A, A), A), :]
        return remote(block, block, rowf_s.at[g, t], rowf_r.at[g, t], row_of(t))

    def row_fwd_own(g):
        mine = pl.ds(pl.multiple_of(row * A, A), A)
        return pltpu.make_async_copy(spread.at[g, row], grid.at[g, :, :, mine, :], rowf_r.at[g, row])

    def row_back(g, t):
        theirs = pl.ds(pl.multiple_of(t * A, A), A)
        return remote(grid.at[g, :, :, theirs, :], returned.at[g, row], rowb_s.at[g, t], rowb_r.at[g, row], row_of(t))

    def row_back_in(g, t):
        block = returned.at[g, t]
        return remote(block, block, rowb_s.at[g, t], rowb_r.at[g, t], row_of(t))

    def row_back_own(g):
        mine = pl.ds(pl.multiple_of(row * A, A), A)
        return pltpu.make_async_copy(grid.at[g, :, :, mine, :], returned.at[g, row], rowb_r.at[g, row])

    def col_back(g, s):
        return remote(arrived.at[g, s], folded.at[g, part], colb_s.at[g, s], colb_r.at[g, part], (row, s))

    def col_back_in(g, q):
        block = folded.at[g, q]
        return remote(block, block, colb_s.at[g, q], colb_r.at[g, q], col_of(q))

    def col_back_own(g):
        return pltpu.make_async_copy(arrived.at[g, col], folded.at[g, part], colb_r.at[g, part])

    def others(first, count, do):
        @pl.loop(1, count)
        def _(i):
            do((first + i) % count)

    half = COLS * ZC * PAIRS

    @pl.loop(0, G)
    def _(g):
        @pl.loop(0, PAIRS)
        def _(p):
            rows = pl.ds(pl.multiple_of(p * LANES, LANES), LANES)
            tall[pl.ds(p, COLS * ZC, stride=PAIRS), :] = mm(lift[g], vel[rows, :], ((1,), (1,)))
            tall[pl.ds(half + p, COLS * ZC, stride=PAIRS), :] = mm(slope[g], buoy[rows, :], ((1,), (1,)))

        size = ZC * PAIRS

        @pl.loop(0, COLS)
        def _(q):
            for f in range(2):
                rows = pl.ds(pl.multiple_of(q * size + f * half, size), size)
                lifted[g, q, f] = tall[rows, :].astype(BF)

        others(part, COLS, lambda q: col_fwd(g, q).start())
        col_fwd_own(g).start()

    @pl.loop(0, COLS)
    def _(s):
        for a in range(2):
            for h in range(2):
                own = pl.ds(pl.multiple_of(s * LANES + a * K, K), K)
                other = pl.ds(pl.multiple_of(s * LANES + (1 - a) * K, K), K)
                wide_eval[a * 2 + h, own, :] = eval_y[pl.ds(pl.multiple_of(s * K, K), K), h * YH : (h + 1) * YH]
                wide_eval[a * 2 + h, other, :] = jnp.zeros((K, YH), BF)

    @pl.loop(0, G)
    def _(g):
        others(col, COLS, lambda s: col_fwd_in(g, s).wait_recv())
        col_fwd_own(g).wait()

        @pl.loop(0, 2)
        def _(f):
            left = jnp.concatenate([arrived[g, s, f] for s in range(COLS)], axis=1)
            for a in range(2):
                for h in range(2):
                    values = mm(left, wide_eval[a * 2 + h]).astype(BF)
                    spread[g, h * 8 : (h + 1) * 8, f, :, a * PAIRS : (a + 1) * PAIRS, :] = values.reshape(
                        8, ZI, PAIRS, YH
                    )

        others(row, ROWS, lambda t: row_fwd(g, t).start())
        row_fwd_own(g).start()

    lane = lax.broadcasted_iota(jnp.int32, (YG, LANES), 1)
    for j in range(COLS // 2):
        tile = proj_y[:, j * LANES : (j + 1) * LANES].astype(F32)
        turned = pltpu.roll(tile, K, 1)
        for s in (2 * j, 2 * j + 1):
            straight, moved = (tile, turned) if s % 2 == 0 else (turned, tile)
            for a in range(2):
                keep = jnp.where((lane < K) == (a == 0), straight if a == 0 else moved, 0.0).astype(BF)
                wide_proj[s // 4, a * YG : (a + 1) * YG, (s % 4) * LANES : (s % 4 + 1) * LANES] = keep

    swap.wait()

    @pl.loop(0, G)
    def _(g):
        others(row, ROWS, lambda t: row_fwd_in(g, t).wait_recv())
        row_fwd_own(g).wait()

        @pl.loop(0, ZI)
        def _(i):
            level = strata_all[high, pl.ds(g * ZC + (row % 8) * ZI + i, 1), :]
            tile = XG // 3
            for x in range(3):
                rows = slice(x * tile, (x + 1) * tile)
                velocity = mm(eval_x[rows, :], grid[g, 0, i]).astype(BF).astype(F32)
                gradient = mm(eval_x[rows, :], grid[g, 1, i]).astype(BF).astype(F32)
                flux[0, rows, :] = (-(velocity * gradient) - level * velocity).astype(BF)
                flux[1, rows, :] = (-(velocity * jnp.abs(velocity))).astype(BF)
            for f in range(2):
                grid[g, f, i] = mm(proj_x[...], flux[f]).astype(BF)

        others(row, ROWS, lambda t: row_back(g, t).start())
        row_back_own(g).start()

    @pl.loop(0, G)
    def _(g):
        others(row, ROWS, lambda t: row_back_in(g, t).wait_recv())
        row_back_own(g).wait()

        @pl.loop(0, 2)
        def _(f):
            left = jnp.concatenate(
                [
                    returned[g, h * 8 : (h + 1) * 8, f, :, a * PAIRS : (a + 1) * PAIRS, :].reshape(ZC * PAIRS, YH)
                    for a in range(2)
                    for h in range(2)
                ],
                axis=1,
            )
            for h in range(2):
                values = mm(left, wide_proj[h]).astype(BF)
                for s in range(4):
                    arrived[g, 4 * h + s, f] = values[:, s * LANES : (s + 1) * LANES]

        others(col, COLS, lambda s: col_back(g, s).start())
        col_back_own(g).start()

    for g in range(G):
        others(part, COLS, lambda q: col_back_in(g, q).wait_recv())
        col_back_own(g).wait()

    for f, (field, out) in enumerate(((buoy, out_buoy), (vel, out_vel))):
        size = ZC * PAIRS

        @pl.loop(0, G * COLS)
        def _(i):
            tall[pl.ds(pl.multiple_of(i * size, size), size), :] = folded[i // COLS, i % COLS, f].astype(F32)

        @pl.loop(0, PAIRS)
        def _(p):
            rows = pl.ds(pl.multiple_of(p * LANES, LANES), LANES)
            column = tall[pl.ds(p, ZG, stride=PAIRS), :].astype(BF)
            tend = mm(column, drop[...], ((0,), (0,)))
            out[rows, :] = (field[rows, :].astype(F32) + explicit_step * tend).astype(BF)

    block = 256

    @pl.loop(0, A * K // block)
    def _(i):
        rows = pl.ds(pl.multiple_of(i * block, block), block)
        modal_buoy = mm(out_buoy[rows, :], eig_left[...])
        modal_vel = mm(out_vel[rows, :], eig_left[...])
        place = i * block + lax.broadcasted_iota(jnp.int32, (block, NZ), 0)
        freq_x = ((row * A + place // K + 1) // 2).astype(F32) * (2.0 / KX)
        freq_y = ((col * K + place % K + 1) // 2).astype(F32) * (2.0 / KY)
        lapl = 4.0 * (freq_x * freq_x + freq_y * freq_y) + eig_val[...]
        diag_buoy = 1.0 + diffuse_buoy * lapl
        diag_vel = 1.0 + diffuse_vel * lapl
        inverse = 1.0 / (diag_buoy * diag_vel + couple_buoy * couple_vel)
        solved_buoy = ((diag_vel * modal_buoy - couple_buoy * modal_vel) * inverse).astype(BF)
        solved_vel = ((diag_buoy * modal_vel + couple_vel * modal_buoy) * inverse).astype(BF)
        out_buoy[rows, :] = mm(solved_buoy, eig_right[...]).astype(BF)
        out_vel[rows, :] = mm(solved_vel, eig_right[...]).astype(BF)

    @pl.loop(0, G)
    def _(g):
        others(part, COLS, lambda q: col_fwd(g, q).wait_send())
        others(row, ROWS, lambda t: row_fwd(g, t).wait_send())
        others(row, ROWS, lambda t: row_back(g, t).wait_send())
        others(col, COLS, lambda s: col_back(g, s).wait_send())


def per_device(buoy, vel_w, strat, eig_val, eig_left, eig_right):
    modes = A * K
    dma = pltpu.SemaphoreType.DMA
    strata = jnp.broadcast_to(strat[:, None], (ZPART, YH))
    vmem = pl.BlockSpec(memory_space=pltpu.VMEM)
    shape = jax.ShapeDtypeStruct((modes, NZ), BF)
    size = ZC * PAIRS
    consts = [jnp.asarray(t) for t in tables()]
    new_buoy, new_vel = pl.pallas_call(
        kernel,
        out_shape=(shape, shape),
        in_specs=[vmem] * 13,
        out_specs=(vmem, vmem),
        scratch_shapes=[
            pltpu.VMEM((G, COLS, 2, size, LANES), BF),
            pltpu.VMEM((G, COLS, 2, size, LANES), BF),
            pltpu.VMEM((G, ROWS, 2, ZI, A, YH), BF),
            pltpu.VMEM((G, 2, ZI, KX, YH), BF),
            pltpu.VMEM((G, ROWS, 2, ZI, A, YH), BF),
            pltpu.VMEM((G, COLS, 2, size, LANES), BF),
            pltpu.VMEM((ZG * PAIRS, LANES), F32),
            pltpu.VMEM((4, COLS * LANES, YH), BF),
            pltpu.VMEM((2, 2 * YG, COLS * LANES // 2), BF),
            pltpu.VMEM((2, XG, YH), BF),
            pltpu.VMEM((2, ZPART, YH), F32),
            dma((G, COLS)), dma((G, COLS)), dma((G, ROWS)), dma((G, ROWS)),
            dma((G, ROWS)), dma((G, ROWS)), dma((G, COLS)), dma((G, COLS)),
            dma, dma,
        ],
        compiler_params=pltpu.CompilerParams(
            collective_id=0, has_side_effects=True, vmem_limit_bytes=VMEM_LIMIT
        ),
        name="section",
    )(
        vel_w.reshape(modes, NZ), buoy.reshape(modes, NZ), *consts, strata,
        eig_val.reshape(1, NZ), eig_left, eig_right,
    )
    return new_buoy.reshape(buoy.shape), new_vel.reshape(buoy.shape)


def solution(mesh):
    in_specs = (P("row", "col", None), P("row", "col", None), P("col"), P(), P(), P())
    out_specs = (P("row", "col", None), P("row", "col", None))
    return jax.shard_map(
        per_device, mesh=mesh, in_specs=in_specs, out_specs=out_specs, check_vma=False
    )
```

```python
import functools
import math

import jax
import jax.numpy as jnp
import numpy as np
from jax import lax
from jax.experimental import pallas as pl
from jax.experimental.pallas import tpu as pltpu
from jax.sharding import PartitionSpec as P

KX = 512
KY = 512
NZ = 384
XG = 768
YG = 768
ZG = 576

explicit_step = 0.5
diffuse_buoy = 0.5
diffuse_vel = 0.25
couple_buoy = 0.7
couple_vel = 0.7

ROWS = 16
COLS = 8
A = KX // ROWS
K = KY // COLS
PAIRS = A // 2
LANES = 2 * K
G = 9
ZPART = ZG // COLS
ZC = ZPART // G
SIZE = ZC * PAIRS
YH = YG // 2
TWO = 2 * LANES
TALL = ZG * PAIRS // 2
ENDS = (4, 7, 9)
BF = jnp.bfloat16
F32 = jnp.float32
MESH = pl.DeviceIdType.MESH
VMEM_LIMIT = 67_000_000


def trig(modes, points):
    order = np.arange(modes)
    freq = ((order + 1) // 2).astype(np.float32)
    step = np.float32(2.0 * math.pi / points)
    angle = (step * freq)[:, None] * np.arange(points, dtype=np.float32)[None, :]
    angle = angle.astype(np.float64)
    values = np.where((order % 2 == 0)[:, None], np.cos(angle), np.sin(angle))
    return order, values.astype(np.float32)


def fourier_eval(modes, points):
    _, values = trig(modes, points)
    return (values * np.float32(math.sqrt(2.0 / modes))).astype(BF)


def fourier_proj(modes, points):
    order, values = trig(modes, points)
    weight = np.where(order == 0, 1.0 / points, 2.0 / points).astype(np.float32)
    return (values * weight[:, None] * np.float32(math.sqrt(modes / 2.0))).T.astype(BF)


def cheb_tables(degree, points):
    order = np.arange(degree, dtype=np.float32)
    theta = np.float32(math.pi) * (np.arange(points, dtype=np.float32) + np.float32(0.5))
    theta = theta / np.float32(points)
    angle = (order[:, None] * theta[None, :]).astype(np.float64)
    cos, sin = np.cos(angle).astype(np.float32), np.sin(angle).astype(np.float32)
    norm = np.float32(math.sqrt(2.0 / degree))
    weight = np.where(order == 0, 1.0 / points, 2.0 / points).astype(np.float32)
    levels = cos * norm
    slopes = -(order[:, None] / np.float32(degree)) * sin * norm
    projector = (cos * weight[:, None] * np.float32(math.sqrt(degree / 2.0))).T
    return levels.astype(BF), slopes.astype(BF), projector.astype(BF)


def tables():
    levels, slopes, projector = cheb_tables(NZ, ZG)
    drop = np.asarray(projector).reshape(COLS, G, ZC, NZ).transpose(1, 0, 2, 3).reshape(ZG, NZ)
    lift, slope = (np.ascontiguousarray(np.asarray(t).T) for t in (levels, slopes))
    return lift, slope, np.ascontiguousarray(drop), fourier_eval(KY, YG), np.ascontiguousarray(fourier_proj(KY, YG))


def mm(left, right, dims=((1,), (0,))):
    return lax.dot_general(left, right, (dims, ((), ())), preferred_element_type=F32)


def kernel(
    vel, buoy, lift, slope, drop, evals, projs, strat, eig_val, eig_left, eig_right,
    out_buoy, out_vel,
    lifted, arrived, spread, grid, returned, folded, tall, wide_eval, wide_proj, eval_x, proj_x, flux, partial,
    strat_in,
    colf_s, colf_r, rowf_s, rowf_r, rowb_s, rowb_r, colb_s, colb_r, strat_s, strat_r,
):
    row, col = lax.axis_index("row"), lax.axis_index("col")
    high = row // (ROWS // 2)
    base, low = (col // 2) * 2, col % 2
    part = base + (low + high) % 2

    def col_of(q):
        return (row, (q // 2) * 2 + (q % 2 + high) % 2)

    def row_of(t):
        return (t, base + (low + high + t // (ROWS // 2)) % 2)

    barrier = pltpu.get_barrier_semaphore()

    @pl.loop(1, COLS)
    def _(i):
        pl.semaphore_signal(barrier, inc=1, device_id=col_of((part + i) % COLS), device_id_type=MESH)

    @pl.loop(1, ROWS)
    def _(i):
        pl.semaphore_signal(barrier, inc=1, device_id=row_of((row + i) % ROWS), device_id_type=MESH)

    pl.semaphore_wait(barrier, COLS + ROWS - 2)

    def remote(src, dst, send, recv, device):
        return pltpu.make_async_remote_copy(
            src_ref=src, dst_ref=dst, send_sem=send, recv_sem=recv, device_id=device, device_id_type=MESH
        )

    swap = remote(strat, strat_in, strat_s, strat_r, (row, base + 1 - low))
    swap.start()

    def col_fwd(g, q):
        return remote(lifted.at[g, q], arrived.at[g, col], colf_s.at[g, q], colf_r.at[g, col], col_of(q))

    def col_fwd_in(g, s):
        block = arrived.at[g, s]
        return remote(block, block, colf_s.at[g, s], colf_r.at[g, s], col_of(0))

    def col_fwd_own(g):
        return pltpu.make_async_copy(lifted.at[g, part], arrived.at[g, col], colf_r.at[g, col])

    def row_fwd(g, t):
        mine = pl.ds(pl.multiple_of(row * A, A), A)
        return remote(spread.at[g, t], grid.at[g, :, mine, :], rowf_s.at[g, t], rowf_r.at[g, row], row_of(t))

    def row_fwd_in(g, t):
        block = grid.at[g, :, pl.ds(pl.multiple_of(t * A, A), A), :]
        return remote(block, block, rowf_s.at[g, t], rowf_r.at[g, t], row_of(t))

    def row_fwd_own(g):
        mine = pl.ds(pl.multiple_of(row * A, A), A)
        return pltpu.make_async_copy(spread.at[g, row], grid.at[g, :, mine, :], rowf_r.at[g, row])

    def row_back(g, t):
        theirs = pl.ds(pl.multiple_of(t * A, A), A)
        return remote(grid.at[g, :, theirs, :], returned.at[g, row], rowb_s.at[g, t], rowb_r.at[g, row], row_of(t))

    def row_back_in(g, t):
        block = returned.at[g, t]
        return remote(block, block, rowb_s.at[g, t], rowb_r.at[g, t], row_of(t))

    def row_back_own(g):
        mine = pl.ds(pl.multiple_of(row * A, A), A)
        return pltpu.make_async_copy(grid.at[g, :, mine, :], returned.at[g, row], rowb_r.at[g, row])

    def col_back(g, s):
        return remote(arrived.at[g, s], folded.at[g, part], colb_s.at[g, s], colb_r.at[g, part], (row, s))

    def col_back_in(g, q):
        block = folded.at[g, q]
        return remote(block, block, colb_s.at[g, q], colb_r.at[g, q], col_of(q))

    def col_back_own(g):
        return pltpu.make_async_copy(arrived.at[g, col], folded.at[g, part], colb_r.at[g, part])

    def others(first, count, do):
        @pl.loop(1, count)
        def _(i):
            do((first + i) % count)

    @pl.loop(0, 2)
    def _(side):
        count = ZG // 2
        points = pl.ds(pl.multiple_of(side * count, count), count)
        for f, (table, field) in enumerate(((lift, vel), (slope, buoy))):

            @pl.loop(0, PAIRS // 2)
            def _(p):
                rows = pl.ds(pl.multiple_of(p * TWO, TWO), TWO)
                values = mm(table[points, :], field[rows, :], ((1,), (1,)))
                tall[pl.ds(2 * p, count, stride=PAIRS), :] = values[:, :LANES]
                tall[pl.ds(2 * p + 1, count, stride=PAIRS), :] = values[:, LANES:]

            @pl.loop(0, COLS // 2 * G)
            def _(i):
                rows = pl.ds(pl.multiple_of(i * SIZE, SIZE), SIZE)
                lifted[i % G, side * (COLS // 2) + i // G, f] = tall[rows, :].astype(BF)

    @pl.loop(0, G)
    def _(g):
        others(part, COLS, lambda q: col_fwd(g, q).start())
        col_fwd_own(g).start()

    @pl.loop(0, COLS)
    def _(s):
        for a in range(2):
            own = pl.ds(pl.multiple_of(s * LANES + a * K, K), K)
            other = pl.ds(pl.multiple_of(s * LANES + (1 - a) * K, K), K)
            wide_eval[a, own, :] = evals[pl.ds(pl.multiple_of(s * K, K), K), :]
            wide_eval[a, other, :] = jnp.zeros((K, YG), BF)

    @pl.loop(0, G)
    def _(g):
        others(col, COLS, lambda s: col_fwd_in(g, s).wait_recv())
        col_fwd_own(g).wait()
        left = jnp.concatenate(
            [jnp.concatenate([arrived[g, s, f] for s in range(COLS)], axis=1) for f in range(2)], axis=0
        )
        for a in range(2):
            values = mm(left, wide_eval[a]).astype(BF)
            for f in range(2):
                for h in range(2):
                    block = values[f * SIZE : (f + 1) * SIZE, h * YH : (h + 1) * YH]
                    spread[g, h * 8 : (h + 1) * 8, f, a * PAIRS : (a + 1) * PAIRS, :] = block.reshape(8, PAIRS, YH)

        others(row, ROWS, lambda t: row_fwd(g, t).start())
        row_fwd_own(g).start()

    lane = lax.broadcasted_iota(jnp.int32, (YG, LANES), 1)
    for j in range(COLS // 2):
        tile = projs[:, j * LANES : (j + 1) * LANES].astype(F32)
        turned = pltpu.roll(tile, K, 1)
        for s in (2 * j, 2 * j + 1):
            straight, moved = (tile, turned) if s % 2 == 0 else (turned, tile)
            for a in range(2):
                keep = jnp.where((lane < K) == (a == 0), straight if a == 0 else moved, 0.0).astype(BF)
                wide_proj[a * YG : (a + 1) * YG, s * LANES : (s + 1) * LANES] = keep

    @pl.loop(0, XG // LANES)
    def _(j):
        points = pl.ds(pl.multiple_of(j * LANES, LANES), LANES)

        def ordered(values):
            tall[:KX, :] = values
            return jnp.concatenate(
                [tall[pl.ds(r * A + a, PAIRS, stride=2), :] for r in range(ROWS) for a in range(2)], axis=0
            )

        eval_x[points, :] = ordered(evals[:, points].astype(F32)).T.astype(BF)
        proj_x[:, points] = ordered(projs[points, :].astype(F32).T).astype(BF)

    swap.wait()
    strata = jnp.where(high == 0, strat[...], strat_in[...]).reshape(1, ZPART)
    level_of = lax.broadcasted_iota(jnp.int32, (1, ZPART), 1)

    @pl.loop(0, G)
    def _(g):
        others(row, ROWS, lambda t: row_fwd_in(g, t).wait_recv())
        row_fwd_own(g).wait()
        level = jnp.sum(jnp.where(level_of == g * ZC + row % 8, strata, 0.0), axis=1, keepdims=True)
        right = jnp.concatenate([grid[g, 0], grid[g, 1]], axis=1)
        tile = XG // 3
        for x in range(3):
            rows = slice(x * tile, (x + 1) * tile)
            both = mm(eval_x[rows, :], right).astype(BF).astype(F32)
            velocity, gradient = both[:, :YH], both[:, YH:]
            flux[rows, :YH] = (-(velocity * gradient) - level * velocity).astype(BF)
            flux[rows, YH:] = (-(velocity * jnp.abs(velocity))).astype(BF)
        for x in range(2):
            rows = slice(x * KX // 2, (x + 1) * KX // 2)
            both = mm(proj_x[rows, :], flux[...]).astype(BF)
            grid[g, 0, rows, :] = both[:, :YH]
            grid[g, 1, rows, :] = both[:, YH:]

        others(row, ROWS, lambda t: row_back(g, t).start())
        row_back_own(g).start()

    def to_modes(g):
        others(row, ROWS, lambda t: row_back_in(g, t).wait_recv())
        row_back_own(g).wait()

        def side(f, a, h):
            return returned[g, h * 8 : (h + 1) * 8, f, a * PAIRS : (a + 1) * PAIRS, :].reshape(SIZE, YH)

        left = jnp.concatenate(
            [
                jnp.concatenate([side(f, a, h) for a in range(2) for h in range(2)], axis=1)
                for f in range(2)
            ],
            axis=0,
        )
        half = COLS * LANES // 2
        for n in range(2):
            values = mm(left, wide_proj[:, n * half : (n + 1) * half]).astype(BF)
            for f in range(2):
                for s in range(COLS // 2):
                    arrived[g, n * COLS // 2 + s, f] = values[
                        f * SIZE : (f + 1) * SIZE, s * LANES : (s + 1) * LANES
                    ]

        others(col, COLS, lambda s: col_back(g, s).start())
        col_back_own(g).start()

    def gather(first, last, f, start):
        @pl.loop(first, last)
        def _(g):
            for q in range(COLS):
                place = pl.multiple_of(start + ((g - first) * COLS + q) * SIZE, SIZE)
                tall[pl.ds(place, SIZE), :] = folded[g, q, f].astype(F32)

    def tendency(first, last, p, start):
        count = (last - first) * COLS * ZC
        columns = [tall[pl.ds(start + 2 * p + a, count, stride=PAIRS), :].astype(BF) for a in range(2)]
        rows = slice(first * COLS * ZC, last * COLS * ZC)
        return mm(jnp.concatenate(columns, axis=1), drop[rows, :], ((0,), (0,)))

    def wait_modes(first, last):
        @pl.loop(first, last)
        def _(g):
            others(part, COLS, lambda q: col_back_in(g, q).wait_recv())
            col_back_own(g).wait()

    pl.loop(0, ENDS[0] + 1)(to_modes)
    wait_modes(0, ENDS[0])
    for f in range(2):
        gather(0, ENDS[0], f, 0)

        @pl.loop(0, PAIRS // 2)
        def _(p):
            rows = pl.ds(pl.multiple_of(p * TWO, TWO), TWO)
            partial[f, rows, :] = tendency(0, ENDS[0], p, 0)

    pl.loop(ENDS[0] + 1, ENDS[1] + 1)(to_modes)
    wait_modes(ENDS[0], ENDS[1])
    for f in range(2):
        gather(ENDS[0], ENDS[1], f, 0)

        @pl.loop(0, PAIRS // 2)
        def _(p):
            rows = pl.ds(pl.multiple_of(p * TWO, TWO), TWO)
            partial[f, rows, :] += tendency(ENDS[0], ENDS[1], p, 0)

    pl.loop(ENDS[1] + 1, G)(to_modes)
    wait_modes(ENDS[1], G)
    start = (G - ENDS[1]) * COLS * SIZE
    for f in range(2):
        gather(ENDS[1], G, f, f * start)

    @pl.loop(0, PAIRS // 2)
    def _(p):
        rows = pl.ds(pl.multiple_of(p * TWO, TWO), TWO)
        modal = []
        for f, field in enumerate((buoy, vel)):
            tend = partial[f, rows, :] + tendency(ENDS[1], G, p, f * start)
            rhs = (field[rows, :].astype(F32) + explicit_step * tend).astype(BF)
            modal.append(mm(rhs, eig_left[...]))
        modal_buoy, modal_vel = modal
        place = p * TWO + lax.broadcasted_iota(jnp.int32, (TWO, LANES), 0)
        freq_x = ((row * A + (place >> 6) + 1) >> 1).astype(F32) * (2.0 / KX)
        freq_y = ((col * K + (place & (K - 1)) + 1) >> 1).astype(F32) * (2.0 / KY)
        wave = 4.0 * (freq_x * freq_x + freq_y * freq_y)
        lapl = jnp.concatenate([wave] * (NZ // LANES), axis=1) + eig_val[...].reshape(1, NZ)
        diag_buoy = 1.0 + diffuse_buoy * lapl
        diag_vel = 1.0 + diffuse_vel * lapl
        inverse = 1.0 / (diag_buoy * diag_vel + couple_buoy * couple_vel)
        solved_buoy = ((diag_vel * modal_buoy - couple_buoy * modal_vel) * inverse).astype(BF)
        solved_vel = ((diag_buoy * modal_vel + couple_vel * modal_buoy) * inverse).astype(BF)
        out_buoy[rows, :] = mm(solved_buoy, eig_right[...]).astype(BF)
        out_vel[rows, :] = mm(solved_vel, eig_right[...]).astype(BF)

    @pl.loop(0, G)
    def _(g):
        others(part, COLS, lambda q: col_fwd(g, q).wait_send())
        others(row, ROWS, lambda t: row_fwd(g, t).wait_send())
        others(row, ROWS, lambda t: row_back(g, t).wait_send())
        others(col, COLS, lambda s: col_back(g, s).wait_send())


def per_device(buoy, vel_w, strat, eig_val, eig_left, eig_right):
    modes = A * K
    dma = pltpu.SemaphoreType.DMA
    vmem = pl.BlockSpec(memory_space=pltpu.VMEM)
    shape = jax.ShapeDtypeStruct((modes, NZ), BF)
    consts = [jnp.asarray(t) for t in tables()]
    new_buoy, new_vel = pl.pallas_call(
        kernel,
        out_shape=(shape, shape),
        in_specs=[vmem] * 11,
        out_specs=(vmem, vmem),
        scratch_shapes=[
            pltpu.VMEM((G, COLS, 2, SIZE, LANES), BF),
            pltpu.VMEM((G, COLS, 2, SIZE, LANES), BF),
            pltpu.VMEM((G, ROWS, 2, A, YH), BF),
            pltpu.VMEM((G, 2, KX, YH), BF),
            pltpu.VMEM((G, ROWS, 2, A, YH), BF),
            pltpu.VMEM((G, COLS, 2, SIZE, LANES), BF),
            pltpu.VMEM((TALL, LANES), F32),
            pltpu.VMEM((2, COLS * LANES, YG), BF),
            pltpu.VMEM((2 * YG, COLS * LANES), BF),
            pltpu.VMEM((XG, KX), BF),
            pltpu.VMEM((KX, XG), BF),
            pltpu.VMEM((XG, 2 * YH), BF),
            pltpu.VMEM((2, modes, NZ), F32),
            pltpu.VMEM((ZPART,), F32),
            dma((G, COLS)), dma((G, COLS)), dma((G, ROWS)), dma((G, ROWS)),
            dma((G, ROWS)), dma((G, ROWS)), dma((G, COLS)), dma((G, COLS)),
            dma, dma,
        ],
        compiler_params=pltpu.CompilerParams(
            collective_id=0, has_side_effects=True, vmem_limit_bytes=VMEM_LIMIT
        ),
        name="section",
    )(
        vel_w.reshape(modes, NZ), buoy.reshape(modes, NZ), *consts, strat, eig_val, eig_left, eig_right
    )
    return new_buoy.reshape(buoy.shape), new_vel.reshape(buoy.shape)


def solution(mesh):
    in_specs = (P("row", "col", None), P("row", "col", None), P("col"), P(), P(), P())
    out_specs = (P("row", "col", None), P("row", "col", None))
    return jax.shard_map(
        per_device, mesh=mesh, in_specs=in_specs, out_specs=out_specs, check_vma=False
    )
```

```python
import functools
import math

import jax
import jax.numpy as jnp
import numpy as np
from jax import lax
from jax.experimental import pallas as pl
from jax.experimental.pallas import tpu as pltpu
from jax.sharding import PartitionSpec as P

KX = 512
KY = 512
NZ = 384
XG = 768
YG = 768
ZG = 576

explicit_step = 0.5
diffuse_buoy = 0.5
diffuse_vel = 0.25
couple_buoy = 0.7
couple_vel = 0.7

ROWS = 16
COLS = 8
A = KX // ROWS
K = KY // COLS
PAIRS = A // 2
LANES = 2 * K
G = 9
PASSES = 3
ZPART = ZG // COLS
ZC = ZPART // G
SIZE = ZC * PAIRS
YH = YG // 2
TWO = 2 * LANES
TALL = 5 * COLS * SIZE
ENDS = (5, 8, 9)
BF = jnp.bfloat16
F32 = jnp.float32
MESH = pl.DeviceIdType.MESH
VMEM_LIMIT = 67_000_000


def trig(modes, points):
    order = np.arange(modes)
    freq = ((order + 1) // 2).astype(np.float32)
    step = np.float32(2.0 * math.pi / points)
    angle = (step * freq)[:, None] * np.arange(points, dtype=np.float32)[None, :]
    angle = angle.astype(np.float64)
    values = np.where((order % 2 == 0)[:, None], np.cos(angle), np.sin(angle))
    return order, values.astype(np.float32)


def fourier_eval(modes, points):
    _, values = trig(modes, points)
    return (values * np.float32(math.sqrt(2.0 / modes))).astype(BF)


def fourier_proj(modes, points):
    order, values = trig(modes, points)
    weight = np.where(order == 0, 1.0 / points, 2.0 / points).astype(np.float32)
    return (values * weight[:, None] * np.float32(math.sqrt(modes / 2.0))).T.astype(BF)


def cheb_tables(degree, points):
    order = np.arange(degree, dtype=np.float32)
    theta = np.float32(math.pi) * (np.arange(points, dtype=np.float32) + np.float32(0.5))
    theta = theta / np.float32(points)
    angle = (order[:, None] * theta[None, :]).astype(np.float64)
    cos, sin = np.cos(angle).astype(np.float32), np.sin(angle).astype(np.float32)
    norm = np.float32(math.sqrt(2.0 / degree))
    weight = np.where(order == 0, 1.0 / points, 2.0 / points).astype(np.float32)
    levels = cos * norm
    slopes = -(order[:, None] / np.float32(degree)) * sin * norm
    projector = (cos * weight[:, None] * np.float32(math.sqrt(degree / 2.0))).T
    return levels.astype(BF), slopes.astype(BF), projector.astype(BF)


def tables():
    levels, slopes, projector = cheb_tables(NZ, ZG)
    drop = np.asarray(projector).reshape(COLS, G, ZC, NZ).transpose(1, 0, 2, 3).reshape(ZG, NZ)
    lift, slope = (
        np.asarray(t).T.reshape(COLS, PASSES, -1, NZ).transpose(1, 0, 2, 3).reshape(PASSES, -1, NZ)
        for t in (levels, slopes)
    )
    return lift, slope, np.ascontiguousarray(drop), fourier_eval(KY, YG), np.ascontiguousarray(fourier_proj(KY, YG))


def mm(left, right, dims=((1,), (0,))):
    return lax.dot_general(left, right, (dims, ((), ())), preferred_element_type=F32)


def kernel(
    vel, buoy, lift, slope, drop_in, evals_in, projs_in, strat, eig_val, left_in, right_in,
    out_buoy, out_vel,
    lifted, arrived, spread, grid, returned, folded, tall, wide_eval, wide_proj, eval_x, proj_x, flux, partial,
    strat_in, drop, evals, projs, eig_left, eig_right, load_s,
    colf_s, colf_r, rowf_s, rowf_r, rowb_s, rowb_r, colb_s, colb_r, strat_s, strat_r,
):
    row, col = lax.axis_index("row"), lax.axis_index("col")
    high = row // (ROWS // 2)
    base, low = (col // 2) * 2, col % 2
    part = base + (low + high) % 2

    def col_of(q):
        return (row, (q // 2) * 2 + (q % 2 + high) % 2)

    def row_of(t):
        return (t, base + (low + high + t // (ROWS // 2)) % 2)

    barrier = pltpu.get_barrier_semaphore()

    @pl.loop(1, COLS)
    def _(i):
        pl.semaphore_signal(barrier, inc=1, device_id=col_of((part + i) % COLS), device_id_type=MESH)

    @pl.loop(1, ROWS)
    def _(i):
        pl.semaphore_signal(barrier, inc=1, device_id=row_of((row + i) % ROWS), device_id_type=MESH)

    loads = [
        pltpu.make_async_copy(src, dst, load_s.at[n])
        for n, (src, dst) in enumerate(
            ((evals_in, evals), (projs_in, projs), (drop_in, drop), (left_in, eig_left), (right_in, eig_right))
        )
    ]
    for load in loads:
        load.start()

    def remote(src, dst, send, recv, device):
        return pltpu.make_async_remote_copy(
            src_ref=src, dst_ref=dst, send_sem=send, recv_sem=recv, device_id=device, device_id_type=MESH
        )

    def col_fwd(g, q):
        return remote(lifted.at[g, q], arrived.at[g, col], colf_s.at[g, q], colf_r.at[g, col], col_of(q))

    def col_fwd_in(g, s):
        block = arrived.at[g, s]
        return remote(block, block, colf_s.at[g, s], colf_r.at[g, s], col_of(0))

    def col_fwd_own(g):
        return pltpu.make_async_copy(lifted.at[g, part], arrived.at[g, col], colf_r.at[g, col])

    def row_fwd(g, t):
        mine = pl.ds(pl.multiple_of(row * A, A), A)
        return remote(spread.at[g, t], grid.at[g, :, mine, :], rowf_s.at[g, t], rowf_r.at[g, row], row_of(t))

    def row_fwd_in(g, t):
        block = grid.at[g, :, pl.ds(pl.multiple_of(t * A, A), A), :]
        return remote(block, block, rowf_s.at[g, t], rowf_r.at[g, t], row_of(t))

    def row_fwd_own(g):
        mine = pl.ds(pl.multiple_of(row * A, A), A)
        return pltpu.make_async_copy(spread.at[g, row], grid.at[g, :, mine, :], rowf_r.at[g, row])

    def row_back(g, t):
        theirs = pl.ds(pl.multiple_of(t * A, A), A)
        return remote(grid.at[g, :, theirs, :], returned.at[g, row], rowb_s.at[g, t], rowb_r.at[g, row], row_of(t))

    def row_back_in(g, t):
        block = returned.at[g, t]
        return remote(block, block, rowb_s.at[g, t], rowb_r.at[g, t], row_of(t))

    def row_back_own(g):
        mine = pl.ds(pl.multiple_of(row * A, A), A)
        return pltpu.make_async_copy(grid.at[g, :, mine, :], returned.at[g, row], rowb_r.at[g, row])

    def col_back(g, s):
        return remote(arrived.at[g, s], folded.at[g, part], colb_s.at[g, s], colb_r.at[g, part], (row, s))

    def col_back_in(g, q):
        block = folded.at[g, q]
        return remote(block, block, colb_s.at[g, q], colb_r.at[g, q], col_of(q))

    def col_back_own(g):
        return pltpu.make_async_copy(arrived.at[g, col], folded.at[g, part], colb_r.at[g, part])

    def others(first, count, do):
        @pl.loop(1, count)
        def _(i):
            do((first + i) % count)

    count = ZG // PASSES
    chunks = G // PASSES

    def to_points(u):
        for f, (table, field) in enumerate(((lift, vel), (slope, buoy))):

            @pl.loop(0, PAIRS // 2)
            def _(p):
                rows = pl.ds(pl.multiple_of(p * TWO, TWO), TWO)
                values = mm(table[u], field[rows, :], ((1,), (1,)))
                tall[pl.ds(2 * p, count, stride=PAIRS), :] = values[:, :LANES]
                tall[pl.ds(2 * p + 1, count, stride=PAIRS), :] = values[:, LANES:]

            @pl.loop(0, COLS * chunks)
            def _(i):
                rows = pl.ds(pl.multiple_of(i * SIZE, SIZE), SIZE)
                lifted[u * chunks + i % chunks, i // chunks, f] = tall[rows, :].astype(BF)

    def send_points(u):
        @pl.loop(u * chunks, (u + 1) * chunks)
        def _(g):
            others(part, COLS, lambda q: col_fwd(g, q).start())
            col_fwd_own(g).start()

    to_points(0)
    pl.semaphore_wait(barrier, COLS + ROWS - 2)
    send_points(0)
    swap = remote(strat, strat_in, strat_s, strat_r, (row, base + 1 - low))
    swap.start()

    @pl.loop(1, PASSES)
    def _(u):
        to_points(u)
        send_points(u)

    for load in loads:
        load.wait()

    @pl.loop(0, COLS)
    def _(s):
        for a in range(2):
            own = pl.ds(pl.multiple_of(s * LANES + a * K, K), K)
            other = pl.ds(pl.multiple_of(s * LANES + (1 - a) * K, K), K)
            wide_eval[a, own, :] = evals[pl.ds(pl.multiple_of(s * K, K), K), :]
            wide_eval[a, other, :] = jnp.zeros((K, YG), BF)

    @pl.loop(0, G)
    def _(g):
        others(col, COLS, lambda s: col_fwd_in(g, s).wait_recv())
        col_fwd_own(g).wait()
        left = jnp.concatenate(
            [jnp.concatenate([arrived[g, s, f] for s in range(COLS)], axis=1) for f in range(2)], axis=0
        )
        for a in range(2):
            values = mm(left, wide_eval[a]).astype(BF)
            for f in range(2):
                for h in range(2):
                    block = values[f * SIZE : (f + 1) * SIZE, h * YH : (h + 1) * YH]
                    spread[g, h * 8 : (h + 1) * 8, f, a * PAIRS : (a + 1) * PAIRS, :] = block.reshape(8, PAIRS, YH)

        others(row, ROWS, lambda t: row_fwd(g, t).start())
        row_fwd_own(g).start()

    lane = lax.broadcasted_iota(jnp.int32, (YG, LANES), 1)
    for j in range(COLS // 2):
        tile = projs[:, j * LANES : (j + 1) * LANES].astype(F32)
        turned = pltpu.roll(tile, K, 1)
        for s in (2 * j, 2 * j + 1):
            straight, moved = (tile, turned) if s % 2 == 0 else (turned, tile)
            for a in range(2):
                keep = jnp.where((lane < K) == (a == 0), straight if a == 0 else moved, 0.0).astype(BF)
                wide_proj[a * YG : (a + 1) * YG, s * LANES : (s + 1) * LANES] = keep

    @pl.loop(0, XG // LANES)
    def _(j):
        points = pl.ds(pl.multiple_of(j * LANES, LANES), LANES)

        def ordered(values):
            tall[:KX, :] = values
            return jnp.concatenate(
                [tall[pl.ds(r * A + a, PAIRS, stride=2), :] for r in range(ROWS) for a in range(2)], axis=0
            )

        eval_x[points, :] = ordered(evals[:, points].astype(F32)).T.astype(BF)
        proj_x[:, points] = ordered(projs[points, :].astype(F32).T).astype(BF)

    swap.wait()
    strata = jnp.where(high == 0, strat[...], strat_in[...]).reshape(1, ZPART)
    level_of = lax.broadcasted_iota(jnp.int32, (1, ZPART), 1)

    @pl.loop(0, G)
    def _(g):
        others(row, ROWS, lambda t: row_fwd_in(g, t).wait_recv())
        row_fwd_own(g).wait()
        level = jnp.sum(jnp.where(level_of == g * ZC + row % 8, strata, 0.0), axis=1, keepdims=True)
        right = jnp.concatenate([grid[g, 0], grid[g, 1]], axis=1)
        tile = XG // 3
        for x in range(3):
            rows = slice(x * tile, (x + 1) * tile)
            both = mm(eval_x[rows, :], right).astype(BF).astype(F32)
            velocity, gradient = both[:, :YH], both[:, YH:]
            flux[rows, :YH] = (-(velocity * gradient) - level * velocity).astype(BF)
            flux[rows, YH:] = (-(velocity * jnp.abs(velocity))).astype(BF)
        for x in range(2):
            rows = slice(x * KX // 2, (x + 1) * KX // 2)
            both = mm(proj_x[rows, :], flux[...]).astype(BF)
            grid[g, 0, rows, :] = both[:, :YH]
            grid[g, 1, rows, :] = both[:, YH:]

        others(row, ROWS, lambda t: row_back(g, t).start())
        row_back_own(g).start()

    def to_modes(g):
        others(row, ROWS, lambda t: row_back_in(g, t).wait_recv())
        row_back_own(g).wait()

        def side(f, a, h):
            return returned[g, h * 8 : (h + 1) * 8, f, a * PAIRS : (a + 1) * PAIRS, :].reshape(SIZE, YH)

        left = jnp.concatenate(
            [
                jnp.concatenate([side(f, a, h) for a in range(2) for h in range(2)], axis=1)
                for f in range(2)
            ],
            axis=0,
        )
        half = COLS * LANES // 2
        for n in range(2):
            values = mm(left, wide_proj[:, n * half : (n + 1) * half]).astype(BF)
            for f in range(2):
                for s in range(COLS // 2):
                    arrived[g, n * COLS // 2 + s, f] = values[
                        f * SIZE : (f + 1) * SIZE, s * LANES : (s + 1) * LANES
                    ]

        others(col, COLS, lambda s: col_back(g, s).start())
        col_back_own(g).start()

    def gather(first, last, f, start):
        @pl.loop(first, last)
        def _(g):
            for q in range(COLS):
                place = pl.multiple_of(start + ((g - first) * COLS + q) * SIZE, SIZE)
                tall[pl.ds(place, SIZE), :] = folded[g, q, f].astype(F32)

    def tendency(first, last, p, start):
        count = (last - first) * COLS * ZC
        columns = [tall[pl.ds(start + 2 * p + a, count, stride=PAIRS), :].astype(BF) for a in range(2)]
        rows = slice(first * COLS * ZC, last * COLS * ZC)
        return mm(jnp.concatenate(columns, axis=1), drop[rows, :], ((0,), (0,)))

    def wait_modes(first, last):
        @pl.loop(first, last)
        def _(g):
            others(part, COLS, lambda q: col_back_in(g, q).wait_recv())
            col_back_own(g).wait()

    pl.loop(0, ENDS[0] + 1)(to_modes)
    wait_modes(0, ENDS[0])
    for f in range(2):
        gather(0, ENDS[0], f, 0)

        @pl.loop(0, PAIRS // 2)
        def _(p):
            rows = pl.ds(pl.multiple_of(p * TWO, TWO), TWO)
            partial[f, rows, :] = tendency(0, ENDS[0], p, 0)

    pl.loop(ENDS[0] + 1, ENDS[1] + 1)(to_modes)
    wait_modes(ENDS[0], ENDS[1])
    for f in range(2):
        gather(ENDS[0], ENDS[1], f, 0)

        @pl.loop(0, PAIRS // 2)
        def _(p):
            rows = pl.ds(pl.multiple_of(p * TWO, TWO), TWO)
            partial[f, rows, :] += tendency(ENDS[0], ENDS[1], p, 0)

    pl.loop(ENDS[1] + 1, G)(to_modes)
    wait_modes(ENDS[1], G)
    start = (G - ENDS[1]) * COLS * SIZE
    for f in range(2):
        gather(ENDS[1], G, f, f * start)

    @pl.loop(0, PAIRS // 2)
    def _(p):
        rows = pl.ds(pl.multiple_of(p * TWO, TWO), TWO)
        modal = []
        for f, field in enumerate((buoy, vel)):
            tend = partial[f, rows, :] + tendency(ENDS[1], G, p, f * start)
            rhs = (field[rows, :].astype(F32) + explicit_step * tend).astype(BF)
            modal.append(mm(rhs, eig_left[...]))
        modal_buoy, modal_vel = modal
        place = p * TWO + lax.broadcasted_iota(jnp.int32, (TWO, LANES), 0)
        freq_x = ((row * A + (place >> 6) + 1) >> 1).astype(F32) * (2.0 / KX)
        freq_y = ((col * K + (place & (K - 1)) + 1) >> 1).astype(F32) * (2.0 / KY)
        wave = 4.0 * (freq_x * freq_x + freq_y * freq_y)
        lapl = jnp.concatenate([wave] * (NZ // LANES), axis=1) + eig_val[...].reshape(1, NZ)
        diag_buoy = 1.0 + diffuse_buoy * lapl
        diag_vel = 1.0 + diffuse_vel * lapl
        inverse = 1.0 / (diag_buoy * diag_vel + couple_buoy * couple_vel)
        solved_buoy = ((diag_vel * modal_buoy - couple_buoy * modal_vel) * inverse).astype(BF)
        solved_vel = ((diag_buoy * modal_vel + couple_vel * modal_buoy) * inverse).astype(BF)
        out_buoy[rows, :] = mm(solved_buoy, eig_right[...]).astype(BF)
        out_vel[rows, :] = mm(solved_vel, eig_right[...]).astype(BF)

    @pl.loop(0, G)
    def _(g):
        others(part, COLS, lambda q: col_fwd(g, q).wait_send())
        others(row, ROWS, lambda t: row_fwd(g, t).wait_send())
        others(row, ROWS, lambda t: row_back(g, t).wait_send())
        others(col, COLS, lambda s: col_back(g, s).wait_send())


def per_device(buoy, vel_w, strat, eig_val, eig_left, eig_right):
    modes = A * K
    dma = pltpu.SemaphoreType.DMA
    vmem = pl.BlockSpec(memory_space=pltpu.VMEM)
    hbm = pl.BlockSpec(memory_space=pl.ANY)
    shape = jax.ShapeDtypeStruct((modes, NZ), BF)
    consts = [jnp.asarray(t) for t in tables()]
    new_buoy, new_vel = pl.pallas_call(
        kernel,
        out_shape=(shape, shape),
        in_specs=[vmem] * 4 + [hbm] * 3 + [vmem] * 2 + [hbm] * 2,
        out_specs=(vmem, vmem),
        scratch_shapes=[
            pltpu.VMEM((G, COLS, 2, SIZE, LANES), BF),
            pltpu.VMEM((G, COLS, 2, SIZE, LANES), BF),
            pltpu.VMEM((G, ROWS, 2, A, YH), BF),
            pltpu.VMEM((G, 2, KX, YH), BF),
            pltpu.VMEM((G, ROWS, 2, A, YH), BF),
            pltpu.VMEM((G, COLS, 2, SIZE, LANES), BF),
            pltpu.VMEM((TALL, LANES), F32),
            pltpu.VMEM((2, COLS * LANES, YG), BF),
            pltpu.VMEM((2 * YG, COLS * LANES), BF),
            pltpu.VMEM((XG, KX), BF),
            pltpu.VMEM((KX, XG), BF),
            pltpu.VMEM((XG, 2 * YH), BF),
            pltpu.VMEM((2, modes, NZ), F32),
            pltpu.VMEM((ZPART,), F32),
            pltpu.VMEM((ZG, NZ), BF),
            pltpu.VMEM((KY, YG), BF),
            pltpu.VMEM((YG, KY), BF),
            pltpu.VMEM((NZ, NZ), BF),
            pltpu.VMEM((NZ, NZ), BF),
            dma((5,)),
            dma((G, COLS)), dma((G, COLS)), dma((G, ROWS)), dma((G, ROWS)),
            dma((G, ROWS)), dma((G, ROWS)), dma((G, COLS)), dma((G, COLS)),
            dma, dma,
        ],
        compiler_params=pltpu.CompilerParams(
            collective_id=0, has_side_effects=True, vmem_limit_bytes=VMEM_LIMIT
        ),
        name="section",
    )(
        vel_w.reshape(modes, NZ), buoy.reshape(modes, NZ), *consts, strat, eig_val, eig_left, eig_right
    )
    return new_buoy.reshape(buoy.shape), new_vel.reshape(buoy.shape)


def solution(mesh):
    in_specs = (P("row", "col", None), P("row", "col", None), P("col"), P(), P(), P())
    out_specs = (P("row", "col", None), P("row", "col", None))
    return jax.shard_map(
        per_device, mesh=mesh, in_specs=in_specs, out_specs=out_specs, check_vma=False
    )
```

```python
import functools
import math

import jax
import jax.numpy as jnp
import numpy as np
from jax import lax
from jax.experimental import pallas as pl
from jax.experimental.pallas import tpu as pltpu
from jax.sharding import PartitionSpec as P

KX = 512
KY = 512
NZ = 384
XG = 768
YG = 768
ZG = 576

explicit_step = 0.5
diffuse_buoy = 0.5
diffuse_vel = 0.25
couple_buoy = 0.7
couple_vel = 0.7

ROWS = 16
COLS = 8
A = KX // ROWS
K = KY // COLS
PAIRS = A // 2
LANES = 2 * K
G = 9
PASSES = 3
ZPART = ZG // COLS
ZC = ZPART // G
SIZE = ZC * PAIRS
TWO = 2 * LANES
TALL = 5 * COLS * SIZE
ENDS = (5, 8, 9)
BF = jnp.bfloat16
F32 = jnp.float32
MESH = pl.DeviceIdType.MESH
VMEM_LIMIT = 67_000_000


def trig(modes, points):
    order = np.arange(modes)
    freq = ((order + 1) // 2).astype(np.float32)
    step = np.float32(2.0 * math.pi / points)
    angle = (step * freq)[:, None] * np.arange(points, dtype=np.float32)[None, :]
    angle = angle.astype(np.float64)
    values = np.where((order % 2 == 0)[:, None], np.cos(angle), np.sin(angle))
    return order, values.astype(np.float32)


def fourier_eval(modes, points):
    _, values = trig(modes, points)
    return (values * np.float32(math.sqrt(2.0 / modes))).astype(BF)


def fourier_proj(modes, points):
    order, values = trig(modes, points)
    weight = np.where(order == 0, 1.0 / points, 2.0 / points).astype(np.float32)
    return (values * weight[:, None] * np.float32(math.sqrt(modes / 2.0))).T.astype(BF)


def cheb_tables(degree, points):
    order = np.arange(degree, dtype=np.float32)
    theta = np.float32(math.pi) * (np.arange(points, dtype=np.float32) + np.float32(0.5))
    theta = theta / np.float32(points)
    angle = (order[:, None] * theta[None, :]).astype(np.float64)
    cos, sin = np.cos(angle).astype(np.float32), np.sin(angle).astype(np.float32)
    norm = np.float32(math.sqrt(2.0 / degree))
    weight = np.where(order == 0, 1.0 / points, 2.0 / points).astype(np.float32)
    levels = cos * norm
    slopes = -(order[:, None] / np.float32(degree)) * sin * norm
    projector = (cos * weight[:, None] * np.float32(math.sqrt(degree / 2.0))).T
    return levels.astype(BF), slopes.astype(BF), projector.astype(BF)


def tables():
    levels, slopes, projector = cheb_tables(NZ, ZG)

    def by_chunk(rows):
        return np.asarray(rows).reshape(COLS, ZC, G, NZ).transpose(2, 0, 1, 3).reshape(ZG, NZ)

    lift, slope = (by_chunk(np.asarray(t).T).reshape(PASSES, -1, NZ) for t in (levels, slopes))
    return lift, slope, by_chunk(projector), fourier_eval(KY, YG), np.ascontiguousarray(fourier_proj(KY, YG))


def mm(left, right, dims=((1,), (0,))):
    return lax.dot_general(left, right, (dims, ((), ())), preferred_element_type=F32)


def kernel(
    vel, buoy, lift, slope, drop_in, evals_in, projs_in, strat, eig_val, left_in, right_in,
    out_buoy, out_vel,
    lifted, arrived, planes, passed, folded, tall, wide_eval, wide_proj, eval_x, proj_x, middle, flux, partial,
    strat_in, drop, evals, projs, eig_left, eig_right, load_s,
    colf_s, colf_r, rowf_s, rowf_r, rowb_s, rowb_r, colb_s, colb_r, strat_s, strat_r,
):
    row, col = lax.axis_index("row"), lax.axis_index("col")
    high = row // (ROWS // 2)
    base, low = (col // 2) * 2, col % 2
    part = base + (low + high) % 2

    def col_of(q):
        return (row, (q // 2) * 2 + (q % 2 + high) % 2)

    def row_of(t):
        return (t, base + (low + high + t // (ROWS // 2)) % 2)

    barrier = pltpu.get_barrier_semaphore()

    @pl.loop(1, COLS)
    def _(i):
        pl.semaphore_signal(barrier, inc=1, device_id=col_of((part + i) % COLS), device_id_type=MESH)

    @pl.loop(1, ROWS)
    def _(i):
        pl.semaphore_signal(barrier, inc=1, device_id=row_of((row + i) % ROWS), device_id_type=MESH)

    loads = [
        pltpu.make_async_copy(src, dst, load_s.at[n])
        for n, (src, dst) in enumerate(
            ((evals_in, evals), (projs_in, projs), (drop_in, drop), (left_in, eig_left), (right_in, eig_right))
        )
    ]
    for load in loads:
        load.start()

    def remote(src, dst, send, recv, device):
        return pltpu.make_async_remote_copy(
            src_ref=src, dst_ref=dst, send_sem=send, recv_sem=recv, device_id=device, device_id_type=MESH
        )

    chip, core = row // 2, row % 2

    def col_fwd(g, q):
        return remote(lifted.at[g, q], arrived.at[g, :, col], colf_s.at[g, q], colf_r.at[g, col], col_of(q))

    def col_fwd_in(g, s):
        block = arrived.at[g, :, s]
        return remote(block, block, colf_s.at[g, s], colf_r.at[g, s], col_of(0))

    def col_fwd_own(g):
        return pltpu.make_async_copy(lifted.at[g, part], arrived.at[g, :, col], colf_r.at[g, col])

    def col_back(g, s):
        return remote(passed.at[g, :, s], folded.at[g, part], colb_s.at[g, s], colb_r.at[g, part], (row, s))

    def col_back_in(g, q):
        block = folded.at[g, q]
        return remote(block, block, colb_s.at[g, q], colb_r.at[g, q], col_of(q))

    def col_back_own(g):
        return pltpu.make_async_copy(passed.at[g, :, col], folded.at[g, part], colb_r.at[g, part])

    def others(first, count, do):
        @pl.loop(1, count)
        def _(i):
            do((first + i) % count)

    def row_fwd(g, t):
        m = g // 2
        return remote(arrived.at[g, t // 2], planes.at[m, row], rowf_s.at[m, t], rowf_r.at[m, row], row_of(t))

    def row_fwd_in(m, t):
        block = planes.at[m, t]
        return remote(block, block, rowf_s.at[m, t], rowf_r.at[m, t], row_of(t))

    def row_fwd_own(g):
        m = g // 2
        return pltpu.make_async_copy(arrived.at[g, chip], planes.at[m, row], rowf_r.at[m, row])

    def row_back(m, g, t):
        return remote(planes.at[m, t], passed.at[g, chip], rowb_s.at[m, t], rowb_r.at[g, chip], row_of(t))

    def row_back_in(g, t):
        block = passed.at[g, t // 2]
        return remote(block, block, rowb_s.at[0, t], rowb_r.at[g, t // 2], row_of(t))

    def row_back_own(m, g):
        return pltpu.make_async_copy(planes.at[m, row], passed.at[g, chip], rowb_r.at[g, chip])

    def chips(side, here, there):
        @pl.loop(0, ZC)
        def _(i):
            t = ((chip + i) % ZC) * 2 + side
            pl.when(t == row)(lambda: here())
            pl.when(t != row)(lambda: there(t))

    def members(here, there):
        chips(core, here, there)
        chips(1 - core, here, there)

    def relay_fwd(g):
        others(col, COLS, lambda s: col_fwd_in(g, s).wait_recv())
        col_fwd_own(g).wait()

        @pl.when(g < G - 1)
        def _():
            chips(g % 2, lambda: row_fwd_own(g).start(), lambda t: row_fwd(g, t).start())

        @pl.when(g == G - 1)
        def _():
            members(lambda: row_fwd_own(g).start(), lambda t: row_fwd(g, t).start())

    def relay_back(g):
        side = jnp.where(g == G - 1, core, g % 2)
        chips(side, lambda: row_back_own(0, g).wait(), lambda t: row_back_in(g, t).wait_recv())
        others(col, COLS, lambda s: col_back(g, s).start())
        col_back_own(g).start()

    count = ZG // PASSES
    chunks = G // PASSES

    def to_points(u):
        for f, (table, field) in enumerate(((lift, vel), (slope, buoy))):

            @pl.loop(0, PAIRS // 2)
            def _(p):
                rows = pl.ds(pl.multiple_of(p * TWO, TWO), TWO)
                values = mm(table[u], field[rows, :], ((1,), (1,)))
                tall[pl.ds(2 * p, count, stride=PAIRS), :] = values[:, :LANES]
                tall[pl.ds(2 * p + 1, count, stride=PAIRS), :] = values[:, LANES:]

            @pl.loop(0, COLS * chunks)
            def _(i):
                rows = pl.ds(pl.multiple_of(i * SIZE, SIZE), SIZE)
                block = tall[rows, :].astype(BF).reshape(ZC, PAIRS, LANES)
                lifted[u * chunks + i // COLS, i % COLS, :, f] = block

    def send_points(u):
        @pl.loop(u * chunks, (u + 1) * chunks)
        def _(g):
            others(part, COLS, lambda q: col_fwd(g, q).start())
            col_fwd_own(g).start()

    to_points(0)
    pl.semaphore_wait(barrier, COLS + ROWS - 2)
    send_points(0)
    swap = remote(strat, strat_in, strat_s, strat_r, (row, base + 1 - low))
    swap.start()

    @pl.loop(1, PASSES)
    def _(u):
        to_points(u)
        send_points(u)

    for load in loads:
        load.wait()

    @pl.loop(0, COLS)
    def _(s):
        for a in range(2):
            own = pl.ds(pl.multiple_of(s * LANES + a * K, K), K)
            other = pl.ds(pl.multiple_of(s * LANES + (1 - a) * K, K), K)
            wide_eval[a, own, :] = evals[pl.ds(pl.multiple_of(s * K, K), K), :]
            wide_eval[a, other, :] = jnp.zeros((K, YG), BF)

    relay_fwd(0)

    lane = lax.broadcasted_iota(jnp.int32, (YG, LANES), 1)
    for j in range(COLS // 2):
        tile = projs[:, j * LANES : (j + 1) * LANES].astype(F32)
        turned = pltpu.roll(tile, K, 1)
        for s in (2 * j, 2 * j + 1):
            straight, moved = (tile, turned) if s % 2 == 0 else (turned, tile)
            for a in range(2):
                keep = jnp.where((lane < K) == (a == 0), straight if a == 0 else moved, 0.0).astype(BF)
                wide_proj[a * YG : (a + 1) * YG, s * LANES : (s + 1) * LANES] = keep

    @pl.loop(0, XG // LANES)
    def _(j):
        points = pl.ds(pl.multiple_of(j * LANES, LANES), LANES)

        def ordered(values):
            tall[:KX, :] = values
            return jnp.concatenate([tall[pl.ds(a, KX // 2, stride=2), :] for a in range(2)], axis=0)

        eval_x[points, :] = ordered(evals[:, points].astype(F32)).T.astype(BF)
        proj_x[:, points] = ordered(projs[points, :].astype(F32).T).astype(BF)

    pl.loop(1, 3)(relay_fwd)
    swap.wait()
    strata = jnp.where(high == 0, strat[...], strat_in[...]).reshape(1, ZPART)
    level_of = lax.broadcasted_iota(jnp.int32, (1, ZPART), 1)

    half = KX // 2
    last = G // 2

    @pl.loop(0, last + 1)
    def _(m):
        chunk = jnp.where(m == last, G - 1, 2 * m + core)
        members(lambda: row_fwd_own(2 * m).wait(), lambda t: row_fwd_in(m, t).wait_recv())
        for f in range(2):
            left = jnp.concatenate([planes[m, :, s, f].reshape(half, LANES) for s in range(COLS)], axis=1)
            for a in range(2):
                middle[a * half : (a + 1) * half, f * YG : (f + 1) * YG] = mm(left, wide_eval[a]).astype(BF)

        pl.when(2 * m + 3 < G)(lambda: relay_fwd(2 * m + 3))
        pl.when(m >= 2)(lambda: relay_back(2 * m - 4))

        level = jnp.sum(jnp.where(level_of == chip * G + chunk, strata, 0.0), axis=1, keepdims=True)
        tile = XG // 3
        for x in range(3):
            rows = slice(x * tile, (x + 1) * tile)
            velocity = mm(eval_x[rows, :], middle[:, :YG]).astype(BF).astype(F32)
            gradient = mm(eval_x[rows, :], middle[:, YG:]).astype(BF).astype(F32)
            flux[rows, :YG] = (-(velocity * gradient) - level * velocity).astype(BF)
            flux[rows, YG:] = (-(velocity * jnp.abs(velocity))).astype(BF)

        pl.when(2 * m + 4 < G)(lambda: relay_fwd(2 * m + 4))
        pl.when(m >= 2)(lambda: relay_back(2 * m - 3))

        for a in range(2):
            rows = slice(a * half, (a + 1) * half)
            for f in range(2):
                middle[rows, f * YG : (f + 1) * YG] = mm(proj_x[rows, :], flux[:, f * YG : (f + 1) * YG]).astype(BF)
        for f in range(2):
            left = jnp.concatenate(
                [middle[a * half : (a + 1) * half, f * YG : (f + 1) * YG] for a in range(2)], axis=1
            )
            values = mm(left, wide_proj[...]).astype(BF)
            for s in range(COLS):
                planes[m, :, s, f] = values[:, s * LANES : (s + 1) * LANES].reshape(ROWS, PAIRS, LANES)

        def here():
            row_back_own(m, chunk).start()

        def there(t):
            row_back(m, chunk, t).start()

        chips(core, here, there)
        pl.when(m < last)(lambda: chips(1 - core, here, there))

    def gather(first, last, f, start):
        @pl.loop(first, last)
        def _(g):
            for q in range(COLS):
                place = pl.multiple_of(start + ((g - first) * COLS + q) * SIZE, SIZE)
                tall[pl.ds(place, SIZE), :] = folded[g, q, :, f].reshape(SIZE, LANES).astype(F32)

    def tendency(first, last, p, start):
        count = (last - first) * COLS * ZC
        columns = [tall[pl.ds(start + 2 * p + a, count, stride=PAIRS), :].astype(BF) for a in range(2)]
        rows = slice(first * COLS * ZC, last * COLS * ZC)
        return mm(jnp.concatenate(columns, axis=1), drop[rows, :], ((0,), (0,)))

    def wait_modes(first, last):
        @pl.loop(first, last)
        def _(g):
            others(part, COLS, lambda q: col_back_in(g, q).wait_recv())
            col_back_own(g).wait()

    pl.loop(2 * last - 2, G)(relay_back)
    wait_modes(0, ENDS[0])
    for f in range(2):
        gather(0, ENDS[0], f, 0)

        @pl.loop(0, PAIRS // 2)
        def _(p):
            rows = pl.ds(pl.multiple_of(p * TWO, TWO), TWO)
            partial[f, rows, :] = tendency(0, ENDS[0], p, 0)

    wait_modes(ENDS[0], ENDS[1])
    for f in range(2):
        gather(ENDS[0], ENDS[1], f, 0)

        @pl.loop(0, PAIRS // 2)
        def _(p):
            rows = pl.ds(pl.multiple_of(p * TWO, TWO), TWO)
            partial[f, rows, :] += tendency(ENDS[0], ENDS[1], p, 0)

    wait_modes(ENDS[1], G)
    start = (G - ENDS[1]) * COLS * SIZE
    for f in range(2):
        gather(ENDS[1], G, f, f * start)

    @pl.loop(0, PAIRS // 2)
    def _(p):
        rows = pl.ds(pl.multiple_of(p * TWO, TWO), TWO)
        modal = []
        for f, field in enumerate((buoy, vel)):
            tend = partial[f, rows, :] + tendency(ENDS[1], G, p, f * start)
            rhs = (field[rows, :].astype(F32) + explicit_step * tend).astype(BF)
            modal.append(mm(rhs, eig_left[...]))
        modal_buoy, modal_vel = modal
        place = p * TWO + lax.broadcasted_iota(jnp.int32, (TWO, LANES), 0)
        freq_x = ((row * A + (place >> 6) + 1) >> 1).astype(F32) * (2.0 / KX)
        freq_y = ((col * K + (place & (K - 1)) + 1) >> 1).astype(F32) * (2.0 / KY)
        wave = 4.0 * (freq_x * freq_x + freq_y * freq_y)
        lapl = jnp.concatenate([wave] * (NZ // LANES), axis=1) + eig_val[...].reshape(1, NZ)
        diag_buoy = 1.0 + diffuse_buoy * lapl
        diag_vel = 1.0 + diffuse_vel * lapl
        inverse = 1.0 / (diag_buoy * diag_vel + couple_buoy * couple_vel)
        solved_buoy = ((diag_vel * modal_buoy - couple_buoy * modal_vel) * inverse).astype(BF)
        solved_vel = ((diag_buoy * modal_vel + couple_vel * modal_buoy) * inverse).astype(BF)
        out_buoy[rows, :] = mm(solved_buoy, eig_right[...]).astype(BF)
        out_vel[rows, :] = mm(solved_vel, eig_right[...]).astype(BF)

    @pl.loop(0, G)
    def _(g):
        others(part, COLS, lambda q: col_fwd(g, q).wait_send())
        others(col, COLS, lambda s: col_back(g, s).wait_send())

    def nothing():
        pass

    @pl.loop(0, last)
    def _(m):
        members(nothing, lambda t: row_fwd(2 * m, t).wait_send())
        members(nothing, lambda t: row_back(m, 2 * m, t).wait_send())

    members(nothing, lambda t: row_fwd(G - 1, t).wait_send())
    chips(core, nothing, lambda t: row_back(last, G - 1, t).wait_send())


def per_device(buoy, vel_w, strat, eig_val, eig_left, eig_right):
    modes = A * K
    dma = pltpu.SemaphoreType.DMA
    vmem = pl.BlockSpec(memory_space=pltpu.VMEM)
    hbm = pl.BlockSpec(memory_space=pl.ANY)
    shape = jax.ShapeDtypeStruct((modes, NZ), BF)
    consts = [jnp.asarray(t) for t in tables()]
    new_buoy, new_vel = pl.pallas_call(
        kernel,
        out_shape=(shape, shape),
        in_specs=[vmem] * 4 + [hbm] * 3 + [vmem] * 2 + [hbm] * 2,
        out_specs=(vmem, vmem),
        scratch_shapes=[
            pltpu.VMEM((G, COLS, ZC, 2, PAIRS, LANES), BF),
            pltpu.VMEM((G, ZC, COLS, 2, PAIRS, LANES), BF),
            pltpu.VMEM((G // 2 + 1, ROWS, COLS, 2, PAIRS, LANES), BF),
            pltpu.VMEM((G, ZC, COLS, 2, PAIRS, LANES), BF),
            pltpu.VMEM((G, COLS, ZC, 2, PAIRS, LANES), BF),
            pltpu.VMEM((TALL, LANES), F32),
            pltpu.VMEM((2, COLS * LANES, YG), BF),
            pltpu.VMEM((2 * YG, COLS * LANES), BF),
            pltpu.VMEM((XG, KX), BF),
            pltpu.VMEM((KX, XG), BF),
            pltpu.VMEM((KX, 2 * YG), BF),
            pltpu.VMEM((XG, 2 * YG), BF),
            pltpu.VMEM((2, modes, NZ), F32),
            pltpu.VMEM((ZPART,), F32),
            pltpu.VMEM((ZG, NZ), BF),
            pltpu.VMEM((KY, YG), BF),
            pltpu.VMEM((YG, KY), BF),
            pltpu.VMEM((NZ, NZ), BF),
            pltpu.VMEM((NZ, NZ), BF),
            dma((5,)),
            dma((G, COLS)), dma((G, COLS)), dma((G // 2 + 1, ROWS)), dma((G // 2 + 1, ROWS)),
            dma((G // 2 + 1, ROWS)), dma((G, ZC)), dma((G, COLS)), dma((G, COLS)),
            dma, dma,
        ],
        compiler_params=pltpu.CompilerParams(
            collective_id=0, has_side_effects=True, vmem_limit_bytes=VMEM_LIMIT
        ),
        name="section",
    )(
        vel_w.reshape(modes, NZ), buoy.reshape(modes, NZ), *consts, strat, eig_val, eig_left, eig_right
    )
    return new_buoy.reshape(buoy.shape), new_vel.reshape(buoy.shape)


def solution(mesh):
    in_specs = (P("row", "col", None), P("row", "col", None), P("col"), P(), P(), P())
    out_specs = (P("row", "col", None), P("row", "col", None))
    return jax.shard_map(
        per_device, mesh=mesh, in_specs=in_specs, out_specs=out_specs, check_vma=False
    )
```

```python
import functools
import math

import jax
import jax.numpy as jnp
import numpy as np
from jax import lax
from jax.experimental import pallas as pl
from jax.experimental.pallas import tpu as pltpu
from jax.sharding import PartitionSpec as P

KX = 512
KY = 512
NZ = 384
XG = 768
YG = 768
ZG = 576

explicit_step = 0.5
diffuse_buoy = 0.5
diffuse_vel = 0.25
couple_buoy = 0.7
couple_vel = 0.7

ROWS = 16
COLS = 8
A = KX // ROWS
K = KY // COLS
PAIRS = A // 2
LANES = 2 * K
G = 9
PASSES = 3
ZPART = ZG // COLS
ZC = ZPART // G
SIZE = ZC * PAIRS
TWO = 2 * LANES
TALL = 4 * COLS * SIZE
ENDS = (4, 8, 9)
BF = jnp.bfloat16
F32 = jnp.float32
MESH = pl.DeviceIdType.MESH
VMEM_LIMIT = 67_000_000


def trig(modes, points):
    order = np.arange(modes)
    freq = ((order + 1) // 2).astype(np.float32)
    step = np.float32(2.0 * math.pi / points)
    angle = (step * freq)[:, None] * np.arange(points, dtype=np.float32)[None, :]
    angle = angle.astype(np.float64)
    values = np.where((order % 2 == 0)[:, None], np.cos(angle), np.sin(angle))
    return order, values.astype(np.float32)


def fourier_eval(modes, points):
    _, values = trig(modes, points)
    return (values * np.float32(math.sqrt(2.0 / modes))).astype(BF)


def fourier_proj(modes, points):
    order, values = trig(modes, points)
    weight = np.where(order == 0, 1.0 / points, 2.0 / points).astype(np.float32)
    return (values * weight[:, None] * np.float32(math.sqrt(modes / 2.0))).T.astype(BF)


def cheb_tables(degree, points):
    order = np.arange(degree, dtype=np.float32)
    theta = np.float32(math.pi) * (np.arange(points, dtype=np.float32) + np.float32(0.5))
    theta = theta / np.float32(points)
    angle = (order[:, None] * theta[None, :]).astype(np.float64)
    cos, sin = np.cos(angle).astype(np.float32), np.sin(angle).astype(np.float32)
    norm = np.float32(math.sqrt(2.0 / degree))
    weight = np.where(order == 0, 1.0 / points, 2.0 / points).astype(np.float32)
    levels = cos * norm
    slopes = -(order[:, None] / np.float32(degree)) * sin * norm
    projector = (cos * weight[:, None] * np.float32(math.sqrt(degree / 2.0))).T
    return levels.astype(BF), slopes.astype(BF), projector.astype(BF)


def tables():
    levels, slopes, projector = cheb_tables(NZ, ZG)

    def by_chunk(rows):
        return np.asarray(rows).reshape(COLS, ZC, G, NZ).transpose(2, 0, 1, 3).reshape(ZG, NZ)

    lift, slope = (by_chunk(np.asarray(t).T).reshape(PASSES, -1, NZ) for t in (levels, slopes))
    return lift, slope, by_chunk(projector), fourier_eval(KY, YG), np.ascontiguousarray(fourier_proj(KY, YG))


def mm(left, right, dims=((1,), (0,))):
    return lax.dot_general(left, right, (dims, ((), ())), preferred_element_type=F32)


def kernel(
    vel, buoy, lift, slope, drop_in, evals_in, projs_in, strat, eig_val, left_in, right_in,
    out_buoy, out_vel,
    lifted, arrived, planes, passed, folded, tall, wide_eval, wide_proj, eval_x, proj_x, middle, flux, partial,
    strat_in, drop, evals, projs, eig_left, eig_right, load_s,
    colf_s, colf_r, rowf_s, rowf_r, rowb_s, rowb_r, colb_s, colb_r, strat_s, strat_r,
):
    row, col = lax.axis_index("row"), lax.axis_index("col")
    high = row // (ROWS // 2)
    base, low = (col // 2) * 2, col % 2
    part = base + (low + high) % 2

    def col_of(q):
        return (row, (q // 2) * 2 + (q % 2 + high) % 2)

    def row_of(t):
        return (t, base + (low + high + t // (ROWS // 2)) % 2)

    barrier = pltpu.get_barrier_semaphore()

    @pl.loop(1, COLS)
    def _(i):
        pl.semaphore_signal(barrier, inc=1, device_id=col_of((part + i) % COLS), device_id_type=MESH)

    @pl.loop(1, ROWS)
    def _(i):
        pl.semaphore_signal(barrier, inc=1, device_id=row_of((row + i) % ROWS), device_id_type=MESH)

    loads = [
        pltpu.make_async_copy(src, dst, load_s.at[n])
        for n, (src, dst) in enumerate(
            ((evals_in, evals), (projs_in, projs), (drop_in, drop), (left_in, eig_left), (right_in, eig_right))
        )
    ]
    for load in loads:
        load.start()

    def remote(src, dst, send, recv, device):
        return pltpu.make_async_remote_copy(
            src_ref=src, dst_ref=dst, send_sem=send, recv_sem=recv, device_id=device, device_id_type=MESH
        )

    chip, core = row // 2, row % 2

    def col_fwd(g, q):
        return remote(lifted.at[g, q], arrived.at[g, :, col], colf_s.at[g, q], colf_r.at[g, col], col_of(q))

    def col_fwd_in(g, s):
        block = arrived.at[g, :, s]
        return remote(block, block, colf_s.at[g, s], colf_r.at[g, s], col_of(0))

    def col_fwd_own(g):
        return pltpu.make_async_copy(lifted.at[g, part], arrived.at[g, :, col], colf_r.at[g, col])

    def col_back(g, s):
        return remote(passed.at[g, :, s], folded.at[g, part], colb_s.at[g, s], colb_r.at[g, part], (row, s))

    def col_back_in(g, q):
        block = folded.at[g, q]
        return remote(block, block, colb_s.at[g, q], colb_r.at[g, q], col_of(q))

    def col_back_own(g):
        return pltpu.make_async_copy(passed.at[g, :, col], folded.at[g, part], colb_r.at[g, part])

    def others(first, count, do):
        @pl.loop(1, count)
        def _(i):
            do((first + i) % count)

    def row_fwd(g, t):
        m = g // 2
        return remote(arrived.at[g, t // 2], planes.at[m, row], rowf_s.at[m, t], rowf_r.at[m, row], row_of(t))

    def row_fwd_in(m, t):
        block = planes.at[m, t]
        return remote(block, block, rowf_s.at[m, t], rowf_r.at[m, t], row_of(t))

    def row_fwd_own(g):
        m = g // 2
        return pltpu.make_async_copy(arrived.at[g, chip], planes.at[m, row], rowf_r.at[m, row])

    def row_back(m, g, t):
        return remote(planes.at[m, t], passed.at[g, chip], rowb_s.at[m, t], rowb_r.at[g, chip], row_of(t))

    def row_back_in(g, t):
        block = passed.at[g, t // 2]
        return remote(block, block, rowb_s.at[0, t], rowb_r.at[g, t // 2], row_of(t))

    def row_back_own(m, g):
        return pltpu.make_async_copy(planes.at[m, row], passed.at[g, chip], rowb_r.at[g, chip])

    def chips(side, here, there):
        @pl.loop(0, ZC)
        def _(i):
            t = ((chip + i) % ZC) * 2 + side
            pl.when(t == row)(lambda: here())
            pl.when(t != row)(lambda: there(t))

    def members(here, there):
        chips(core, here, there)
        chips(1 - core, here, there)

    def relay_fwd(g):
        others(col, COLS, lambda s: col_fwd_in(g, s).wait_recv())
        col_fwd_own(g).wait()

        @pl.when(g < G - 1)
        def _():
            chips(g % 2, lambda: row_fwd_own(g).start(), lambda t: row_fwd(g, t).start())

        @pl.when(g == G - 1)
        def _():
            members(lambda: row_fwd_own(g).start(), lambda t: row_fwd(g, t).start())

    def relay_back(g):
        side = jnp.where(g == G - 1, core, g % 2)
        chips(side, lambda: row_back_own(0, g).wait(), lambda t: row_back_in(g, t).wait_recv())
        others(col, COLS, lambda s: col_back(g, s).start())
        col_back_own(g).start()

    count = ZG // PASSES
    chunks = G // PASSES

    def to_points(u):
        for f, (table, field) in enumerate(((lift, vel), (slope, buoy))):

            @pl.loop(0, PAIRS // 2)
            def _(p):
                rows = pl.ds(pl.multiple_of(p * TWO, TWO), TWO)
                values = mm(table[u], field[rows, :], ((1,), (1,)))
                tall[pl.ds(2 * p, count, stride=PAIRS), :] = values[:, :LANES]
                tall[pl.ds(2 * p + 1, count, stride=PAIRS), :] = values[:, LANES:]

            @pl.loop(0, COLS * chunks)
            def _(i):
                rows = pl.ds(pl.multiple_of(i * SIZE, SIZE), SIZE)
                block = tall[rows, :].astype(BF).reshape(ZC, PAIRS, LANES)
                lifted[u * chunks + i // COLS, i % COLS, :, f] = block

    def send_points(u):
        @pl.loop(u * chunks, (u + 1) * chunks)
        def _(g):
            others(part, COLS, lambda q: col_fwd(g, q).start())
            col_fwd_own(g).start()

    to_points(0)
    pl.semaphore_wait(barrier, COLS + ROWS - 2)
    send_points(0)
    swap = remote(strat, strat_in, strat_s, strat_r, (row, base + 1 - low))
    swap.start()

    @pl.loop(1, PASSES)
    def _(u):
        to_points(u)
        send_points(u)

    for load in loads:
        load.wait()

    @pl.loop(0, COLS)
    def _(s):
        for a in range(2):
            own = pl.ds(pl.multiple_of(s * LANES + a * K, K), K)
            other = pl.ds(pl.multiple_of(s * LANES + (1 - a) * K, K), K)
            wide_eval[a, own, :] = evals[pl.ds(pl.multiple_of(s * K, K), K), :]
            wide_eval[a, other, :] = jnp.zeros((K, YG), BF)

    relay_fwd(0)

    lane = lax.broadcasted_iota(jnp.int32, (LANES, LANES), 1)

    @pl.loop(0, YG // LANES)
    def _(i):
        for j in range(COLS // 2):
            rows = pl.ds(pl.multiple_of(i * LANES, LANES), LANES)
            tile = projs[rows, j * LANES : (j + 1) * LANES].astype(F32)
            turned = pltpu.roll(tile, K, 1)
            for s in (2 * j, 2 * j + 1):
                straight, moved = (tile, turned) if s % 2 == 0 else (turned, tile)
                for a in range(2):
                    keep = jnp.where((lane < K) == (a == 0), straight if a == 0 else moved, 0.0).astype(BF)
                    to = pl.ds(pl.multiple_of(a * YG + i * LANES, LANES), LANES)
                    wide_proj[to, s * LANES : (s + 1) * LANES] = keep

    @pl.loop(0, XG // LANES)
    def _(j):
        points = pl.ds(pl.multiple_of(j * LANES, LANES), LANES)

        def ordered(values):
            tall[:KX, :] = values
            return jnp.concatenate([tall[pl.ds(a, KX // 2, stride=2), :] for a in range(2)], axis=0)

        eval_x[points, :] = ordered(evals[:, points].astype(F32)).T.astype(BF)
        proj_x[:, points] = ordered(projs[points, :].astype(F32).T).astype(BF)

    pl.loop(1, 5)(relay_fwd)
    swap.wait()
    strata = jnp.where(high == 0, strat[...], strat_in[...]).reshape(1, ZPART)
    level_of = lax.broadcasted_iota(jnp.int32, (1, ZPART), 1)

    half = KX // 2
    last = G // 2

    @pl.loop(0, last + 1)
    def _(m):
        chunk = jnp.where(m == last, G - 1, 2 * m + core)
        members(lambda: row_fwd_own(2 * m).wait(), lambda t: row_fwd_in(m, t).wait_recv())
        for f in range(2):
            left = jnp.concatenate([planes[m, :, s, f].reshape(half, LANES) for s in range(COLS)], axis=1)
            for a in range(2):
                middle[a * half : (a + 1) * half, f * YG : (f + 1) * YG] = mm(left, wide_eval[a]).astype(BF)

        pl.when(2 * m + 5 < G)(lambda: relay_fwd(2 * m + 5))

        level = jnp.sum(jnp.where(level_of == chip * G + chunk, strata, 0.0), axis=1, keepdims=True)
        tile = XG // 3

        @pl.loop(0, 3)
        def _(x):
            rows = pl.ds(pl.multiple_of(x * tile, tile), tile)
            velocity = mm(eval_x[rows, :], middle[:, :YG]).astype(BF).astype(F32)
            gradient = mm(eval_x[rows, :], middle[:, YG:]).astype(BF).astype(F32)
            flux[rows, :YG] = (-(velocity * gradient) - level * velocity).astype(BF)
            flux[rows, YG:] = (-(velocity * jnp.abs(velocity))).astype(BF)

        pl.when(2 * m + 6 < G)(lambda: relay_fwd(2 * m + 6))

        @pl.loop(0, 2)
        def _(a):
            rows = pl.ds(pl.multiple_of(a * half, half), half)
            for f in range(2):
                middle[rows, f * YG : (f + 1) * YG] = mm(proj_x[rows, :], flux[:, f * YG : (f + 1) * YG]).astype(BF)
        for f in range(2):
            left = jnp.concatenate(
                [middle[a * half : (a + 1) * half, f * YG : (f + 1) * YG] for a in range(2)], axis=1
            )
            values = mm(left, wide_proj[...]).astype(BF)
            for s in range(COLS):
                planes[m, :, s, f] = values[:, s * LANES : (s + 1) * LANES].reshape(ROWS, PAIRS, LANES)

        def here():
            row_back_own(m, chunk).start()

        def there(t):
            row_back(m, chunk, t).start()

        chips(core, here, there)
        pl.when(m < last)(lambda: chips(1 - core, here, there))

        @pl.when(m == last - 1)
        def _():
            pl.loop(0, 2)(relay_back)

    def gather(first, last, f, start):
        @pl.loop(first, last)
        def _(g):
            for q in range(COLS):
                place = pl.multiple_of(start + ((g - first) * COLS + q) * SIZE, SIZE)
                tall[pl.ds(place, SIZE), :] = folded[g, q, :, f].reshape(SIZE, LANES).astype(F32)

    def tendency(first, last, p, start):
        count = (last - first) * COLS * ZC
        columns = [tall[pl.ds(start + 2 * p + a, count, stride=PAIRS), :].astype(BF) for a in range(2)]
        rows = slice(first * COLS * ZC, last * COLS * ZC)
        return mm(jnp.concatenate(columns, axis=1), drop[rows, :], ((0,), (0,)))

    def wait_modes(first, last):
        @pl.loop(first, last)
        def _(g):
            others(part, COLS, lambda q: col_back_in(g, q).wait_recv())
            col_back_own(g).wait()

    pl.loop(2, ENDS[0] + 2)(relay_back)
    wait_modes(0, ENDS[0])
    for f in range(2):
        gather(0, ENDS[0], f, 0)

        @pl.loop(0, PAIRS // 2)
        def _(p):
            rows = pl.ds(pl.multiple_of(p * TWO, TWO), TWO)
            partial[f, rows, :] = tendency(0, ENDS[0], p, 0)

    pl.loop(ENDS[0] + 2, G)(relay_back)
    wait_modes(ENDS[0], ENDS[1])
    for f in range(2):
        gather(ENDS[0], ENDS[1], f, 0)

        @pl.loop(0, PAIRS // 2)
        def _(p):
            rows = pl.ds(pl.multiple_of(p * TWO, TWO), TWO)
            partial[f, rows, :] += tendency(ENDS[0], ENDS[1], p, 0)

    wait_modes(ENDS[1], G)
    start = (G - ENDS[1]) * COLS * SIZE
    for f in range(2):
        gather(ENDS[1], G, f, f * start)

    @pl.loop(0, PAIRS // 2)
    def _(p):
        rows = pl.ds(pl.multiple_of(p * TWO, TWO), TWO)
        modal = []
        for f, field in enumerate((buoy, vel)):
            tend = partial[f, rows, :] + tendency(ENDS[1], G, p, f * start)
            rhs = (field[rows, :].astype(F32) + explicit_step * tend).astype(BF)
            modal.append(mm(rhs, eig_left[...]))
        modal_buoy, modal_vel = modal
        place = p * TWO + lax.broadcasted_iota(jnp.int32, (TWO, LANES), 0)
        freq_x = ((row * A + (place >> 6) + 1) >> 1).astype(F32) * (2.0 / KX)
        freq_y = ((col * K + (place & (K - 1)) + 1) >> 1).astype(F32) * (2.0 / KY)
        wave = 4.0 * (freq_x * freq_x + freq_y * freq_y)
        lapl = jnp.concatenate([wave] * (NZ // LANES), axis=1) + eig_val[...].reshape(1, NZ)
        diag_buoy = 1.0 + diffuse_buoy * lapl
        diag_vel = 1.0 + diffuse_vel * lapl
        inverse = 1.0 / (diag_buoy * diag_vel + couple_buoy * couple_vel)
        solved_buoy = ((diag_vel * modal_buoy - couple_buoy * modal_vel) * inverse).astype(BF)
        solved_vel = ((diag_buoy * modal_vel + couple_vel * modal_buoy) * inverse).astype(BF)
        out_buoy[rows, :] = mm(solved_buoy, eig_right[...]).astype(BF)
        out_vel[rows, :] = mm(solved_vel, eig_right[...]).astype(BF)

    @pl.loop(0, G)
    def _(g):
        others(part, COLS, lambda q: col_fwd(g, q).wait_send())
        others(col, COLS, lambda s: col_back(g, s).wait_send())

    def nothing():
        pass

    @pl.loop(0, last)
    def _(m):
        members(nothing, lambda t: row_fwd(2 * m, t).wait_send())
        members(nothing, lambda t: row_back(m, 2 * m, t).wait_send())

    members(nothing, lambda t: row_fwd(G - 1, t).wait_send())
    chips(core, nothing, lambda t: row_back(last, G - 1, t).wait_send())


def per_device(buoy, vel_w, strat, eig_val, eig_left, eig_right):
    modes = A * K
    dma = pltpu.SemaphoreType.DMA
    vmem = pl.BlockSpec(memory_space=pltpu.VMEM)
    hbm = pl.BlockSpec(memory_space=pl.ANY)
    shape = jax.ShapeDtypeStruct((modes, NZ), BF)
    consts = [jnp.asarray(t) for t in tables()]
    new_buoy, new_vel = pl.pallas_call(
        kernel,
        out_shape=(shape, shape),
        in_specs=[vmem] * 4 + [hbm] * 3 + [vmem] * 2 + [hbm] * 2,
        out_specs=(vmem, vmem),
        scratch_shapes=[
            pltpu.VMEM((G, COLS, ZC, 2, PAIRS, LANES), BF),
            pltpu.VMEM((G, ZC, COLS, 2, PAIRS, LANES), BF),
            pltpu.VMEM((G // 2 + 1, ROWS, COLS, 2, PAIRS, LANES), BF),
            pltpu.VMEM((G, ZC, COLS, 2, PAIRS, LANES), BF),
            pltpu.VMEM((G, COLS, ZC, 2, PAIRS, LANES), BF),
            pltpu.VMEM((TALL, LANES), F32),
            pltpu.VMEM((2, COLS * LANES, YG), BF),
            pltpu.VMEM((2 * YG, COLS * LANES), BF),
            pltpu.VMEM((XG, KX), BF),
            pltpu.VMEM((KX, XG), BF),
            pltpu.VMEM((KX, 2 * YG), BF),
            pltpu.VMEM((XG, 2 * YG), BF),
            pltpu.VMEM((2, modes, NZ), F32),
            pltpu.VMEM((ZPART,), F32),
            pltpu.VMEM((ZG, NZ), BF),
            pltpu.VMEM((KY, YG), BF),
            pltpu.VMEM((YG, KY), BF),
            pltpu.VMEM((NZ, NZ), BF),
            pltpu.VMEM((NZ, NZ), BF),
            dma((5,)),
            dma((G, COLS)), dma((G, COLS)), dma((G // 2 + 1, ROWS)), dma((G // 2 + 1, ROWS)),
            dma((G // 2 + 1, ROWS)), dma((G, ZC)), dma((G, COLS)), dma((G, COLS)),
            dma, dma,
        ],
        compiler_params=pltpu.CompilerParams(
            collective_id=0, has_side_effects=True, vmem_limit_bytes=VMEM_LIMIT
        ),
        name="section",
    )(
        vel_w.reshape(modes, NZ), buoy.reshape(modes, NZ), *consts, strat, eig_val, eig_left, eig_right
    )
    return new_buoy.reshape(buoy.shape), new_vel.reshape(buoy.shape)


def solution(mesh):
    in_specs = (P("row", "col", None), P("row", "col", None), P("col"), P(), P(), P())
    out_specs = (P("row", "col", None), P("row", "col", None))
    return jax.shard_map(
        per_device, mesh=mesh, in_specs=in_specs, out_specs=out_specs, check_vma=False
    )
```

```python
import functools
import math

import jax
import jax.numpy as jnp
import numpy as np
from jax import lax
from jax.experimental import pallas as pl
from jax.experimental.pallas import tpu as pltpu
from jax.sharding import PartitionSpec as P

KX = 512
KY = 512
NZ = 384
XG = 768
YG = 768
ZG = 576

explicit_step = 0.5
diffuse_buoy = 0.5
diffuse_vel = 0.25
couple_buoy = 0.7
couple_vel = 0.7

ROWS = 16
COLS = 8
A = KX // ROWS
K = KY // COLS
PAIRS = A // 2
LANES = 2 * K
G = 9
PASSES = 3
ZPART = ZG // COLS
ZC = ZPART // G
SIZE = ZC * PAIRS
TWO = 2 * LANES
TALL = 4 * COLS * SIZE
ENDS = (4, 8, 9)
BF = jnp.bfloat16
F32 = jnp.float32
MESH = pl.DeviceIdType.MESH
VMEM_LIMIT = 67_000_000


def trig(modes, points):
    order = np.arange(modes)
    freq = ((order + 1) // 2).astype(np.float32)
    step = np.float32(2.0 * math.pi / points)
    angle = (step * freq)[:, None] * np.arange(points, dtype=np.float32)[None, :]
    angle = angle.astype(np.float64)
    values = np.where((order % 2 == 0)[:, None], np.cos(angle), np.sin(angle))
    return order, values.astype(np.float32)


def fourier_eval(modes, points):
    _, values = trig(modes, points)
    return (values * np.float32(math.sqrt(2.0 / modes))).astype(BF)


def fourier_proj(modes, points):
    order, values = trig(modes, points)
    weight = np.where(order == 0, 1.0 / points, 2.0 / points).astype(np.float32)
    return (values * weight[:, None] * np.float32(math.sqrt(modes / 2.0))).T.astype(BF)


def cheb_tables(degree, points):
    order = np.arange(degree, dtype=np.float32)
    theta = np.float32(math.pi) * (np.arange(points, dtype=np.float32) + np.float32(0.5))
    theta = theta / np.float32(points)
    angle = (order[:, None] * theta[None, :]).astype(np.float64)
    cos, sin = np.cos(angle).astype(np.float32), np.sin(angle).astype(np.float32)
    norm = np.float32(math.sqrt(2.0 / degree))
    weight = np.where(order == 0, 1.0 / points, 2.0 / points).astype(np.float32)
    levels = cos * norm
    slopes = -(order[:, None] / np.float32(degree)) * sin * norm
    projector = (cos * weight[:, None] * np.float32(math.sqrt(degree / 2.0))).T
    return levels.astype(BF), slopes.astype(BF), projector.astype(BF)


def tables():
    levels, slopes, projector = cheb_tables(NZ, ZG)

    def by_chunk(rows):
        return np.asarray(rows).reshape(COLS, ZC, G, NZ).transpose(2, 0, 1, 3).reshape(ZG, NZ)

    lift, slope = (by_chunk(np.asarray(t).T).reshape(PASSES, -1, NZ) for t in (levels, slopes))
    return lift, slope, by_chunk(projector), fourier_eval(KY, YG), np.ascontiguousarray(fourier_proj(KY, YG))


def mm(left, right, dims=((1,), (0,))):
    return lax.dot_general(left, right, (dims, ((), ())), preferred_element_type=F32)


def kernel(
    vel, buoy, lift, slope, drop_in, evals_in, projs_in, strat, eig_val, left_in, right_in,
    out_buoy, out_vel,
    lifted, arrived, planes, passed, folded, tall, wide_eval, wide_proj, eval_x, proj_x, middle, flux, partial,
    strat_in, drop, evals, projs, eig_left, eig_right, load_s,
    colf_s, colf_r, rowf_s, rowf_r, rowb_s, rowb_r, colb_s, colb_r, strat_s, strat_r,
):
    row, col = lax.axis_index("row"), lax.axis_index("col")
    high = row // (ROWS // 2)
    base, low = (col // 2) * 2, col % 2
    part = base + (low + high) % 2

    def col_of(q):
        return (row, (q // 2) * 2 + (q % 2 + high) % 2)

    def row_of(t):
        return (t, base + (low + high + t // (ROWS // 2)) % 2)

    barrier = pltpu.get_barrier_semaphore()

    @pl.loop(1, COLS)
    def _(i):
        pl.semaphore_signal(barrier, inc=1, device_id=col_of((part + i) % COLS), device_id_type=MESH)

    @pl.loop(1, ROWS)
    def _(i):
        pl.semaphore_signal(barrier, inc=1, device_id=row_of((row + i) % ROWS), device_id_type=MESH)

    loads = [
        pltpu.make_async_copy(src, dst, load_s.at[n])
        for n, (src, dst) in enumerate(
            ((evals_in, evals), (projs_in, projs), (drop_in, drop), (left_in, eig_left), (right_in, eig_right))
        )
    ]
    for load in loads:
        load.start()

    def remote(src, dst, send, recv, device):
        return pltpu.make_async_remote_copy(
            src_ref=src, dst_ref=dst, send_sem=send, recv_sem=recv, device_id=device, device_id_type=MESH
        )

    chip, core = row // 2, row % 2

    def col_fwd(g, q):
        return remote(lifted.at[g, q], arrived.at[g, :, col], colf_s.at[g, q], colf_r.at[g, col], col_of(q))

    def col_fwd_in(g, s):
        block = arrived.at[g, :, s]
        return remote(block, block, colf_s.at[g, s], colf_r.at[g, s], col_of(0))

    def col_fwd_own(g):
        return pltpu.make_async_copy(lifted.at[g, part], arrived.at[g, :, col], colf_r.at[g, col])

    def col_back(g, s):
        return remote(passed.at[g, :, s], folded.at[g, part], colb_s.at[g, s], colb_r.at[g, part], (row, s))

    def col_back_in(g, q):
        block = folded.at[g, q]
        return remote(block, block, colb_s.at[g, q], colb_r.at[g, q], col_of(q))

    def col_back_own(g):
        return pltpu.make_async_copy(passed.at[g, :, col], folded.at[g, part], colb_r.at[g, part])

    def others(first, count, do):
        @pl.loop(1, count)
        def _(i):
            do((first + i) % count)

    def row_fwd(g, t):
        m = g // 2
        return remote(arrived.at[g, t // 2], planes.at[m, row], rowf_s.at[m, t], rowf_r.at[m, row], row_of(t))

    def row_fwd_in(m, t):
        block = planes.at[m, t]
        return remote(block, block, rowf_s.at[m, t], rowf_r.at[m, t], row_of(t))

    def row_fwd_own(g):
        m = g // 2
        return pltpu.make_async_copy(arrived.at[g, chip], planes.at[m, row], rowf_r.at[m, row])

    def row_back(m, g, t):
        return remote(planes.at[m, t], passed.at[g, chip], rowb_s.at[m, t], rowb_r.at[g, chip], row_of(t))

    def row_back_in(g, t):
        block = passed.at[g, t // 2]
        return remote(block, block, rowb_s.at[0, t], rowb_r.at[g, t // 2], row_of(t))

    def row_back_own(m, g):
        return pltpu.make_async_copy(planes.at[m, row], passed.at[g, chip], rowb_r.at[g, chip])

    def chips(side, here, there):
        @pl.loop(0, ZC)
        def _(i):
            t = ((chip + i) % ZC) * 2 + side
            pl.when(t == row)(lambda: here())
            pl.when(t != row)(lambda: there(t))

    def members(here, there):
        chips(core, here, there)
        chips(1 - core, here, there)

    def relay_fwd(g):
        others(col, COLS, lambda s: col_fwd_in(g, s).wait_recv())
        col_fwd_own(g).wait()

        chips(g % 2, lambda: row_fwd_own(g).start(), lambda t: row_fwd(g, t).start())

    def relay_back(g):
        chips(g % 2, lambda: row_back_own(0, g).wait(), lambda t: row_back_in(g, t).wait_recv())
        others(col, COLS, lambda s: col_back(g, s).start())
        col_back_own(g).start()

    count = ZG // PASSES
    chunks = G // PASSES

    def to_points(u):
        for f, (table, field) in enumerate(((lift, vel), (slope, buoy))):

            @pl.loop(0, PAIRS // 2)
            def _(p):
                rows = pl.ds(pl.multiple_of(p * TWO, TWO), TWO)
                values = mm(table[u], field[rows, :], ((1,), (1,)))
                tall[pl.ds(2 * p, count, stride=PAIRS), :] = values[:, :LANES]
                tall[pl.ds(2 * p + 1, count, stride=PAIRS), :] = values[:, LANES:]

            @pl.loop(0, COLS * chunks)
            def _(i):
                rows = pl.ds(pl.multiple_of(i * SIZE, SIZE), SIZE)
                block = tall[rows, :].astype(BF).reshape(ZC, PAIRS, LANES)
                lifted[u * chunks + i // COLS, i % COLS, :, f] = block

    def send_points(u):
        @pl.loop(u * chunks, (u + 1) * chunks)
        def _(g):
            others(part, COLS, lambda q: col_fwd(g, q).start())
            col_fwd_own(g).start()

    to_points(0)
    pl.semaphore_wait(barrier, COLS + ROWS - 2)
    send_points(0)
    swap = remote(strat, strat_in, strat_s, strat_r, (row, base + 1 - low))
    swap.start()

    @pl.loop(1, PASSES)
    def _(u):
        to_points(u)
        send_points(u)

    for load in loads:
        load.wait()

    @pl.loop(0, COLS)
    def _(s):
        for a in range(2):
            own = pl.ds(pl.multiple_of(s * LANES + a * K, K), K)
            other = pl.ds(pl.multiple_of(s * LANES + (1 - a) * K, K), K)
            wide_eval[a, own, :] = evals[pl.ds(pl.multiple_of(s * K, K), K), :]
            wide_eval[a, other, :] = jnp.zeros((K, YG), BF)

    relay_fwd(0)

    lane = lax.broadcasted_iota(jnp.int32, (LANES, LANES), 1)

    @pl.loop(0, YG // LANES)
    def _(i):
        for j in range(COLS // 2):
            rows = pl.ds(pl.multiple_of(i * LANES, LANES), LANES)
            tile = projs[rows, j * LANES : (j + 1) * LANES].astype(F32)
            turned = pltpu.roll(tile, K, 1)
            for s in (2 * j, 2 * j + 1):
                straight, moved = (tile, turned) if s % 2 == 0 else (turned, tile)
                for a in range(2):
                    keep = jnp.where((lane < K) == (a == 0), straight if a == 0 else moved, 0.0).astype(BF)
                    to = pl.ds(pl.multiple_of(a * YG + i * LANES, LANES), LANES)
                    wide_proj[to, s * LANES : (s + 1) * LANES] = keep

    @pl.loop(0, XG // LANES)
    def _(j):
        points = pl.ds(pl.multiple_of(j * LANES, LANES), LANES)

        def ordered(values):
            tall[:KX, :] = values
            return jnp.concatenate([tall[pl.ds(a, KX // 2, stride=2), :] for a in range(2)], axis=0)

        eval_x[points, :] = ordered(evals[:, points].astype(F32)).T.astype(BF)
        proj_x[:, points] = ordered(projs[points, :].astype(F32).T).astype(BF)

    pl.loop(1, 5)(relay_fwd)
    swap.wait()
    strata = jnp.where(high == 0, strat[...], strat_in[...]).reshape(1, ZPART)
    level_of = lax.broadcasted_iota(jnp.int32, (1, ZPART), 1)

    half = KX // 2
    last = G // 2

    @pl.loop(0, last + 1 - core)
    def _(m):
        chunk = 2 * m + core
        members(lambda: row_fwd_own(2 * m).wait(), lambda t: row_fwd_in(m, t).wait_recv())
        for f in range(2):
            left = jnp.concatenate([planes[m, :, s, f].reshape(half, LANES) for s in range(COLS)], axis=1)
            for a in range(2):
                middle[a * half : (a + 1) * half, f * YG : (f + 1) * YG] = mm(left, wide_eval[a]).astype(BF)

        pl.when(2 * m + 5 < G)(lambda: relay_fwd(2 * m + 5))

        level = jnp.sum(jnp.where(level_of == chip * G + chunk, strata, 0.0), axis=1, keepdims=True)
        tile = XG // 3

        @pl.loop(0, 3)
        def _(x):
            rows = pl.ds(pl.multiple_of(x * tile, tile), tile)
            velocity = mm(eval_x[rows, :], middle[:, :YG]).astype(BF).astype(F32)
            gradient = mm(eval_x[rows, :], middle[:, YG:]).astype(BF).astype(F32)
            flux[rows, :YG] = (-(velocity * gradient) - level * velocity).astype(BF)
            flux[rows, YG:] = (-(velocity * jnp.abs(velocity))).astype(BF)

        pl.when(2 * m + 6 < G)(lambda: relay_fwd(2 * m + 6))

        @pl.loop(0, 2)
        def _(a):
            rows = pl.ds(pl.multiple_of(a * half, half), half)
            for f in range(2):
                middle[rows, f * YG : (f + 1) * YG] = mm(proj_x[rows, :], flux[:, f * YG : (f + 1) * YG]).astype(BF)
        for f in range(2):
            left = jnp.concatenate(
                [middle[a * half : (a + 1) * half, f * YG : (f + 1) * YG] for a in range(2)], axis=1
            )
            values = mm(left, wide_proj[...]).astype(BF)
            for s in range(COLS):
                planes[m, :, s, f] = values[:, s * LANES : (s + 1) * LANES].reshape(ROWS, PAIRS, LANES)

        members(lambda: row_back_own(m, chunk).start(), lambda t: row_back(m, chunk, t).start())

        @pl.when(m == last - 1)
        def _():
            pl.loop(0, 2)(relay_back)

    def gather(first, last, f, start):
        @pl.loop(first, last)
        def _(g):
            for q in range(COLS):
                place = pl.multiple_of(start + ((g - first) * COLS + q) * SIZE, SIZE)
                tall[pl.ds(place, SIZE), :] = folded[g, q, :, f].reshape(SIZE, LANES).astype(F32)

    def tendency(first, last, p, start):
        count = (last - first) * COLS * ZC
        columns = [tall[pl.ds(start + 2 * p + a, count, stride=PAIRS), :].astype(BF) for a in range(2)]
        rows = slice(first * COLS * ZC, last * COLS * ZC)
        return mm(jnp.concatenate(columns, axis=1), drop[rows, :], ((0,), (0,)))

    def wait_modes(first, last):
        @pl.loop(first, last)
        def _(g):
            others(part, COLS, lambda q: col_back_in(g, q).wait_recv())
            col_back_own(g).wait()

    pl.loop(2, ENDS[0] + 2)(relay_back)
    wait_modes(0, ENDS[0])
    for f in range(2):
        gather(0, ENDS[0], f, 0)

        @pl.loop(0, PAIRS // 2)
        def _(p):
            rows = pl.ds(pl.multiple_of(p * TWO, TWO), TWO)
            partial[f, rows, :] = tendency(0, ENDS[0], p, 0)

    pl.loop(ENDS[0] + 2, G)(relay_back)
    wait_modes(ENDS[0], ENDS[1])
    for f in range(2):
        gather(ENDS[0], ENDS[1], f, 0)

        @pl.loop(0, PAIRS // 2)
        def _(p):
            rows = pl.ds(pl.multiple_of(p * TWO, TWO), TWO)
            partial[f, rows, :] += tendency(ENDS[0], ENDS[1], p, 0)

    wait_modes(ENDS[1], G)
    start = (G - ENDS[1]) * COLS * SIZE
    for f in range(2):
        gather(ENDS[1], G, f, f * start)

    @pl.loop(0, PAIRS // 2)
    def _(p):
        rows = pl.ds(pl.multiple_of(p * TWO, TWO), TWO)
        modal = []
        for f, field in enumerate((buoy, vel)):
            tend = partial[f, rows, :] + tendency(ENDS[1], G, p, f * start)
            rhs = (field[rows, :].astype(F32) + explicit_step * tend).astype(BF)
            modal.append(mm(rhs, eig_left[...]))
        modal_buoy, modal_vel = modal
        place = p * TWO + lax.broadcasted_iota(jnp.int32, (TWO, LANES), 0)
        freq_x = ((row * A + (place >> 6) + 1) >> 1).astype(F32) * (2.0 / KX)
        freq_y = ((col * K + (place & (K - 1)) + 1) >> 1).astype(F32) * (2.0 / KY)
        wave = 4.0 * (freq_x * freq_x + freq_y * freq_y)
        lapl = jnp.concatenate([wave] * (NZ // LANES), axis=1) + eig_val[...].reshape(1, NZ)
        diag_buoy = 1.0 + diffuse_buoy * lapl
        diag_vel = 1.0 + diffuse_vel * lapl
        inverse = 1.0 / (diag_buoy * diag_vel + couple_buoy * couple_vel)
        solved_buoy = ((diag_vel * modal_buoy - couple_buoy * modal_vel) * inverse).astype(BF)
        solved_vel = ((diag_buoy * modal_vel + couple_vel * modal_buoy) * inverse).astype(BF)
        out_buoy[rows, :] = mm(solved_buoy, eig_right[...]).astype(BF)
        out_vel[rows, :] = mm(solved_vel, eig_right[...]).astype(BF)

    @pl.loop(0, G)
    def _(g):
        others(part, COLS, lambda q: col_fwd(g, q).wait_send())
        others(col, COLS, lambda s: col_back(g, s).wait_send())

    def nothing():
        pass

    @pl.loop(0, last)
    def _(m):
        members(nothing, lambda t: row_fwd(2 * m, t).wait_send())

    @pl.loop(0, last + 1 - core)
    def _(m):
        members(nothing, lambda t: row_back(m, 2 * m, t).wait_send())

    chips(0, nothing, lambda t: row_fwd(G - 1, t).wait_send())


def per_device(buoy, vel_w, strat, eig_val, eig_left, eig_right):
    modes = A * K
    dma = pltpu.SemaphoreType.DMA
    vmem = pl.BlockSpec(memory_space=pltpu.VMEM)
    hbm = pl.BlockSpec(memory_space=pl.ANY)
    shape = jax.ShapeDtypeStruct((modes, NZ), BF)
    consts = [jnp.asarray(t) for t in tables()]
    new_buoy, new_vel = pl.pallas_call(
        kernel,
        out_shape=(shape, shape),
        in_specs=[vmem] * 4 + [hbm] * 3 + [vmem] * 2 + [hbm] * 2,
        out_specs=(vmem, vmem),
        scratch_shapes=[
            pltpu.VMEM((G, COLS, ZC, 2, PAIRS, LANES), BF),
            pltpu.VMEM((G, ZC, COLS, 2, PAIRS, LANES), BF),
            pltpu.VMEM((G // 2 + 1, ROWS, COLS, 2, PAIRS, LANES), BF),
            pltpu.VMEM((G, ZC, COLS, 2, PAIRS, LANES), BF),
            pltpu.VMEM((G, COLS, ZC, 2, PAIRS, LANES), BF),
            pltpu.VMEM((TALL, LANES), F32),
            pltpu.VMEM((2, COLS * LANES, YG), BF),
            pltpu.VMEM((2 * YG, COLS * LANES), BF),
            pltpu.VMEM((XG, KX), BF),
            pltpu.VMEM((KX, XG), BF),
            pltpu.VMEM((KX, 2 * YG), BF),
            pltpu.VMEM((XG, 2 * YG), BF),
            pltpu.VMEM((2, modes, NZ), F32),
            pltpu.VMEM((ZPART,), F32),
            pltpu.VMEM((ZG, NZ), BF),
            pltpu.VMEM((KY, YG), BF),
            pltpu.VMEM((YG, KY), BF),
            pltpu.VMEM((NZ, NZ), BF),
            pltpu.VMEM((NZ, NZ), BF),
            dma((5,)),
            dma((G, COLS)), dma((G, COLS)), dma((G // 2 + 1, ROWS)), dma((G // 2 + 1, ROWS)),
            dma((G // 2 + 1, ROWS)), dma((G, ZC)), dma((G, COLS)), dma((G, COLS)),
            dma, dma,
        ],
        compiler_params=pltpu.CompilerParams(
            collective_id=0, has_side_effects=True, vmem_limit_bytes=VMEM_LIMIT
        ),
        name="section",
    )(
        vel_w.reshape(modes, NZ), buoy.reshape(modes, NZ), *consts, strat, eig_val, eig_left, eig_right
    )
    return new_buoy.reshape(buoy.shape), new_vel.reshape(buoy.shape)


def solution(mesh):
    in_specs = (P("row", "col", None), P("row", "col", None), P("col"), P(), P(), P())
    out_specs = (P("row", "col", None), P("row", "col", None))
    return jax.shard_map(
        per_device, mesh=mesh, in_specs=in_specs, out_specs=out_specs, check_vma=False
    )
```

```python
import functools
import math

import jax
import jax.numpy as jnp
import numpy as np
from jax import lax
from jax.experimental import pallas as pl
from jax.experimental.pallas import tpu as pltpu
from jax.sharding import PartitionSpec as P

KX = 512
KY = 512
NZ = 384
XG = 768
YG = 768
ZG = 576

explicit_step = 0.5
diffuse_buoy = 0.5
diffuse_vel = 0.25
couple_buoy = 0.7
couple_vel = 0.7

ROWS = 16
COLS = 8
A = KX // ROWS
K = KY // COLS
PAIRS = A // 2
LANES = 2 * K
G = 9
PASSES = 3
ZPART = ZG // COLS
ZC = ZPART // G
SIZE = ZC * PAIRS
TWO = 2 * LANES
TALL = 4 * COLS * SIZE
ORDER = (0, 6, 7, 1, 2, 3, 4, 5, 8)
TURN = 3
ENDS = (4, 8, 9)
BF = jnp.bfloat16
F32 = jnp.float32
MESH = pl.DeviceIdType.MESH
VMEM_LIMIT = 67_000_000


def trig(modes, points):
    order = np.arange(modes)
    freq = ((order + 1) // 2).astype(np.float32)
    step = np.float32(2.0 * math.pi / points)
    angle = (step * freq)[:, None] * np.arange(points, dtype=np.float32)[None, :]
    angle = angle.astype(np.float64)
    values = np.where((order % 2 == 0)[:, None], np.cos(angle), np.sin(angle))
    return order, values.astype(np.float32)


def fourier_eval(modes, points):
    _, values = trig(modes, points)
    return (values * np.float32(math.sqrt(2.0 / modes))).astype(BF)


def fourier_proj(modes, points):
    order, values = trig(modes, points)
    weight = np.where(order == 0, 1.0 / points, 2.0 / points).astype(np.float32)
    return (values * weight[:, None] * np.float32(math.sqrt(modes / 2.0))).T.astype(BF)


def cheb_tables(degree, points):
    order = np.arange(degree, dtype=np.float32)
    theta = np.float32(math.pi) * (np.arange(points, dtype=np.float32) + np.float32(0.5))
    theta = theta / np.float32(points)
    angle = (order[:, None] * theta[None, :]).astype(np.float64)
    cos, sin = np.cos(angle).astype(np.float32), np.sin(angle).astype(np.float32)
    norm = np.float32(math.sqrt(2.0 / degree))
    weight = np.where(order == 0, 1.0 / points, 2.0 / points).astype(np.float32)
    levels = cos * norm
    slopes = -(order[:, None] / np.float32(degree)) * sin * norm
    projector = (cos * weight[:, None] * np.float32(math.sqrt(degree / 2.0))).T
    return levels.astype(BF), slopes.astype(BF), projector.astype(BF)


def tables():
    levels, slopes, projector = cheb_tables(NZ, ZG)

    def by_chunk(rows):
        return np.asarray(rows).reshape(COLS, ZC, G, NZ).transpose(2, 0, 1, 3).reshape(ZG, NZ)

    lift, slope = (
        by_chunk(np.asarray(t).T).reshape(G, -1, NZ)[list(ORDER)].reshape(PASSES, -1, NZ) for t in (levels, slopes)
    )
    return lift, slope, by_chunk(projector), fourier_eval(KY, YG), np.ascontiguousarray(fourier_proj(KY, YG))


def mm(left, right, dims=((1,), (0,))):
    return lax.dot_general(left, right, (dims, ((), ())), preferred_element_type=F32)


def kernel(
    vel, buoy, lift, slope, drop_in, evals_in, projs_in, strat, eig_val, left_in, right_in,
    out_buoy, out_vel,
    lifted, arrived, planes, passed, folded, tall, wide_eval, wide_proj, eval_x, proj_x, middle, flux, partial,
    strat_in, drop, evals, projs, eig_left, eig_right, load_s,
    turn_s, turn_r, hop_s, hop_r, colf_s, colf_r, rowf_s, rowf_r, rowb_s, rowb_r, colb_s, colb_r, strat_s, strat_r,
):
    row, col = lax.axis_index("row"), lax.axis_index("col")
    high = row // (ROWS // 2)
    base, low = (col // 2) * 2, col % 2
    part = base + (low + high) % 2

    def col_of(q):
        return (row, (q // 2) * 2 + (q % 2 + high) % 2)

    def row_of(t):
        return (t, base + (low + high + t // (ROWS // 2)) % 2)

    barrier = pltpu.get_barrier_semaphore()

    @pl.loop(1, COLS)
    def _(i):
        pl.semaphore_signal(barrier, inc=1, device_id=col_of((part + i) % COLS), device_id_type=MESH)

    @pl.loop(1, ROWS)
    def _(i):
        pl.semaphore_signal(barrier, inc=1, device_id=row_of((row + i) % ROWS), device_id_type=MESH)

    loads = [
        pltpu.make_async_copy(src, dst, load_s.at[n])
        for n, (src, dst) in enumerate(
            ((evals_in, evals), (projs_in, projs), (drop_in, drop), (left_in, eig_left), (right_in, eig_right))
        )
    ]
    for load in loads:
        load.start()

    def remote(src, dst, send, recv, device):
        return pltpu.make_async_remote_copy(
            src_ref=src, dst_ref=dst, send_sem=send, recv_sem=recv, device_id=device, device_id_type=MESH
        )

    chip, core = row // 2, row % 2

    def col_fwd(g, q):
        return remote(lifted.at[g, q], arrived.at[g, :, col], colf_s.at[g, q], colf_r.at[g, col], col_of(q))

    def col_fwd_in(g, s):
        block = arrived.at[g, :, s]
        return remote(block, block, colf_s.at[g, s], colf_r.at[g, s], col_of(0))

    def col_fwd_own(g):
        return pltpu.make_async_copy(lifted.at[g, part], arrived.at[g, :, col], colf_r.at[g, col])

    def col_back(g, s):
        return remote(passed.at[g, :, s], folded.at[g, part], colb_s.at[g, s], colb_r.at[g, part], (row, s))

    def col_back_in(g, q):
        block = folded.at[g, q]
        return remote(block, block, colb_s.at[g, q], colb_r.at[g, q], col_of(q))

    def col_back_own(g):
        return pltpu.make_async_copy(passed.at[g, :, col], folded.at[g, part], colb_r.at[g, part])

    def others(first, count, do):
        @pl.loop(1, count)
        def _(i):
            do((first + i) % count)

    def row_fwd(g, t):
        m = g // 2
        return remote(arrived.at[g, t // 2], planes.at[m, row], rowf_s.at[m, t], rowf_r.at[m, row], row_of(t))

    def row_fwd_in(m, t):
        block = planes.at[m, t]
        return remote(block, block, rowf_s.at[m, t], rowf_r.at[m, t], row_of(t))

    def row_fwd_own(g):
        m = g // 2
        return pltpu.make_async_copy(arrived.at[g, chip], planes.at[m, row], rowf_r.at[m, row])

    def row_back(m, g, t):
        return remote(planes.at[m, t], passed.at[g, chip], rowb_s.at[m, t], rowb_r.at[g, chip], row_of(t))

    def row_back_in(g, t):
        block = passed.at[g, t // 2]
        return remote(block, block, rowb_s.at[0, t], rowb_r.at[g, t // 2], row_of(t))

    def row_back_own(m, g):
        return pltpu.make_async_copy(planes.at[m, row], passed.at[g, chip], rowb_r.at[g, chip])

    def chips(side, here, there):
        @pl.loop(0, ZC)
        def _(i):
            t = ((chip + i) % ZC) * 2 + side
            pl.when(t == row)(lambda: here())
            pl.when(t != row)(lambda: there(t))

    def members(here, there):
        chips(core, here, there)
        chips(1 - core, here, there)

    def turn_out(g, t):
        return remote(
            lifted.at[g, t // 2], arrived.at[2 * TURN + high, row % 8], turn_s.at[g % 2, t // 2], turn_r.at[row], row_of(t)
        )

    def turn_own(g):
        return pltpu.make_async_copy(lifted.at[g, chip], arrived.at[2 * TURN + high, row % 8], turn_r.at[row])

    def turn_in(t):
        block = arrived.at[2 * TURN + t // 8, t % 8]
        return remote(block, block, turn_s.at[0, 0], turn_r.at[t], row_of(t))

    def landing(h, s):
        return planes.at[TURN, h * 8 : (h + 1) * 8, (s // 2) * 2 + (s % 2 + high + h) % 2]

    def hop(h, q):
        return remote(arrived.at[2 * TURN + h, :, q], landing(h, col), hop_s.at[h, q], hop_r.at[h, col], col_of(q))

    def hop_in(h, s):
        return remote(landing(h, s), landing(h, s), hop_s.at[h, s], hop_r.at[h, s], col_of(0))

    def hop_own(h):
        return pltpu.make_async_copy(arrived.at[2 * TURN + h, :, part], landing(h, col), hop_r.at[h, col])

    def relay_turned():
        members(lambda: turn_own(2 * TURN).wait(), lambda t: turn_in(t).wait_recv())
        for h in range(2):
            others(part, COLS, lambda q: hop(h, q).start())
            hop_own(h).start()

    def relay_fwd(g):
        others(col, COLS, lambda s: col_fwd_in(g, s).wait_recv())
        col_fwd_own(g).wait()

        chips(g % 2, lambda: row_fwd_own(g).start(), lambda t: row_fwd(g, t).start())

    def relay_back(g):
        chips(g % 2, lambda: row_back_own(0, g).wait(), lambda t: row_back_in(g, t).wait_recv())
        others(col, COLS, lambda s: col_back(g, s).start())
        col_back_own(g).start()

    count = ZG // PASSES
    chunks = G // PASSES

    def chunk_at(i):
        return jnp.where(i == 0, 0, jnp.where(i < 3, i + 5, jnp.where(i < 8, i - 2, 8)))

    def to_points(u):
        for f, (table, field) in enumerate(((lift, vel), (slope, buoy))):

            @pl.loop(0, PAIRS // 2)
            def _(p):
                rows = pl.ds(pl.multiple_of(p * TWO, TWO), TWO)
                values = mm(table[u], field[rows, :], ((1,), (1,)))
                tall[pl.ds(2 * p, count, stride=PAIRS), :] = values[:, :LANES]
                tall[pl.ds(2 * p + 1, count, stride=PAIRS), :] = values[:, LANES:]

            @pl.loop(0, COLS * chunks)
            def _(i):
                rows = pl.ds(pl.multiple_of(i * SIZE, SIZE), SIZE)
                block = tall[rows, :].astype(BF).reshape(ZC, PAIRS, LANES)
                g, q = chunk_at(u * chunks + i // COLS), i % COLS

                @pl.when(g // 2 != TURN)
                def _():
                    lifted[g, q, :, f] = block

                @pl.when(g // 2 == TURN)
                def _():
                    lifted[g, :, q, f] = block

    def send_points(u):
        @pl.loop(u * chunks, (u + 1) * chunks)
        def _(i):
            g = chunk_at(i)

            @pl.when(g // 2 != TURN)
            def _():
                others(part, COLS, lambda q: col_fwd(g, q).start())
                col_fwd_own(g).start()

            @pl.when(g // 2 == TURN)
            def _():
                chips(g % 2, lambda: turn_own(g).start(), lambda t: turn_out(g, t).start())

    to_points(0)
    pl.semaphore_wait(barrier, COLS + ROWS - 2)
    send_points(0)
    swap = remote(strat, strat_in, strat_s, strat_r, (row, base + 1 - low))
    swap.start()

    @pl.loop(1, PASSES)
    def _(u):
        to_points(u)
        send_points(u)

    for load in loads:
        load.wait()

    @pl.loop(0, COLS)
    def _(s):
        for a in range(2):
            own = pl.ds(pl.multiple_of(s * LANES + a * K, K), K)
            other = pl.ds(pl.multiple_of(s * LANES + (1 - a) * K, K), K)
            wide_eval[a, own, :] = evals[pl.ds(pl.multiple_of(s * K, K), K), :]
            wide_eval[a, other, :] = jnp.zeros((K, YG), BF)

    relay_fwd(0)

    lane = lax.broadcasted_iota(jnp.int32, (LANES, LANES), 1)

    @pl.loop(0, YG // LANES)
    def _(i):
        for j in range(COLS // 2):
            rows = pl.ds(pl.multiple_of(i * LANES, LANES), LANES)
            tile = projs[rows, j * LANES : (j + 1) * LANES].astype(F32)
            turned = pltpu.roll(tile, K, 1)
            for s in (2 * j, 2 * j + 1):
                straight, moved = (tile, turned) if s % 2 == 0 else (turned, tile)
                for a in range(2):
                    keep = jnp.where((lane < K) == (a == 0), straight if a == 0 else moved, 0.0).astype(BF)
                    to = pl.ds(pl.multiple_of(a * YG + i * LANES, LANES), LANES)
                    wide_proj[to, s * LANES : (s + 1) * LANES] = keep

    relay_fwd(1)

    @pl.loop(0, XG // LANES)
    def _(j):
        points = pl.ds(pl.multiple_of(j * LANES, LANES), LANES)

        def ordered(values):
            tall[:KX, :] = values
            return jnp.concatenate([tall[pl.ds(a, KX // 2, stride=2), :] for a in range(2)], axis=0)

        eval_x[points, :] = ordered(evals[:, points].astype(F32)).T.astype(BF)
        proj_x[:, points] = ordered(projs[points, :].astype(F32).T).astype(BF)

    pl.loop(2, 5)(relay_fwd)
    relay_turned()
    swap.wait()
    strata = jnp.where(high == 0, strat[...], strat_in[...]).reshape(1, ZPART)
    level_of = lax.broadcasted_iota(jnp.int32, (1, ZPART), 1)

    half = KX // 2
    last = G // 2

    @pl.loop(0, last + 1 - core)
    def _(m):
        chunk = 2 * m + core

        @pl.when(m != TURN)
        def _():
            members(lambda: row_fwd_own(2 * m).wait(), lambda t: row_fwd_in(m, t).wait_recv())

        @pl.when(m == TURN)
        def _():
            for h in range(2):
                others(col, COLS, lambda s: hop_in(h, s).wait_recv())
                hop_own(h).wait()

        for f in range(2):
            left = jnp.concatenate([planes[m, :, s, f].reshape(half, LANES) for s in range(COLS)], axis=1)
            for a in range(2):
                middle[a * half : (a + 1) * half, f * YG : (f + 1) * YG] = mm(left, wide_eval[a]).astype(BF)

        pl.when(m < 2)(lambda: relay_fwd(5 + 3 * m))

        level = jnp.sum(jnp.where(level_of == chip * G + chunk, strata, 0.0), axis=1, keepdims=True)
        tile = XG // 3

        @pl.loop(0, 3)
        def _(x):
            rows = pl.ds(pl.multiple_of(x * tile, tile), tile)
            velocity = mm(eval_x[rows, :], middle[:, :YG]).astype(BF).astype(F32)
            gradient = mm(eval_x[rows, :], middle[:, YG:]).astype(BF).astype(F32)
            flux[rows, :YG] = (-(velocity * gradient) - level * velocity).astype(BF)
            flux[rows, YG:] = (-(velocity * jnp.abs(velocity))).astype(BF)


        @pl.loop(0, 2)
        def _(a):
            rows = pl.ds(pl.multiple_of(a * half, half), half)
            for f in range(2):
                middle[rows, f * YG : (f + 1) * YG] = mm(proj_x[rows, :], flux[:, f * YG : (f + 1) * YG]).astype(BF)
        for f in range(2):
            left = jnp.concatenate(
                [middle[a * half : (a + 1) * half, f * YG : (f + 1) * YG] for a in range(2)], axis=1
            )
            values = mm(left, wide_proj[...]).astype(BF)
            for s in range(COLS):
                planes[m, :, s, f] = values[:, s * LANES : (s + 1) * LANES].reshape(ROWS, PAIRS, LANES)

        members(lambda: row_back_own(m, chunk).start(), lambda t: row_back(m, chunk, t).start())

        @pl.when(m == last - 1)
        def _():
            pl.loop(0, 2)(relay_back)

    def gather(first, last, f, start):
        @pl.loop(first, last)
        def _(g):
            for q in range(COLS):
                place = pl.multiple_of(start + ((g - first) * COLS + q) * SIZE, SIZE)
                tall[pl.ds(place, SIZE), :] = folded[g, q, :, f].reshape(SIZE, LANES).astype(F32)

    def tendency(first, last, p, start):
        count = (last - first) * COLS * ZC
        columns = [tall[pl.ds(start + 2 * p + a, count, stride=PAIRS), :].astype(BF) for a in range(2)]
        rows = slice(first * COLS * ZC, last * COLS * ZC)
        return mm(jnp.concatenate(columns, axis=1), drop[rows, :], ((0,), (0,)))

    def wait_modes(first, last):
        @pl.loop(first, last)
        def _(g):
            others(part, COLS, lambda q: col_back_in(g, q).wait_recv())
            col_back_own(g).wait()

    pl.loop(2, ENDS[0] + 2)(relay_back)
    wait_modes(0, ENDS[0])
    for f in range(2):
        gather(0, ENDS[0], f, 0)

        @pl.loop(0, PAIRS // 2)
        def _(p):
            rows = pl.ds(pl.multiple_of(p * TWO, TWO), TWO)
            partial[f, rows, :] = tendency(0, ENDS[0], p, 0)

    pl.loop(ENDS[0] + 2, G)(relay_back)
    wait_modes(ENDS[0], ENDS[1])
    for f in range(2):
        gather(ENDS[0], ENDS[1], f, 0)

        @pl.loop(0, PAIRS // 2)
        def _(p):
            rows = pl.ds(pl.multiple_of(p * TWO, TWO), TWO)
            partial[f, rows, :] += tendency(ENDS[0], ENDS[1], p, 0)

    wait_modes(ENDS[1], G)
    start = (G - ENDS[1]) * COLS * SIZE
    for f in range(2):
        gather(ENDS[1], G, f, f * start)

    @pl.loop(0, PAIRS // 2)
    def _(p):
        rows = pl.ds(pl.multiple_of(p * TWO, TWO), TWO)
        modal = []
        for f, field in enumerate((buoy, vel)):
            tend = partial[f, rows, :] + tendency(ENDS[1], G, p, f * start)
            rhs = (field[rows, :].astype(F32) + explicit_step * tend).astype(BF)
            modal.append(mm(rhs, eig_left[...]))
        modal_buoy, modal_vel = modal
        place = p * TWO + lax.broadcasted_iota(jnp.int32, (TWO, LANES), 0)
        freq_x = ((row * A + (place >> 6) + 1) >> 1).astype(F32) * (2.0 / KX)
        freq_y = ((col * K + (place & (K - 1)) + 1) >> 1).astype(F32) * (2.0 / KY)
        wave = 4.0 * (freq_x * freq_x + freq_y * freq_y)
        lapl = jnp.concatenate([wave] * (NZ // LANES), axis=1) + eig_val[...].reshape(1, NZ)
        diag_buoy = 1.0 + diffuse_buoy * lapl
        diag_vel = 1.0 + diffuse_vel * lapl
        inverse = 1.0 / (diag_buoy * diag_vel + couple_buoy * couple_vel)
        solved_buoy = ((diag_vel * modal_buoy - couple_buoy * modal_vel) * inverse).astype(BF)
        solved_vel = ((diag_buoy * modal_vel + couple_vel * modal_buoy) * inverse).astype(BF)
        out_buoy[rows, :] = mm(solved_buoy, eig_right[...]).astype(BF)
        out_vel[rows, :] = mm(solved_vel, eig_right[...]).astype(BF)

    def nothing():
        pass

    for h in range(2):
        others(part, COLS, lambda q: hop(h, q).wait_send())

    @pl.loop(0, G)
    def _(g):
        @pl.when(g // 2 != TURN)
        def _():
            others(part, COLS, lambda q: col_fwd(g, q).wait_send())

        @pl.when(g // 2 == TURN)
        def _():
            chips(g % 2, nothing, lambda t: turn_out(g, t).wait_send())

        others(col, COLS, lambda s: col_back(g, s).wait_send())

    @pl.loop(0, last)
    def _(m):
        pl.when(m != TURN)(lambda: members(nothing, lambda t: row_fwd(2 * m, t).wait_send()))

    @pl.loop(0, last + 1 - core)
    def _(m):
        members(nothing, lambda t: row_back(m, 2 * m, t).wait_send())

    chips(0, nothing, lambda t: row_fwd(G - 1, t).wait_send())


def per_device(buoy, vel_w, strat, eig_val, eig_left, eig_right):
    modes = A * K
    dma = pltpu.SemaphoreType.DMA
    vmem = pl.BlockSpec(memory_space=pltpu.VMEM)
    hbm = pl.BlockSpec(memory_space=pl.ANY)
    shape = jax.ShapeDtypeStruct((modes, NZ), BF)
    consts = [jnp.asarray(t) for t in tables()]
    new_buoy, new_vel = pl.pallas_call(
        kernel,
        out_shape=(shape, shape),
        in_specs=[vmem] * 4 + [hbm] * 3 + [vmem] * 2 + [hbm] * 2,
        out_specs=(vmem, vmem),
        scratch_shapes=[
            pltpu.VMEM((G, COLS, ZC, 2, PAIRS, LANES), BF),
            pltpu.VMEM((G, ZC, COLS, 2, PAIRS, LANES), BF),
            pltpu.VMEM((G // 2 + 1, ROWS, COLS, 2, PAIRS, LANES), BF),
            pltpu.VMEM((G, ZC, COLS, 2, PAIRS, LANES), BF),
            pltpu.VMEM((G, COLS, ZC, 2, PAIRS, LANES), BF),
            pltpu.VMEM((TALL, LANES), F32),
            pltpu.VMEM((2, COLS * LANES, YG), BF),
            pltpu.VMEM((2 * YG, COLS * LANES), BF),
            pltpu.VMEM((XG, KX), BF),
            pltpu.VMEM((KX, XG), BF),
            pltpu.VMEM((KX, 2 * YG), BF),
            pltpu.VMEM((XG, 2 * YG), BF),
            pltpu.VMEM((2, modes, NZ), F32),
            pltpu.VMEM((ZPART,), F32),
            pltpu.VMEM((ZG, NZ), BF),
            pltpu.VMEM((KY, YG), BF),
            pltpu.VMEM((YG, KY), BF),
            pltpu.VMEM((NZ, NZ), BF),
            pltpu.VMEM((NZ, NZ), BF),
            dma((5,)), dma((2, ZC)), dma((ROWS,)), dma((2, COLS)), dma((2, COLS)),
            dma((G, COLS)), dma((G, COLS)), dma((G // 2 + 1, ROWS)), dma((G // 2 + 1, ROWS)),
            dma((G // 2 + 1, ROWS)), dma((G, ZC)), dma((G, COLS)), dma((G, COLS)),
            dma, dma,
        ],
        compiler_params=pltpu.CompilerParams(
            collective_id=0, has_side_effects=True, vmem_limit_bytes=VMEM_LIMIT
        ),
        name="section",
    )(
        vel_w.reshape(modes, NZ), buoy.reshape(modes, NZ), *consts, strat, eig_val, eig_left, eig_right
    )
    return new_buoy.reshape(buoy.shape), new_vel.reshape(buoy.shape)


def solution(mesh):
    in_specs = (P("row", "col", None), P("row", "col", None), P("col"), P(), P(), P())
    out_specs = (P("row", "col", None), P("row", "col", None))
    return jax.shard_map(
        per_device, mesh=mesh, in_specs=in_specs, out_specs=out_specs, check_vma=False
    )
```

```python
import functools
import math

import jax
import jax.numpy as jnp
import numpy as np
from jax import lax
from jax.experimental import pallas as pl
from jax.experimental.pallas import tpu as pltpu
from jax.sharding import PartitionSpec as P

KX = 512
KY = 512
NZ = 384
XG = 768
YG = 768
ZG = 576

explicit_step = 0.5
diffuse_buoy = 0.5
diffuse_vel = 0.25
couple_buoy = 0.7
couple_vel = 0.7

ROWS = 16
COLS = 8
A = KX // ROWS
K = KY // COLS
PAIRS = A // 2
LANES = 2 * K
G = 9
PASSES = 3
ZPART = ZG // COLS
ZC = ZPART // G
SIZE = ZC * PAIRS
TWO = 2 * LANES
TALL = 4 * COLS * SIZE
ORDER = (0, 6, 7, 1, 2, 3, 4, 5, 8)
TURN = 3
ENDS = (4, 8, 9)
BF = jnp.bfloat16
F32 = jnp.float32
MESH = pl.DeviceIdType.MESH
VMEM_LIMIT = 67_000_000


def trig(modes, points):
    order = np.arange(modes)
    freq = ((order + 1) // 2).astype(np.float32)
    step = np.float32(2.0 * math.pi / points)
    angle = (step * freq)[:, None] * np.arange(points, dtype=np.float32)[None, :]
    angle = angle.astype(np.float64)
    values = np.where((order % 2 == 0)[:, None], np.cos(angle), np.sin(angle))
    return order, values.astype(np.float32)


def fourier_eval(modes, points):
    _, values = trig(modes, points)
    return (values * np.float32(math.sqrt(2.0 / modes))).astype(BF)


def fourier_proj(modes, points):
    order, values = trig(modes, points)
    weight = np.where(order == 0, 1.0 / points, 2.0 / points).astype(np.float32)
    return (values * weight[:, None] * np.float32(math.sqrt(modes / 2.0))).T.astype(BF)


def cheb_tables(degree, points):
    order = np.arange(degree, dtype=np.float32)
    theta = np.float32(math.pi) * (np.arange(points, dtype=np.float32) + np.float32(0.5))
    theta = theta / np.float32(points)
    angle = (order[:, None] * theta[None, :]).astype(np.float64)
    cos, sin = np.cos(angle).astype(np.float32), np.sin(angle).astype(np.float32)
    norm = np.float32(math.sqrt(2.0 / degree))
    weight = np.where(order == 0, 1.0 / points, 2.0 / points).astype(np.float32)
    levels = cos * norm
    slopes = -(order[:, None] / np.float32(degree)) * sin * norm
    projector = (cos * weight[:, None] * np.float32(math.sqrt(degree / 2.0))).T
    return levels.astype(BF), slopes.astype(BF), projector.astype(BF)


def tables():
    levels, slopes, projector = cheb_tables(NZ, ZG)

    def by_chunk(rows):
        return np.asarray(rows).reshape(COLS, ZC, G, NZ).transpose(2, 0, 1, 3).reshape(ZG, NZ)

    lift, slope = (
        by_chunk(np.asarray(t).T).reshape(G, -1, NZ)[list(ORDER)].reshape(PASSES, -1, NZ) for t in (levels, slopes)
    )
    return lift, slope, by_chunk(projector), fourier_eval(KY, YG), np.ascontiguousarray(fourier_proj(KY, YG))


def mm(left, right, dims=((1,), (0,))):
    return lax.dot_general(left, right, (dims, ((), ())), preferred_element_type=F32)


def kernel(
    vel, buoy, lift, slope, drop_in, evals_in, projs_in, strat, eig_val, left_in, right_in,
    out_buoy, out_vel,
    lifted, arrived, planes, passed, folded, tall, wide_eval, wide_proj, eval_x, proj_x, middle, flux, partial,
    inverses, done, done_s, strat_in, drop, evals, projs, eig_left, eig_right, load_s,
    turn_s, turn_r, hop_s, hop_r, colf_s, colf_r, rowf_s, rowf_r, rowb_s, rowb_r, colb_s, colb_r, strat_s, strat_r,
):
    row, col = lax.axis_index("row"), lax.axis_index("col")
    high = row // (ROWS // 2)
    base, low = (col // 2) * 2, col % 2
    part = base + (low + high) % 2

    def col_of(q):
        return (row, (q // 2) * 2 + (q % 2 + high) % 2)

    def row_of(t):
        return (t, base + (low + high + t // (ROWS // 2)) % 2)

    barrier = pltpu.get_barrier_semaphore()

    @pl.loop(1, COLS)
    def _(i):
        pl.semaphore_signal(barrier, inc=1, device_id=col_of((part + i) % COLS), device_id_type=MESH)

    @pl.loop(1, ROWS)
    def _(i):
        pl.semaphore_signal(barrier, inc=1, device_id=row_of((row + i) % ROWS), device_id_type=MESH)

    loads = [
        pltpu.make_async_copy(src, dst, load_s.at[n])
        for n, (src, dst) in enumerate(
            ((evals_in, evals), (projs_in, projs), (drop_in, drop), (left_in, eig_left), (right_in, eig_right))
        )
    ]
    for load in loads:
        load.start()

    def remote(src, dst, send, recv, device):
        return pltpu.make_async_remote_copy(
            src_ref=src, dst_ref=dst, send_sem=send, recv_sem=recv, device_id=device, device_id_type=MESH
        )

    chip, core = row // 2, row % 2

    def col_fwd(g, q):
        return remote(lifted.at[g, q], arrived.at[g, :, col], colf_s.at[g, q], colf_r.at[g, col], col_of(q))

    def col_fwd_in(g, s):
        block = arrived.at[g, :, s]
        return remote(block, block, colf_s.at[g, s], colf_r.at[g, s], col_of(0))

    def col_fwd_own(g):
        return pltpu.make_async_copy(lifted.at[g, part], arrived.at[g, :, col], colf_r.at[g, col])

    def col_back(g, s):
        return remote(passed.at[g, :, s], folded.at[g, part], colb_s.at[g, s], colb_r.at[g, part], (row, s))

    def col_back_in(g, q):
        block = folded.at[g, q]
        return remote(block, block, colb_s.at[g, q], colb_r.at[g, q], col_of(q))

    def col_back_own(g):
        return pltpu.make_async_copy(passed.at[g, :, col], folded.at[g, part], colb_r.at[g, part])

    def others(first, count, do):
        @pl.loop(1, count)
        def _(i):
            do((first + i) % count)

    def row_fwd(g, t):
        m = g // 2
        return remote(arrived.at[g, t // 2], planes.at[m, row], rowf_s.at[m, t], rowf_r.at[m, row], row_of(t))

    def row_fwd_in(m, t):
        block = planes.at[m, t]
        return remote(block, block, rowf_s.at[m, t], rowf_r.at[m, t], row_of(t))

    def row_fwd_own(g):
        m = g // 2
        return pltpu.make_async_copy(arrived.at[g, chip], planes.at[m, row], rowf_r.at[m, row])

    def row_back(m, g, t):
        return remote(planes.at[m, t], passed.at[g, chip], rowb_s.at[m, t], rowb_r.at[g, chip], row_of(t))

    def row_back_in(g, t):
        block = passed.at[g, t // 2]
        return remote(block, block, rowb_s.at[0, t], rowb_r.at[g, t // 2], row_of(t))

    def row_back_own(m, g):
        return pltpu.make_async_copy(planes.at[m, row], passed.at[g, chip], rowb_r.at[g, chip])

    def chips(side, here, there):
        @pl.loop(0, ZC)
        def _(i):
            t = ((chip + i) % ZC) * 2 + side
            pl.when(t == row)(lambda: here())
            pl.when(t != row)(lambda: there(t))

    def members(here, there):
        chips(core, here, there)
        chips(1 - core, here, there)

    def turn_out(g, t):
        return remote(
            lifted.at[g, t // 2], arrived.at[2 * TURN + high, row % 8], turn_s.at[g % 2, t // 2], turn_r.at[row], row_of(t)
        )

    def turn_own(g):
        return pltpu.make_async_copy(lifted.at[g, chip], arrived.at[2 * TURN + high, row % 8], turn_r.at[row])

    def turn_in(t):
        block = arrived.at[2 * TURN + t // 8, t % 8]
        return remote(block, block, turn_s.at[0, 0], turn_r.at[t], row_of(t))

    def landing(h, s):
        return planes.at[TURN, h * 8 : (h + 1) * 8, (s // 2) * 2 + (s % 2 + high + h) % 2]

    def hop(h, q):
        return remote(arrived.at[2 * TURN + h, :, q], landing(h, col), hop_s.at[h, q], hop_r.at[h, col], col_of(q))

    def hop_in(h, s):
        return remote(landing(h, s), landing(h, s), hop_s.at[h, s], hop_r.at[h, s], col_of(0))

    def hop_own(h):
        return pltpu.make_async_copy(arrived.at[2 * TURN + h, :, part], landing(h, col), hop_r.at[h, col])

    def relay_turned():
        members(lambda: turn_own(2 * TURN).wait(), lambda t: turn_in(t).wait_recv())
        for h in range(2):
            others(part, COLS, lambda q: hop(h, q).start())
            hop_own(h).start()

    def relay_fwd(g):
        others(col, COLS, lambda s: col_fwd_in(g, s).wait_recv())
        col_fwd_own(g).wait()

        chips(g % 2, lambda: row_fwd_own(g).start(), lambda t: row_fwd(g, t).start())

    def relay_back(g):
        chips(g % 2, lambda: row_back_own(0, g).wait(), lambda t: row_back_in(g, t).wait_recv())
        others(col, COLS, lambda s: col_back(g, s).start())
        col_back_own(g).start()

    count = ZG // PASSES
    chunks = G // PASSES

    def chunk_at(i):
        return jnp.where(i == 0, 0, jnp.where(i < 3, i + 5, jnp.where(i < 8, i - 2, 8)))

    def to_points(u):
        for f, (table, field) in enumerate(((lift, vel), (slope, buoy))):

            @pl.loop(0, PAIRS // 2)
            def _(p):
                rows = pl.ds(pl.multiple_of(p * TWO, TWO), TWO)
                values = mm(table[u], field[rows, :], ((1,), (1,)))
                tall[pl.ds(2 * p, count, stride=PAIRS), :] = values[:, :LANES]
                tall[pl.ds(2 * p + 1, count, stride=PAIRS), :] = values[:, LANES:]

            @pl.loop(0, COLS * chunks)
            def _(i):
                rows = pl.ds(pl.multiple_of(i * SIZE, SIZE), SIZE)
                block = tall[rows, :].astype(BF).reshape(ZC, PAIRS, LANES)
                g, q = chunk_at(u * chunks + i // COLS), i % COLS

                @pl.when(g // 2 != TURN)
                def _():
                    lifted[g, q, :, f] = block

                @pl.when(g // 2 == TURN)
                def _():
                    lifted[g, :, q, f] = block

    def send_points(u):
        @pl.loop(u * chunks, (u + 1) * chunks)
        def _(i):
            g = chunk_at(i)

            @pl.when(g // 2 != TURN)
            def _():
                others(part, COLS, lambda q: col_fwd(g, q).start())
                col_fwd_own(g).start()

            @pl.when(g // 2 == TURN)
            def _():
                chips(g % 2, lambda: turn_own(g).start(), lambda t: turn_out(g, t).start())

    to_points(0)
    pl.semaphore_wait(barrier, COLS + ROWS - 2)
    send_points(0)
    swap = remote(strat, strat_in, strat_s, strat_r, (row, base + 1 - low))
    swap.start()

    @pl.loop(1, PASSES)
    def _(u):
        to_points(u)
        send_points(u)

    for load in loads:
        load.wait()

    @pl.loop(0, COLS)
    def _(s):
        for a in range(2):
            own = pl.ds(pl.multiple_of(s * LANES + a * K, K), K)
            other = pl.ds(pl.multiple_of(s * LANES + (1 - a) * K, K), K)
            wide_eval[a, own, :] = evals[pl.ds(pl.multiple_of(s * K, K), K), :]
            wide_eval[a, other, :] = jnp.zeros((K, YG), BF)

    relay_fwd(0)

    lane = lax.broadcasted_iota(jnp.int32, (LANES, LANES), 1)

    @pl.loop(0, YG // LANES)
    def _(i):
        for j in range(COLS // 2):
            rows = pl.ds(pl.multiple_of(i * LANES, LANES), LANES)
            tile = projs[rows, j * LANES : (j + 1) * LANES].astype(F32)
            turned = pltpu.roll(tile, K, 1)
            for s in (2 * j, 2 * j + 1):
                straight, moved = (tile, turned) if s % 2 == 0 else (turned, tile)
                for a in range(2):
                    keep = jnp.where((lane < K) == (a == 0), straight if a == 0 else moved, 0.0).astype(BF)
                    to = pl.ds(pl.multiple_of(a * YG + i * LANES, LANES), LANES)
                    wide_proj[to, s * LANES : (s + 1) * LANES] = keep

    relay_fwd(1)

    @pl.loop(0, XG // LANES)
    def _(j):
        points = pl.ds(pl.multiple_of(j * LANES, LANES), LANES)

        def ordered(values):
            tall[:KX, :] = values
            return jnp.concatenate([tall[pl.ds(a, KX // 2, stride=2), :] for a in range(2)], axis=0)

        eval_x[points, :] = ordered(evals[:, points].astype(F32)).T.astype(BF)
        proj_x[:, points] = ordered(projs[points, :].astype(F32).T).astype(BF)

    relay_fwd(2)

    def diagonals(p):
        place = p * TWO + lax.broadcasted_iota(jnp.int32, (TWO, LANES), 0)
        freq_x = ((row * A + (place >> 6) + 1) >> 1).astype(F32) * (2.0 / KX)
        freq_y = ((col * K + (place & (K - 1)) + 1) >> 1).astype(F32) * (2.0 / KY)
        wave = 4.0 * (freq_x * freq_x + freq_y * freq_y)
        lapl = jnp.concatenate([wave] * (NZ // LANES), axis=1) + eig_val[...].reshape(1, NZ)
        return 1.0 + diffuse_buoy * lapl, 1.0 + diffuse_vel * lapl

    @pl.loop(0, PAIRS // 2)
    def _(p):
        rows = pl.ds(pl.multiple_of(p * TWO, TWO), TWO)
        diag_buoy, diag_vel = diagonals(p)
        inverses[rows, :] = 1.0 / (diag_buoy * diag_vel + couple_buoy * couple_vel)

    def result(f, p):
        rows = pl.ds(pl.multiple_of(p * TWO, TWO), TWO)
        return pltpu.make_async_copy(done.at[f, rows, :], (out_buoy, out_vel)[f].at[rows, :], done_s.at[f, p])

    pl.loop(3, 5)(relay_fwd)
    relay_turned()
    swap.wait()
    strata = jnp.where(high == 0, strat[...], strat_in[...]).reshape(1, ZPART)
    level_of = lax.broadcasted_iota(jnp.int32, (1, ZPART), 1)

    half = KX // 2
    last = G // 2

    @pl.loop(0, last + 1 - core)
    def _(m):
        chunk = 2 * m + core

        @pl.when(m != TURN)
        def _():
            members(lambda: row_fwd_own(2 * m).wait(), lambda t: row_fwd_in(m, t).wait_recv())

        @pl.when(m == TURN)
        def _():
            for h in range(2):
                others(col, COLS, lambda s: hop_in(h, s).wait_recv())
                hop_own(h).wait()

        for f in range(2):
            left = jnp.concatenate([planes[m, :, s, f].reshape(half, LANES) for s in range(COLS)], axis=1)
            for a in range(2):
                middle[a * half : (a + 1) * half, f * YG : (f + 1) * YG] = mm(left, wide_eval[a]).astype(BF)

        pl.when(m < 2)(lambda: relay_fwd(5 + 3 * m))

        level = jnp.sum(jnp.where(level_of == chip * G + chunk, strata, 0.0), axis=1, keepdims=True)
        tile = XG // 3

        @pl.loop(0, 3)
        def _(x):
            rows = pl.ds(pl.multiple_of(x * tile, tile), tile)
            velocity = mm(eval_x[rows, :], middle[:, :YG]).astype(BF).astype(F32)
            gradient = mm(eval_x[rows, :], middle[:, YG:]).astype(BF).astype(F32)
            flux[rows, :YG] = (-(velocity * gradient) - level * velocity).astype(BF)
            flux[rows, YG:] = (-(velocity * jnp.abs(velocity))).astype(BF)


        @pl.loop(0, 2)
        def _(a):
            rows = pl.ds(pl.multiple_of(a * half, half), half)
            for f in range(2):
                middle[rows, f * YG : (f + 1) * YG] = mm(proj_x[rows, :], flux[:, f * YG : (f + 1) * YG]).astype(BF)
        for f in range(2):
            left = jnp.concatenate(
                [middle[a * half : (a + 1) * half, f * YG : (f + 1) * YG] for a in range(2)], axis=1
            )
            values = mm(left, wide_proj[...]).astype(BF)
            for s in range(COLS):
                planes[m, :, s, f] = values[:, s * LANES : (s + 1) * LANES].reshape(ROWS, PAIRS, LANES)

        members(lambda: row_back_own(m, chunk).start(), lambda t: row_back(m, chunk, t).start())

        @pl.when(m == last - 1)
        def _():
            pl.loop(0, 2)(relay_back)

    def gather(first, last, f, start):
        @pl.loop(first, last)
        def _(g):
            for q in range(COLS):
                place = pl.multiple_of(start + ((g - first) * COLS + q) * SIZE, SIZE)
                tall[pl.ds(place, SIZE), :] = folded[g, q, :, f].reshape(SIZE, LANES).astype(F32)

    def tendency(first, last, p, start):
        count = (last - first) * COLS * ZC
        columns = [tall[pl.ds(start + 2 * p + a, count, stride=PAIRS), :].astype(BF) for a in range(2)]
        rows = slice(first * COLS * ZC, last * COLS * ZC)
        return mm(jnp.concatenate(columns, axis=1), drop[rows, :], ((0,), (0,)))

    def wait_modes(first, last):
        @pl.loop(first, last)
        def _(g):
            others(part, COLS, lambda q: col_back_in(g, q).wait_recv())
            col_back_own(g).wait()

    pl.loop(2, ENDS[0] + 2)(relay_back)
    wait_modes(0, ENDS[0])
    for f in range(2):
        gather(0, ENDS[0], f, 0)

        @pl.loop(0, PAIRS // 2)
        def _(p):
            rows = pl.ds(pl.multiple_of(p * TWO, TWO), TWO)
            partial[f, rows, :] = tendency(0, ENDS[0], p, 0)

    pl.loop(ENDS[0] + 2, G)(relay_back)
    wait_modes(ENDS[0], ENDS[1])
    for f in range(2):
        gather(ENDS[0], ENDS[1], f, 0)

        @pl.loop(0, PAIRS // 2)
        def _(p):
            rows = pl.ds(pl.multiple_of(p * TWO, TWO), TWO)
            partial[f, rows, :] += tendency(ENDS[0], ENDS[1], p, 0)

    wait_modes(ENDS[1], G)
    start = (G - ENDS[1]) * COLS * SIZE
    for f in range(2):
        gather(ENDS[1], G, f, f * start)

    @pl.loop(0, PAIRS // 2)
    def _(p):
        rows = pl.ds(pl.multiple_of(p * TWO, TWO), TWO)
        modal = []
        for f, field in enumerate((buoy, vel)):
            tend = partial[f, rows, :] + tendency(ENDS[1], G, p, f * start)
            rhs = (field[rows, :].astype(F32) + explicit_step * tend).astype(BF)
            modal.append(mm(rhs, eig_left[...]))
        modal_buoy, modal_vel = modal
        diag_buoy, diag_vel = diagonals(p)
        inverse = inverses[rows, :]
        solved_buoy = ((diag_vel * modal_buoy - couple_buoy * modal_vel) * inverse).astype(BF)
        solved_vel = ((diag_buoy * modal_vel + couple_vel * modal_buoy) * inverse).astype(BF)
        done[0, rows, :] = mm(solved_buoy, eig_right[...]).astype(BF)
        done[1, rows, :] = mm(solved_vel, eig_right[...]).astype(BF)
        result(0, p).start()
        result(1, p).start()

    @pl.loop(0, PAIRS // 2)
    def _(p):
        result(0, p).wait()
        result(1, p).wait()

    def nothing():
        pass

    for h in range(2):
        others(part, COLS, lambda q: hop(h, q).wait_send())

    @pl.loop(0, G)
    def _(g):
        @pl.when(g // 2 != TURN)
        def _():
            others(part, COLS, lambda q: col_fwd(g, q).wait_send())

        @pl.when(g // 2 == TURN)
        def _():
            chips(g % 2, nothing, lambda t: turn_out(g, t).wait_send())

        others(col, COLS, lambda s: col_back(g, s).wait_send())

    @pl.loop(0, last)
    def _(m):
        pl.when(m != TURN)(lambda: members(nothing, lambda t: row_fwd(2 * m, t).wait_send()))

    @pl.loop(0, last + 1 - core)
    def _(m):
        members(nothing, lambda t: row_back(m, 2 * m, t).wait_send())

    chips(0, nothing, lambda t: row_fwd(G - 1, t).wait_send())


def per_device(buoy, vel_w, strat, eig_val, eig_left, eig_right):
    modes = A * K
    dma = pltpu.SemaphoreType.DMA
    vmem = pl.BlockSpec(memory_space=pltpu.VMEM)
    hbm = pl.BlockSpec(memory_space=pl.ANY)
    shape = jax.ShapeDtypeStruct((modes, NZ), BF)
    consts = [jnp.asarray(t) for t in tables()]
    new_buoy, new_vel = pl.pallas_call(
        kernel,
        out_shape=(shape, shape),
        in_specs=[vmem] * 4 + [hbm] * 3 + [vmem] * 2 + [hbm] * 2,
        out_specs=(hbm, hbm),
        scratch_shapes=[
            pltpu.VMEM((G, COLS, ZC, 2, PAIRS, LANES), BF),
            pltpu.VMEM((G, ZC, COLS, 2, PAIRS, LANES), BF),
            pltpu.VMEM((G // 2 + 1, ROWS, COLS, 2, PAIRS, LANES), BF),
            pltpu.VMEM((G, ZC, COLS, 2, PAIRS, LANES), BF),
            pltpu.VMEM((G, COLS, ZC, 2, PAIRS, LANES), BF),
            pltpu.VMEM((TALL, LANES), F32),
            pltpu.VMEM((2, COLS * LANES, YG), BF),
            pltpu.VMEM((2 * YG, COLS * LANES), BF),
            pltpu.VMEM((XG, KX), BF),
            pltpu.VMEM((KX, XG), BF),
            pltpu.VMEM((KX, 2 * YG), BF),
            pltpu.VMEM((XG, 2 * YG), BF),
            pltpu.VMEM((2, modes, NZ), F32),
            pltpu.VMEM((modes, NZ), F32),
            pltpu.VMEM((2, modes, NZ), BF),
            dma((2, PAIRS // 2)),
            pltpu.VMEM((ZPART,), F32),
            pltpu.VMEM((ZG, NZ), BF),
            pltpu.VMEM((KY, YG), BF),
            pltpu.VMEM((YG, KY), BF),
            pltpu.VMEM((NZ, NZ), BF),
            pltpu.VMEM((NZ, NZ), BF),
            dma((5,)), dma((2, ZC)), dma((ROWS,)), dma((2, COLS)), dma((2, COLS)),
            dma((G, COLS)), dma((G, COLS)), dma((G // 2 + 1, ROWS)), dma((G // 2 + 1, ROWS)),
            dma((G // 2 + 1, ROWS)), dma((G, ZC)), dma((G, COLS)), dma((G, COLS)),
            dma, dma,
        ],
        compiler_params=pltpu.CompilerParams(
            collective_id=0, has_side_effects=True, vmem_limit_bytes=VMEM_LIMIT
        ),
        name="section",
    )(
        vel_w.reshape(modes, NZ), buoy.reshape(modes, NZ), *consts, strat, eig_val, eig_left, eig_right
    )
    return new_buoy.reshape(buoy.shape), new_vel.reshape(buoy.shape)


def solution(mesh):
    in_specs = (P("row", "col", None), P("row", "col", None), P("col"), P(), P(), P())
    out_specs = (P("row", "col", None), P("row", "col", None))
    return jax.shard_map(
        per_device, mesh=mesh, in_specs=in_specs, out_specs=out_specs, check_vma=False
    )
```

```python
import functools
import math

import jax
import jax.numpy as jnp
import numpy as np
from jax import lax
from jax.experimental import pallas as pl
from jax.experimental.pallas import tpu as pltpu
from jax.sharding import PartitionSpec as P

KX = 512
KY = 512
NZ = 384
XG = 768
YG = 768
ZG = 576

explicit_step = 0.5
diffuse_buoy = 0.5
diffuse_vel = 0.25
couple_buoy = 0.7
couple_vel = 0.7

ROWS = 16
COLS = 8
A = KX // ROWS
K = KY // COLS
PAIRS = A // 2
LANES = 2 * K
G = 9
PASSES = 3
ZPART = ZG // COLS
ZC = ZPART // G
SIZE = ZC * PAIRS
TWO = 2 * LANES
TALL = 4 * COLS * SIZE
ORDER = (0, 6, 7, 1, 2, 3, 4, 5, 8)
TURN = 3
ENDS = (4, 8, 9)
BF = jnp.bfloat16
F32 = jnp.float32
MESH = pl.DeviceIdType.MESH
VMEM_LIMIT = 67_000_000


def trig(modes, points):
    order = np.arange(modes)
    freq = ((order + 1) // 2).astype(np.float32)
    step = np.float32(2.0 * math.pi / points)
    angle = (step * freq)[:, None] * np.arange(points, dtype=np.float32)[None, :]
    angle = angle.astype(np.float64)
    values = np.where((order % 2 == 0)[:, None], np.cos(angle), np.sin(angle))
    return order, values.astype(np.float32)


def fourier_eval(modes, points):
    _, values = trig(modes, points)
    return (values * np.float32(math.sqrt(2.0 / modes))).astype(BF)


def fourier_proj(modes, points):
    order, values = trig(modes, points)
    weight = np.where(order == 0, 1.0 / points, 2.0 / points).astype(np.float32)
    return (values * weight[:, None] * np.float32(math.sqrt(modes / 2.0))).T.astype(BF)


def cheb_tables(degree, points):
    order = np.arange(degree, dtype=np.float32)
    theta = np.float32(math.pi) * (np.arange(points, dtype=np.float32) + np.float32(0.5))
    theta = theta / np.float32(points)
    angle = (order[:, None] * theta[None, :]).astype(np.float64)
    cos, sin = np.cos(angle).astype(np.float32), np.sin(angle).astype(np.float32)
    norm = np.float32(math.sqrt(2.0 / degree))
    weight = np.where(order == 0, 1.0 / points, 2.0 / points).astype(np.float32)
    levels = cos * norm
    slopes = -(order[:, None] / np.float32(degree)) * sin * norm
    projector = (cos * weight[:, None] * np.float32(math.sqrt(degree / 2.0))).T
    return levels.astype(BF), slopes.astype(BF), projector.astype(BF)


def tables():
    levels, slopes, projector = cheb_tables(NZ, ZG)

    def by_chunk(rows):
        return np.asarray(rows).reshape(COLS, ZC, G, NZ).transpose(2, 0, 1, 3).reshape(ZG, NZ)

    lift, slope = (
        by_chunk(np.asarray(t).T).reshape(G, -1, NZ)[list(ORDER)].reshape(PASSES, -1, NZ) for t in (levels, slopes)
    )
    return lift, slope, by_chunk(projector), fourier_eval(KY, YG), np.ascontiguousarray(fourier_proj(KY, YG))


def mm(left, right, dims=((1,), (0,))):
    return lax.dot_general(left, right, (dims, ((), ())), preferred_element_type=F32)


def kernel(
    vel, buoy, lift, slope, drop_in, evals_in, projs_in, strat, eig_val, left_in, right_in,
    out_buoy, out_vel,
    lifted, arrived, planes, passed, folded, tall, wide_eval, wide_proj, eval_x, proj_x, middle, flux, partial,
    inverses, done, done_s, strat_in, drop, evals, projs, eig_left, eig_right, load_s,
    turn_s, turn_r, hop_s, hop_r, colf_s, colf_r, rowf_s, rowf_r, rowb_s, rowb_r, colb_s, colb_r, strat_s, strat_r,
):
    row, col = lax.axis_index("row"), lax.axis_index("col")
    high = row // (ROWS // 2)
    base, low = (col // 2) * 2, col % 2
    part = base + (low + high) % 2

    def col_of(q):
        return (row, (q // 2) * 2 + (q % 2 + high) % 2)

    def row_of(t):
        return (t, base + (low + high + t // (ROWS // 2)) % 2)

    barrier = pltpu.get_barrier_semaphore()

    @pl.loop(1, COLS)
    def _(i):
        pl.semaphore_signal(barrier, inc=1, device_id=col_of((part + i) % COLS), device_id_type=MESH)

    @pl.loop(1, ROWS)
    def _(i):
        pl.semaphore_signal(barrier, inc=1, device_id=row_of((row + i) % ROWS), device_id_type=MESH)

    loads = [
        pltpu.make_async_copy(src, dst, load_s.at[n])
        for n, (src, dst) in enumerate(
            ((evals_in, evals), (projs_in, projs), (drop_in, drop), (left_in, eig_left), (right_in, eig_right))
        )
    ]
    for load in loads:
        load.start()

    def remote(src, dst, send, recv, device):
        return pltpu.make_async_remote_copy(
            src_ref=src, dst_ref=dst, send_sem=send, recv_sem=recv, device_id=device, device_id_type=MESH
        )

    chip, core = row // 2, row % 2

    def col_fwd(g, q):
        return remote(lifted.at[g, q], arrived.at[g, :, col], colf_s.at[g, q], colf_r.at[g, col], col_of(q))

    def col_fwd_in(g, s):
        block = arrived.at[g, :, s]
        return remote(block, block, colf_s.at[g, s], colf_r.at[g, s], col_of(0))

    def col_fwd_own(g):
        return pltpu.make_async_copy(lifted.at[g, part], arrived.at[g, :, col], colf_r.at[g, col])

    def col_back(g, s):
        return remote(passed.at[g, :, s], folded.at[g, part], colb_s.at[g, s], colb_r.at[g, part], (row, s))

    def col_back_in(g, q):
        block = folded.at[g, q]
        return remote(block, block, colb_s.at[g, q], colb_r.at[g, q], col_of(q))

    def col_back_own(g):
        return pltpu.make_async_copy(passed.at[g, :, col], folded.at[g, part], colb_r.at[g, part])

    def others(first, count, do):
        @pl.loop(1, count)
        def _(i):
            do((first + i) % count)

    def row_fwd(g, t):
        m = g // 2
        return remote(arrived.at[g, t // 2], planes.at[m, row], rowf_s.at[m, t], rowf_r.at[m, row], row_of(t))

    def row_fwd_in(m, t):
        block = planes.at[m, t]
        return remote(block, block, rowf_s.at[m, t], rowf_r.at[m, t], row_of(t))

    def row_fwd_own(g):
        m = g // 2
        return pltpu.make_async_copy(arrived.at[g, chip], planes.at[m, row], rowf_r.at[m, row])

    def row_back(m, g, t):
        return remote(planes.at[m, t], passed.at[g, chip], rowb_s.at[m, t], rowb_r.at[g, chip], row_of(t))

    def row_back_in(g, t):
        block = passed.at[g, t // 2]
        return remote(block, block, rowb_s.at[0, t], rowb_r.at[g, t // 2], row_of(t))

    def row_back_own(m, g):
        return pltpu.make_async_copy(planes.at[m, row], passed.at[g, chip], rowb_r.at[g, chip])

    def chips(side, here, there):
        @pl.loop(0, ZC)
        def _(i):
            t = ((chip + i) % ZC) * 2 + side
            pl.when(t == row)(lambda: here())
            pl.when(t != row)(lambda: there(t))

    def members(here, there):
        chips(core, here, there)
        chips(1 - core, here, there)

    def turn_out(g, t):
        return remote(
            lifted.at[g, t // 2], arrived.at[2 * TURN + high, row % 8], turn_s.at[g % 2, t // 2], turn_r.at[row], row_of(t)
        )

    def turn_own(g):
        return pltpu.make_async_copy(lifted.at[g, chip], arrived.at[2 * TURN + high, row % 8], turn_r.at[row])

    def turn_in(t):
        block = arrived.at[2 * TURN + t // 8, t % 8]
        return remote(block, block, turn_s.at[0, 0], turn_r.at[t], row_of(t))

    def landing(h, s):
        return planes.at[TURN, h * 8 : (h + 1) * 8, (s // 2) * 2 + (s % 2 + high + h) % 2]

    def hop(h, q):
        return remote(arrived.at[2 * TURN + h, :, q], landing(h, col), hop_s.at[h, q], hop_r.at[h, col], col_of(q))

    def hop_in(h, s):
        return remote(landing(h, s), landing(h, s), hop_s.at[h, s], hop_r.at[h, s], col_of(0))

    def hop_own(h):
        return pltpu.make_async_copy(arrived.at[2 * TURN + h, :, part], landing(h, col), hop_r.at[h, col])

    def relay_turned():
        members(lambda: turn_own(2 * TURN).wait(), lambda t: turn_in(t).wait_recv())
        for h in range(2):
            others(part, COLS, lambda q: hop(h, q).start())
            hop_own(h).start()

    def relay_fwd(g):
        others(col, COLS, lambda s: col_fwd_in(g, s).wait_recv())
        col_fwd_own(g).wait()

        chips(g % 2, lambda: row_fwd_own(g).start(), lambda t: row_fwd(g, t).start())

    def relay_back(g):
        chips(g % 2, lambda: row_back_own(0, g).wait(), lambda t: row_back_in(g, t).wait_recv())
        others(col, COLS, lambda s: col_back(g, s).start())
        col_back_own(g).start()

    count = ZG // PASSES
    chunks = G // PASSES

    def chunk_at(i):
        return jnp.where(i == 0, 0, jnp.where(i < 3, i + 5, jnp.where(i < 8, i - 2, 8)))

    def to_points(u):
        for f, (table, field) in enumerate(((lift, vel), (slope, buoy))):

            @pl.loop(0, PAIRS // 2)
            def _(p):
                rows = pl.ds(pl.multiple_of(p * TWO, TWO), TWO)
                values = mm(table[u], field[rows, :], ((1,), (1,)))
                tall[pl.ds(2 * p, count, stride=PAIRS), :] = values[:, :LANES]
                tall[pl.ds(2 * p + 1, count, stride=PAIRS), :] = values[:, LANES:]

            @pl.loop(0, COLS * chunks)
            def _(i):
                rows = pl.ds(pl.multiple_of(i * SIZE, SIZE), SIZE)
                block = tall[rows, :].astype(BF).reshape(ZC, PAIRS, LANES)
                g, q = chunk_at(u * chunks + i // COLS), i % COLS

                @pl.when(g // 2 != TURN)
                def _():
                    lifted[g, q, :, f] = block

                @pl.when(g // 2 == TURN)
                def _():
                    lifted[g, :, q, f] = block

    def send_points(u):
        @pl.loop(u * chunks, (u + 1) * chunks)
        def _(i):
            g = chunk_at(i)

            @pl.when(g // 2 != TURN)
            def _():
                others(part, COLS, lambda q: col_fwd(g, q).start())
                col_fwd_own(g).start()

            @pl.when(g // 2 == TURN)
            def _():
                chips(g % 2, lambda: turn_own(g).start(), lambda t: turn_out(g, t).start())

    to_points(0)
    pl.semaphore_wait(barrier, COLS + ROWS - 2)
    send_points(0)
    swap = remote(strat, strat_in, strat_s, strat_r, (row, base + 1 - low))
    swap.start()

    @pl.loop(1, PASSES)
    def _(u):
        to_points(u)
        send_points(u)

    for load in loads:
        load.wait()

    @pl.loop(0, COLS)
    def _(s):
        for a in range(2):
            own = pl.ds(pl.multiple_of(s * LANES + a * K, K), K)
            other = pl.ds(pl.multiple_of(s * LANES + (1 - a) * K, K), K)
            wide_eval[a, own, :] = evals[pl.ds(pl.multiple_of(s * K, K), K), :]
            wide_eval[a, other, :] = jnp.zeros((K, YG), BF)

    relay_fwd(0)

    lane = lax.broadcasted_iota(jnp.int32, (LANES, LANES), 1)

    @pl.loop(0, YG // LANES)
    def _(i):
        for j in range(COLS // 2):
            rows = pl.ds(pl.multiple_of(i * LANES, LANES), LANES)
            tile = projs[rows, j * LANES : (j + 1) * LANES].astype(F32)
            turned = pltpu.roll(tile, K, 1)
            for s in (2 * j, 2 * j + 1):
                straight, moved = (tile, turned) if s % 2 == 0 else (turned, tile)
                for a in range(2):
                    keep = jnp.where((lane < K) == (a == 0), straight if a == 0 else moved, 0.0).astype(BF)
                    to = pl.ds(pl.multiple_of(a * YG + i * LANES, LANES), LANES)
                    wide_proj[to, s * LANES : (s + 1) * LANES] = keep

    relay_fwd(1)

    @pl.loop(0, XG // LANES)
    def _(j):
        points = pl.ds(pl.multiple_of(j * LANES, LANES), LANES)

        def ordered(values):
            tall[:KX, :] = values
            return jnp.concatenate([tall[pl.ds(a, KX // 2, stride=2), :] for a in range(2)], axis=0)

        eval_x[points, :] = ordered(evals[:, points].astype(F32)).T.astype(BF)
        proj_x[:, points] = ordered(projs[points, :].astype(F32).T).astype(BF)

    relay_fwd(2)

    def diagonals(p):
        place = p * TWO + lax.broadcasted_iota(jnp.int32, (TWO, LANES), 0)
        freq_x = ((row * A + (place >> 6) + 1) >> 1).astype(F32) * (2.0 / KX)
        freq_y = ((col * K + (place & (K - 1)) + 1) >> 1).astype(F32) * (2.0 / KY)
        wave = 4.0 * (freq_x * freq_x + freq_y * freq_y)
        lapl = jnp.concatenate([wave] * (NZ // LANES), axis=1) + eig_val[...].reshape(1, NZ)
        return 1.0 + diffuse_buoy * lapl, 1.0 + diffuse_vel * lapl

    @pl.loop(0, PAIRS // 2)
    def _(p):
        rows = pl.ds(pl.multiple_of(p * TWO, TWO), TWO)
        diag_buoy, diag_vel = diagonals(p)
        inverses[rows, :] = 1.0 / (diag_buoy * diag_vel + couple_buoy * couple_vel)

    def result(f, p):
        rows = pl.ds(pl.multiple_of(p * TWO, TWO), TWO)
        return pltpu.make_async_copy(done.at[f, rows, :], (out_buoy, out_vel)[f].at[rows, :], done_s.at[f, p])

    pl.loop(3, 5)(relay_fwd)
    relay_turned()
    swap.wait()
    strata = jnp.where(high == 0, strat[...], strat_in[...]).reshape(1, ZPART)
    level_of = lax.broadcasted_iota(jnp.int32, (1, ZPART), 1)

    half = KX // 2
    last = G // 2

    @pl.loop(0, last + 1 - core)
    def _(m):
        chunk = 2 * m + core

        @pl.when(m != TURN)
        def _():
            members(lambda: row_fwd_own(2 * m).wait(), lambda t: row_fwd_in(m, t).wait_recv())

        @pl.when(m == TURN)
        def _():
            pl.loop(0, 2)(relay_back)
            for h in range(2):
                others(col, COLS, lambda s: hop_in(h, s).wait_recv())
                hop_own(h).wait()

        for f in range(2):
            left = jnp.concatenate([planes[m, :, s, f].reshape(half, LANES) for s in range(COLS)], axis=1)
            for a in range(2):
                middle[a * half : (a + 1) * half, f * YG : (f + 1) * YG] = mm(left, wide_eval[a]).astype(BF)

        pl.when(m < 2)(lambda: relay_fwd(5 + 3 * m))

        level = jnp.sum(jnp.where(level_of == chip * G + chunk, strata, 0.0), axis=1, keepdims=True)
        tile = XG // 3

        @pl.loop(0, 3)
        def _(x):
            rows = pl.ds(pl.multiple_of(x * tile, tile), tile)
            velocity = mm(eval_x[rows, :], middle[:, :YG]).astype(BF).astype(F32)
            gradient = mm(eval_x[rows, :], middle[:, YG:]).astype(BF).astype(F32)
            flux[rows, :YG] = (-(velocity * gradient) - level * velocity).astype(BF)
            flux[rows, YG:] = (-(velocity * jnp.abs(velocity))).astype(BF)


        @pl.loop(0, 2)
        def _(a):
            rows = pl.ds(pl.multiple_of(a * half, half), half)
            for f in range(2):
                middle[rows, f * YG : (f + 1) * YG] = mm(proj_x[rows, :], flux[:, f * YG : (f + 1) * YG]).astype(BF)
        for f in range(2):
            left = jnp.concatenate(
                [middle[a * half : (a + 1) * half, f * YG : (f + 1) * YG] for a in range(2)], axis=1
            )
            values = mm(left, wide_proj[...]).astype(BF)
            for s in range(COLS):
                planes[m, :, s, f] = values[:, s * LANES : (s + 1) * LANES].reshape(ROWS, PAIRS, LANES)

        members(lambda: row_back_own(m, chunk).start(), lambda t: row_back(m, chunk, t).start())

        @pl.when(m == last - 1)
        def _():
            pl.loop(2, 4)(relay_back)

    def gather(first, last, f, start):
        @pl.loop(first, last)
        def _(g):
            for q in range(COLS):
                place = pl.multiple_of(start + ((g - first) * COLS + q) * SIZE, SIZE)
                tall[pl.ds(place, SIZE), :] = folded[g, q, :, f].reshape(SIZE, LANES).astype(F32)

    def tendency(first, last, p, start):
        count = (last - first) * COLS * ZC
        columns = [tall[pl.ds(start + 2 * p + a, count, stride=PAIRS), :].astype(BF) for a in range(2)]
        rows = slice(first * COLS * ZC, last * COLS * ZC)
        return mm(jnp.concatenate(columns, axis=1), drop[rows, :], ((0,), (0,)))

    def wait_modes(first, last):
        @pl.loop(first, last)
        def _(g):
            others(part, COLS, lambda q: col_back_in(g, q).wait_recv())
            col_back_own(g).wait()

    pl.loop(4, ENDS[0] + 2)(relay_back)
    wait_modes(0, ENDS[0])
    for f in range(2):
        gather(0, ENDS[0], f, 0)

        @pl.loop(0, PAIRS // 2)
        def _(p):
            rows = pl.ds(pl.multiple_of(p * TWO, TWO), TWO)
            partial[f, rows, :] = tendency(0, ENDS[0], p, 0)

    pl.loop(ENDS[0] + 2, G)(relay_back)
    wait_modes(ENDS[0], ENDS[1])
    for f in range(2):
        gather(ENDS[0], ENDS[1], f, 0)

        @pl.loop(0, PAIRS // 2)
        def _(p):
            rows = pl.ds(pl.multiple_of(p * TWO, TWO), TWO)
            partial[f, rows, :] += tendency(ENDS[0], ENDS[1], p, 0)

    wait_modes(ENDS[1], G)
    start = (G - ENDS[1]) * COLS * SIZE
    for f in range(2):
        gather(ENDS[1], G, f, f * start)

    @pl.loop(0, PAIRS // 2)
    def _(p):
        rows = pl.ds(pl.multiple_of(p * TWO, TWO), TWO)
        modal = []
        for f, field in enumerate((buoy, vel)):
            tend = partial[f, rows, :] + tendency(ENDS[1], G, p, f * start)
            rhs = (field[rows, :].astype(F32) + explicit_step * tend).astype(BF)
            modal.append(mm(rhs, eig_left[...]))
        modal_buoy, modal_vel = modal
        diag_buoy, diag_vel = diagonals(p)
        inverse = inverses[rows, :]
        solved_buoy = ((diag_vel * modal_buoy - couple_buoy * modal_vel) * inverse).astype(BF)
        solved_vel = ((diag_buoy * modal_vel + couple_vel * modal_buoy) * inverse).astype(BF)
        done[0, rows, :] = mm(solved_buoy, eig_right[...]).astype(BF)
        done[1, rows, :] = mm(solved_vel, eig_right[...]).astype(BF)
        result(0, p).start()
        result(1, p).start()

    @pl.loop(0, PAIRS // 2)
    def _(p):
        result(0, p).wait()
        result(1, p).wait()

    def nothing():
        pass

    for h in range(2):
        others(part, COLS, lambda q: hop(h, q).wait_send())

    @pl.loop(0, G)
    def _(g):
        @pl.when(g // 2 != TURN)
        def _():
            others(part, COLS, lambda q: col_fwd(g, q).wait_send())

        @pl.when(g // 2 == TURN)
        def _():
            chips(g % 2, nothing, lambda t: turn_out(g, t).wait_send())

        others(col, COLS, lambda s: col_back(g, s).wait_send())

    @pl.loop(0, last)
    def _(m):
        pl.when(m != TURN)(lambda: members(nothing, lambda t: row_fwd(2 * m, t).wait_send()))

    @pl.loop(0, last + 1 - core)
    def _(m):
        members(nothing, lambda t: row_back(m, 2 * m, t).wait_send())

    chips(0, nothing, lambda t: row_fwd(G - 1, t).wait_send())


def per_device(buoy, vel_w, strat, eig_val, eig_left, eig_right):
    modes = A * K
    dma = pltpu.SemaphoreType.DMA
    vmem = pl.BlockSpec(memory_space=pltpu.VMEM)
    hbm = pl.BlockSpec(memory_space=pl.ANY)
    shape = jax.ShapeDtypeStruct((modes, NZ), BF)
    consts = [jnp.asarray(t) for t in tables()]
    new_buoy, new_vel = pl.pallas_call(
        kernel,
        out_shape=(shape, shape),
        in_specs=[vmem] * 4 + [hbm] * 3 + [vmem] * 2 + [hbm] * 2,
        out_specs=(hbm, hbm),
        scratch_shapes=[
            pltpu.VMEM((G, COLS, ZC, 2, PAIRS, LANES), BF),
            pltpu.VMEM((G, ZC, COLS, 2, PAIRS, LANES), BF),
            pltpu.VMEM((G // 2 + 1, ROWS, COLS, 2, PAIRS, LANES), BF),
            pltpu.VMEM((G, ZC, COLS, 2, PAIRS, LANES), BF),
            pltpu.VMEM((G, COLS, ZC, 2, PAIRS, LANES), BF),
            pltpu.VMEM((TALL, LANES), F32),
            pltpu.VMEM((2, COLS * LANES, YG), BF),
            pltpu.VMEM((2 * YG, COLS * LANES), BF),
            pltpu.VMEM((XG, KX), BF),
            pltpu.VMEM((KX, XG), BF),
            pltpu.VMEM((KX, 2 * YG), BF),
            pltpu.VMEM((XG, 2 * YG), BF),
            pltpu.VMEM((2, modes, NZ), F32),
            pltpu.VMEM((modes, NZ), F32),
            pltpu.VMEM((2, modes, NZ), BF),
            dma((2, PAIRS // 2)),
            pltpu.VMEM((ZPART,), F32),
            pltpu.VMEM((ZG, NZ), BF),
            pltpu.VMEM((KY, YG), BF),
            pltpu.VMEM((YG, KY), BF),
            pltpu.VMEM((NZ, NZ), BF),
            pltpu.VMEM((NZ, NZ), BF),
            dma((5,)), dma((2, ZC)), dma((ROWS,)), dma((2, COLS)), dma((2, COLS)),
            dma((G, COLS)), dma((G, COLS)), dma((G // 2 + 1, ROWS)), dma((G // 2 + 1, ROWS)),
            dma((G // 2 + 1, ROWS)), dma((G, ZC)), dma((G, COLS)), dma((G, COLS)),
            dma, dma,
        ],
        compiler_params=pltpu.CompilerParams(
            collective_id=0, has_side_effects=True, vmem_limit_bytes=VMEM_LIMIT
        ),
        name="section",
    )(
        vel_w.reshape(modes, NZ), buoy.reshape(modes, NZ), *consts, strat, eig_val, eig_left, eig_right
    )
    return new_buoy.reshape(buoy.shape), new_vel.reshape(buoy.shape)


def solution(mesh):
    in_specs = (P("row", "col", None), P("row", "col", None), P("col"), P(), P(), P())
    out_specs = (P("row", "col", None), P("row", "col", None))
    return jax.shard_map(
        per_device, mesh=mesh, in_specs=in_specs, out_specs=out_specs, check_vma=False
    )
```

```python
import functools
import math

import jax
import jax.numpy as jnp
import numpy as np
from jax import lax
from jax.experimental import pallas as pl
from jax.experimental.pallas import tpu as pltpu
from jax.sharding import PartitionSpec as P

KX = 512
KY = 512
NZ = 384
XG = 768
YG = 768
ZG = 576

explicit_step = 0.5
diffuse_buoy = 0.5
diffuse_vel = 0.25
couple_buoy = 0.7
couple_vel = 0.7

ROWS = 16
COLS = 8
A = KX // ROWS
K = KY // COLS
PAIRS = A // 2
LANES = 2 * K
G = 9
PASSES = 3
ZPART = ZG // COLS
ZC = ZPART // G
SIZE = ZC * PAIRS
TWO = 2 * LANES
TALL = 4 * COLS * SIZE
ORDER = (0, 4, 5, 1, 6, 7, 2, 3, 8)
ENDS = (4, 8, 9)
BF = jnp.bfloat16
F32 = jnp.float32
MESH = pl.DeviceIdType.MESH
VMEM_LIMIT = 67_000_000


def trig(modes, points):
    order = np.arange(modes)
    freq = ((order + 1) // 2).astype(np.float32)
    step = np.float32(2.0 * math.pi / points)
    angle = (step * freq)[:, None] * np.arange(points, dtype=np.float32)[None, :]
    angle = angle.astype(np.float64)
    values = np.where((order % 2 == 0)[:, None], np.cos(angle), np.sin(angle))
    return order, values.astype(np.float32)


def fourier_eval(modes, points):
    _, values = trig(modes, points)
    return (values * np.float32(math.sqrt(2.0 / modes))).astype(BF)


def fourier_proj(modes, points):
    order, values = trig(modes, points)
    weight = np.where(order == 0, 1.0 / points, 2.0 / points).astype(np.float32)
    return (values * weight[:, None] * np.float32(math.sqrt(modes / 2.0))).T.astype(BF)


def cheb_tables(degree, points):
    order = np.arange(degree, dtype=np.float32)
    theta = np.float32(math.pi) * (np.arange(points, dtype=np.float32) + np.float32(0.5))
    theta = theta / np.float32(points)
    angle = (order[:, None] * theta[None, :]).astype(np.float64)
    cos, sin = np.cos(angle).astype(np.float32), np.sin(angle).astype(np.float32)
    norm = np.float32(math.sqrt(2.0 / degree))
    weight = np.where(order == 0, 1.0 / points, 2.0 / points).astype(np.float32)
    levels = cos * norm
    slopes = -(order[:, None] / np.float32(degree)) * sin * norm
    projector = (cos * weight[:, None] * np.float32(math.sqrt(degree / 2.0))).T
    return levels.astype(BF), slopes.astype(BF), projector.astype(BF)


def tables():
    levels, slopes, projector = cheb_tables(NZ, ZG)

    def by_chunk(rows):
        return np.asarray(rows).reshape(COLS, ZC, G, NZ).transpose(2, 0, 1, 3).reshape(ZG, NZ)

    lift, slope = (
        by_chunk(np.asarray(t).T).reshape(G, -1, NZ)[list(ORDER)].reshape(PASSES, -1, NZ) for t in (levels, slopes)
    )
    return lift, slope, by_chunk(projector), fourier_eval(KY, YG), np.ascontiguousarray(fourier_proj(KY, YG))


def mm(left, right, dims=((1,), (0,))):
    return lax.dot_general(left, right, (dims, ((), ())), preferred_element_type=F32)


def kernel(
    vel, buoy, lift, slope, drop_in, evals_in, projs_in, strat, eig_val, left_in, right_in,
    out_buoy, out_vel,
    lifted, arrived, planes, passed, folded, tall, wide_eval, wide_proj, eval_x, proj_x, middle, flux, partial,
    inverses, done, done_s, strat_in, drop, evals, projs, eig_left, eig_right, load_s,
    turn_s, turn_r, hop_s, hop_r, colf_s, colf_r, rowf_s, rowf_r, rowb_s, rowb_r, colb_s, colb_r, strat_s, strat_r,
):
    row, col = lax.axis_index("row"), lax.axis_index("col")
    high = row // (ROWS // 2)
    base, low = (col // 2) * 2, col % 2
    part = base + (low + high) % 2

    def col_of(q):
        return (row, (q // 2) * 2 + (q % 2 + high) % 2)

    def row_of(t):
        return (t, base + (low + high + t // (ROWS // 2)) % 2)

    barrier = pltpu.get_barrier_semaphore()

    @pl.loop(1, COLS)
    def _(i):
        pl.semaphore_signal(barrier, inc=1, device_id=col_of((part + i) % COLS), device_id_type=MESH)

    @pl.loop(1, ROWS)
    def _(i):
        pl.semaphore_signal(barrier, inc=1, device_id=row_of((row + i) % ROWS), device_id_type=MESH)

    loads = [
        pltpu.make_async_copy(src, dst, load_s.at[n])
        for n, (src, dst) in enumerate(
            ((evals_in, evals), (projs_in, projs), (drop_in, drop), (left_in, eig_left), (right_in, eig_right))
        )
    ]
    for load in loads:
        load.start()

    def remote(src, dst, send, recv, device):
        return pltpu.make_async_remote_copy(
            src_ref=src, dst_ref=dst, send_sem=send, recv_sem=recv, device_id=device, device_id_type=MESH
        )

    chip, core = row // 2, row % 2

    def col_fwd(g, q):
        return remote(lifted.at[g, q], arrived.at[g, :, col], colf_s.at[g, q], colf_r.at[g, col], col_of(q))

    def col_fwd_in(g, s):
        block = arrived.at[g, :, s]
        return remote(block, block, colf_s.at[g, s], colf_r.at[g, s], col_of(0))

    def col_fwd_own(g):
        return pltpu.make_async_copy(lifted.at[g, part], arrived.at[g, :, col], colf_r.at[g, col])

    def col_back(g, s):
        return remote(passed.at[g, :, s], folded.at[g, part], colb_s.at[g, s], colb_r.at[g, part], (row, s))

    def col_back_in(g, q):
        block = folded.at[g, q]
        return remote(block, block, colb_s.at[g, q], colb_r.at[g, q], col_of(q))

    def col_back_own(g):
        return pltpu.make_async_copy(passed.at[g, :, col], folded.at[g, part], colb_r.at[g, part])

    def others(first, count, do):
        @pl.loop(1, count)
        def _(i):
            do((first + i) % count)

    def row_fwd(g, t):
        m = g // 2
        return remote(arrived.at[g, t // 2], planes.at[m, row], rowf_s.at[m, t], rowf_r.at[m, row], row_of(t))

    def row_fwd_in(m, t):
        block = planes.at[m, t]
        return remote(block, block, rowf_s.at[m, t], rowf_r.at[m, t], row_of(t))

    def row_fwd_own(g):
        m = g // 2
        return pltpu.make_async_copy(arrived.at[g, chip], planes.at[m, row], rowf_r.at[m, row])

    def row_back(m, g, t):
        return remote(planes.at[m, t], passed.at[g, chip], rowb_s.at[m, t], rowb_r.at[g, chip], row_of(t))

    def row_back_in(g, t):
        block = passed.at[g, t // 2]
        return remote(block, block, rowb_s.at[0, t], rowb_r.at[g, t // 2], row_of(t))

    def row_back_own(m, g):
        return pltpu.make_async_copy(planes.at[m, row], passed.at[g, chip], rowb_r.at[g, chip])

    def chips(side, here, there):
        @pl.loop(0, ZC)
        def _(i):
            t = ((chip + i) % ZC) * 2 + side
            pl.when(t == row)(lambda: here())
            pl.when(t != row)(lambda: there(t))

    def members(here, there):
        chips(core, here, there)
        chips(1 - core, here, there)

    def turn_out(g, t):
        m = g // 2
        return remote(
            lifted.at[g, t // 2], arrived.at[2 * m + high, row % 8], turn_s.at[g - 4, t // 2], turn_r.at[m - 2, row], row_of(t)
        )

    def turn_own(g):
        m = g // 2
        return pltpu.make_async_copy(lifted.at[g, chip], arrived.at[2 * m + high, row % 8], turn_r.at[m - 2, row])

    def turn_in(m, t):
        block = arrived.at[2 * m + t // 8, t % 8]
        return remote(block, block, turn_s.at[0, 0], turn_r.at[m - 2, t], row_of(t))

    def landing(m, h, s):
        return planes.at[m, h * 8 : (h + 1) * 8, (s // 2) * 2 + (s % 2 + high + h) % 2]

    def hop(m, h, q):
        return remote(
            arrived.at[2 * m + h, :, q], landing(m, h, col), hop_s.at[m - 2, h, q], hop_r.at[m - 2, h, col], col_of(q)
        )

    def hop_in(m, h, s):
        return remote(landing(m, h, s), landing(m, h, s), hop_s.at[m - 2, h, s], hop_r.at[m - 2, h, s], col_of(0))

    def hop_own(m, h):
        return pltpu.make_async_copy(arrived.at[2 * m + h, :, part], landing(m, h, col), hop_r.at[m - 2, h, col])

    def relay_turned(m):
        members(lambda: turn_own(2 * m).wait(), lambda t: turn_in(m, t).wait_recv())
        for h in range(2):
            others(part, COLS, lambda q: hop(m, h, q).start())
            hop_own(m, h).start()

    def relay_fwd(g):
        others(col, COLS, lambda s: col_fwd_in(g, s).wait_recv())
        col_fwd_own(g).wait()

        chips(g % 2, lambda: row_fwd_own(g).start(), lambda t: row_fwd(g, t).start())

    def relay_back(g):
        chips(g % 2, lambda: row_back_own(0, g).wait(), lambda t: row_back_in(g, t).wait_recv())
        others(col, COLS, lambda s: col_back(g, s).start())
        col_back_own(g).start()

    count = ZG // PASSES
    chunks = G // PASSES

    def chunk_at(i):
        late = jnp.where(i < 6, i + 2, jnp.where(i < 8, i - 4, 8))
        return jnp.where(i == 0, 0, jnp.where(i < 3, i + 3, jnp.where(i == 3, 1, late)))

    def to_points(u):
        for f, (table, field) in enumerate(((lift, vel), (slope, buoy))):

            @pl.loop(0, PAIRS // 2)
            def _(p):
                rows = pl.ds(pl.multiple_of(p * TWO, TWO), TWO)
                values = mm(table[u], field[rows, :], ((1,), (1,)))
                tall[pl.ds(2 * p, count, stride=PAIRS), :] = values[:, :LANES]
                tall[pl.ds(2 * p + 1, count, stride=PAIRS), :] = values[:, LANES:]

            @pl.loop(0, COLS * chunks)
            def _(i):
                rows = pl.ds(pl.multiple_of(i * SIZE, SIZE), SIZE)
                block = tall[rows, :].astype(BF).reshape(ZC, PAIRS, LANES)
                g, q = chunk_at(u * chunks + i // COLS), i % COLS

                @pl.when(g // 4 != 1)
                def _():
                    lifted[g, q, :, f] = block

                @pl.when(g // 4 == 1)
                def _():
                    lifted[g, :, q, f] = block

    def send_points(u):
        @pl.loop(u * chunks, (u + 1) * chunks)
        def _(i):
            g = chunk_at(i)

            @pl.when(g // 4 != 1)
            def _():
                others(part, COLS, lambda q: col_fwd(g, q).start())
                col_fwd_own(g).start()

            @pl.when(g // 4 == 1)
            def _():
                chips(g % 2, lambda: turn_own(g).start(), lambda t: turn_out(g, t).start())

    to_points(0)
    pl.semaphore_wait(barrier, COLS + ROWS - 2)
    send_points(0)
    swap = remote(strat, strat_in, strat_s, strat_r, (row, base + 1 - low))
    swap.start()

    @pl.loop(1, PASSES)
    def _(u):
        to_points(u)
        send_points(u)

    for load in loads:
        load.wait()

    @pl.loop(0, COLS)
    def _(s):
        for a in range(2):
            own = pl.ds(pl.multiple_of(s * LANES + a * K, K), K)
            other = pl.ds(pl.multiple_of(s * LANES + (1 - a) * K, K), K)
            wide_eval[a, own, :] = evals[pl.ds(pl.multiple_of(s * K, K), K), :]
            wide_eval[a, other, :] = jnp.zeros((K, YG), BF)

    relay_fwd(0)

    lane = lax.broadcasted_iota(jnp.int32, (LANES, LANES), 1)

    @pl.loop(0, YG // LANES)
    def _(i):
        for j in range(COLS // 2):
            rows = pl.ds(pl.multiple_of(i * LANES, LANES), LANES)
            tile = projs[rows, j * LANES : (j + 1) * LANES].astype(F32)
            turned = pltpu.roll(tile, K, 1)
            for s in (2 * j, 2 * j + 1):
                straight, moved = (tile, turned) if s % 2 == 0 else (turned, tile)
                for a in range(2):
                    keep = jnp.where((lane < K) == (a == 0), straight if a == 0 else moved, 0.0).astype(BF)
                    to = pl.ds(pl.multiple_of(a * YG + i * LANES, LANES), LANES)
                    wide_proj[to, s * LANES : (s + 1) * LANES] = keep

    relay_fwd(1)

    @pl.loop(0, XG // LANES)
    def _(j):
        points = pl.ds(pl.multiple_of(j * LANES, LANES), LANES)

        def ordered(values):
            tall[:KX, :] = values
            return jnp.concatenate([tall[pl.ds(a, KX // 2, stride=2), :] for a in range(2)], axis=0)

        eval_x[points, :] = ordered(evals[:, points].astype(F32)).T.astype(BF)
        proj_x[:, points] = ordered(projs[points, :].astype(F32).T).astype(BF)

    relay_fwd(2)

    def diagonals(p):
        place = p * TWO + lax.broadcasted_iota(jnp.int32, (TWO, LANES), 0)
        freq_x = ((row * A + (place >> 6) + 1) >> 1).astype(F32) * (2.0 / KX)
        freq_y = ((col * K + (place & (K - 1)) + 1) >> 1).astype(F32) * (2.0 / KY)
        wave = 4.0 * (freq_x * freq_x + freq_y * freq_y)
        lapl = jnp.concatenate([wave] * (NZ // LANES), axis=1) + eig_val[...].reshape(1, NZ)
        return 1.0 + diffuse_buoy * lapl, 1.0 + diffuse_vel * lapl

    @pl.loop(0, PAIRS // 2)
    def _(p):
        rows = pl.ds(pl.multiple_of(p * TWO, TWO), TWO)
        diag_buoy, diag_vel = diagonals(p)
        inverses[rows, :] = 1.0 / (diag_buoy * diag_vel + couple_buoy * couple_vel)

    def result(f, p):
        rows = pl.ds(pl.multiple_of(p * TWO, TWO), TWO)
        return pltpu.make_async_copy(done.at[f, rows, :], (out_buoy, out_vel)[f].at[rows, :], done_s.at[f, p])

    @pl.loop(2, 4)
    def _(m):
        relay_turned(m)
        pl.when(m == 2)(lambda: relay_fwd(3))

    swap.wait()
    strata = jnp.where(high == 0, strat[...], strat_in[...]).reshape(1, ZPART)
    level_of = lax.broadcasted_iota(jnp.int32, (1, ZPART), 1)

    half = KX // 2
    last = G // 2

    @pl.loop(0, last + 1 - core)
    def _(m):
        chunk = 2 * m + core

        pl.when(m == last - 1)(lambda: pl.loop(0, 2)(relay_back))

        @pl.when(m // 2 != 1)
        def _():
            members(lambda: row_fwd_own(2 * m).wait(), lambda t: row_fwd_in(m, t).wait_recv())

        @pl.when(m // 2 == 1)
        def _():
            for h in range(2):
                others(col, COLS, lambda s: hop_in(m, h, s).wait_recv())
                hop_own(m, h).wait()

        for f in range(2):
            left = jnp.concatenate([planes[m, :, s, f].reshape(half, LANES) for s in range(COLS)], axis=1)
            for a in range(2):
                middle[a * half : (a + 1) * half, f * YG : (f + 1) * YG] = mm(left, wide_eval[a]).astype(BF)

        pl.when(m == 0)(lambda: relay_fwd(G - 1))

        level = jnp.sum(jnp.where(level_of == chip * G + chunk, strata, 0.0), axis=1, keepdims=True)
        tile = XG // 3

        @pl.loop(0, 3)
        def _(x):
            rows = pl.ds(pl.multiple_of(x * tile, tile), tile)
            velocity = mm(eval_x[rows, :], middle[:, :YG]).astype(BF).astype(F32)
            gradient = mm(eval_x[rows, :], middle[:, YG:]).astype(BF).astype(F32)
            flux[rows, :YG] = (-(velocity * gradient) - level * velocity).astype(BF)
            flux[rows, YG:] = (-(velocity * jnp.abs(velocity))).astype(BF)


        @pl.loop(0, 2)
        def _(a):
            rows = pl.ds(pl.multiple_of(a * half, half), half)
            for f in range(2):
                middle[rows, f * YG : (f + 1) * YG] = mm(proj_x[rows, :], flux[:, f * YG : (f + 1) * YG]).astype(BF)
        for f in range(2):
            left = jnp.concatenate(
                [middle[a * half : (a + 1) * half, f * YG : (f + 1) * YG] for a in range(2)], axis=1
            )
            values = mm(left, wide_proj[...]).astype(BF)
            for s in range(COLS):
                planes[m, :, s, f] = values[:, s * LANES : (s + 1) * LANES].reshape(ROWS, PAIRS, LANES)

        members(lambda: row_back_own(m, chunk).start(), lambda t: row_back(m, chunk, t).start())

        @pl.when(m == last - 1)
        def _():
            pl.loop(2, 4)(relay_back)

    def gather(first, last, f, start):
        @pl.loop(first, last)
        def _(g):
            for q in range(COLS):
                place = pl.multiple_of(start + ((g - first) * COLS + q) * SIZE, SIZE)
                tall[pl.ds(place, SIZE), :] = folded[g, q, :, f].reshape(SIZE, LANES).astype(F32)

    def tendency(first, last, p, start):
        count = (last - first) * COLS * ZC
        columns = [tall[pl.ds(start + 2 * p + a, count, stride=PAIRS), :].astype(BF) for a in range(2)]
        rows = slice(first * COLS * ZC, last * COLS * ZC)
        return mm(jnp.concatenate(columns, axis=1), drop[rows, :], ((0,), (0,)))

    def wait_modes(first, last):
        @pl.loop(first, last)
        def _(g):
            others(part, COLS, lambda q: col_back_in(g, q).wait_recv())
            col_back_own(g).wait()

    pl.loop(4, ENDS[0] + 2)(relay_back)
    wait_modes(0, ENDS[0])
    for f in range(2):
        gather(0, ENDS[0], f, 0)

        @pl.loop(0, PAIRS // 2)
        def _(p):
            rows = pl.ds(pl.multiple_of(p * TWO, TWO), TWO)
            partial[f, rows, :] = tendency(0, ENDS[0], p, 0)

    pl.loop(ENDS[0] + 2, G)(relay_back)
    wait_modes(ENDS[0], ENDS[1])
    for f in range(2):
        gather(ENDS[0], ENDS[1], f, 0)

        @pl.loop(0, PAIRS // 2)
        def _(p):
            rows = pl.ds(pl.multiple_of(p * TWO, TWO), TWO)
            partial[f, rows, :] += tendency(ENDS[0], ENDS[1], p, 0)

    wait_modes(ENDS[1], G)
    start = (G - ENDS[1]) * COLS * SIZE
    for f in range(2):
        gather(ENDS[1], G, f, f * start)

    @pl.loop(0, PAIRS // 2)
    def _(p):
        rows = pl.ds(pl.multiple_of(p * TWO, TWO), TWO)
        modal = []
        for f, field in enumerate((buoy, vel)):
            tend = partial[f, rows, :] + tendency(ENDS[1], G, p, f * start)
            rhs = (field[rows, :].astype(F32) + explicit_step * tend).astype(BF)
            modal.append(mm(rhs, eig_left[...]))
        modal_buoy, modal_vel = modal
        diag_buoy, diag_vel = diagonals(p)
        inverse = inverses[rows, :]
        solved_buoy = ((diag_vel * modal_buoy - couple_buoy * modal_vel) * inverse).astype(BF)
        solved_vel = ((diag_buoy * modal_vel + couple_vel * modal_buoy) * inverse).astype(BF)
        done[0, rows, :] = mm(solved_buoy, eig_right[...]).astype(BF)
        done[1, rows, :] = mm(solved_vel, eig_right[...]).astype(BF)
        result(0, p).start()
        result(1, p).start()

    @pl.loop(0, PAIRS // 2)
    def _(p):
        result(0, p).wait()
        result(1, p).wait()

    def nothing():
        pass

    @pl.loop(2, 4)
    def _(m):
        for h in range(2):
            others(part, COLS, lambda q: hop(m, h, q).wait_send())

    @pl.loop(0, G)
    def _(g):
        @pl.when(g // 4 != 1)
        def _():
            others(part, COLS, lambda q: col_fwd(g, q).wait_send())

        @pl.when(g // 4 == 1)
        def _():
            chips(g % 2, nothing, lambda t: turn_out(g, t).wait_send())

        others(col, COLS, lambda s: col_back(g, s).wait_send())

    @pl.loop(0, last)
    def _(m):
        pl.when(m // 2 != 1)(lambda: members(nothing, lambda t: row_fwd(2 * m, t).wait_send()))

    @pl.loop(0, last + 1 - core)
    def _(m):
        members(nothing, lambda t: row_back(m, 2 * m, t).wait_send())

    chips(0, nothing, lambda t: row_fwd(G - 1, t).wait_send())


def per_device(buoy, vel_w, strat, eig_val, eig_left, eig_right):
    modes = A * K
    dma = pltpu.SemaphoreType.DMA
    vmem = pl.BlockSpec(memory_space=pltpu.VMEM)
    hbm = pl.BlockSpec(memory_space=pl.ANY)
    shape = jax.ShapeDtypeStruct((modes, NZ), BF)
    consts = [jnp.asarray(t) for t in tables()]
    new_buoy, new_vel = pl.pallas_call(
        kernel,
        out_shape=(shape, shape),
        in_specs=[vmem] * 4 + [hbm] * 3 + [vmem] * 2 + [hbm] * 2,
        out_specs=(hbm, hbm),
        scratch_shapes=[
            pltpu.VMEM((G, COLS, ZC, 2, PAIRS, LANES), BF),
            pltpu.VMEM((G, ZC, COLS, 2, PAIRS, LANES), BF),
            pltpu.VMEM((G // 2 + 1, ROWS, COLS, 2, PAIRS, LANES), BF),
            pltpu.VMEM((G, ZC, COLS, 2, PAIRS, LANES), BF),
            pltpu.VMEM((G, COLS, ZC, 2, PAIRS, LANES), BF),
            pltpu.VMEM((TALL, LANES), F32),
            pltpu.VMEM((2, COLS * LANES, YG), BF),
            pltpu.VMEM((2 * YG, COLS * LANES), BF),
            pltpu.VMEM((XG, KX), BF),
            pltpu.VMEM((KX, XG), BF),
            pltpu.VMEM((KX, 2 * YG), BF),
            pltpu.VMEM((XG, 2 * YG), BF),
            pltpu.VMEM((2, modes, NZ), F32),
            pltpu.VMEM((modes, NZ), F32),
            pltpu.VMEM((2, modes, NZ), BF),
            dma((2, PAIRS // 2)),
            pltpu.VMEM((ZPART,), F32),
            pltpu.VMEM((ZG, NZ), BF),
            pltpu.VMEM((KY, YG), BF),
            pltpu.VMEM((YG, KY), BF),
            pltpu.VMEM((NZ, NZ), BF),
            pltpu.VMEM((NZ, NZ), BF),
            dma((5,)), dma((4, ZC)), dma((2, ROWS)), dma((2, 2, COLS)), dma((2, 2, COLS)),
            dma((G, COLS)), dma((G, COLS)), dma((G // 2 + 1, ROWS)), dma((G // 2 + 1, ROWS)),
            dma((G // 2 + 1, ROWS)), dma((G, ZC)), dma((G, COLS)), dma((G, COLS)),
            dma, dma,
        ],
        compiler_params=pltpu.CompilerParams(
            collective_id=0, has_side_effects=True, vmem_limit_bytes=VMEM_LIMIT
        ),
        name="section",
    )(
        vel_w.reshape(modes, NZ), buoy.reshape(modes, NZ), *consts, strat, eig_val, eig_left, eig_right
    )
    return new_buoy.reshape(buoy.shape), new_vel.reshape(buoy.shape)


def solution(mesh):
    in_specs = (P("row", "col", None), P("row", "col", None), P("col"), P(), P(), P())
    out_specs = (P("row", "col", None), P("row", "col", None))
    return jax.shard_map(
        per_device, mesh=mesh, in_specs=in_specs, out_specs=out_specs, check_vma=False
    )
```

```python
import functools
import math

import jax
import jax.numpy as jnp
import numpy as np
from jax import lax
from jax.experimental import pallas as pl
from jax.experimental.pallas import tpu as pltpu
from jax.sharding import PartitionSpec as P

KX = 512
KY = 512
NZ = 384
XG = 768
YG = 768
ZG = 576

explicit_step = 0.5
diffuse_buoy = 0.5
diffuse_vel = 0.25
couple_buoy = 0.7
couple_vel = 0.7

ROWS = 16
COLS = 8
A = KX // ROWS
K = KY // COLS
PAIRS = A // 2
LANES = 2 * K
G = 9
PASSES = 3
ZPART = ZG // COLS
ZC = ZPART // G
SIZE = ZC * PAIRS
TWO = 2 * LANES
TALL = 4 * COLS * SIZE
ORDER = (0, 4, 5, 1, 6, 7, 2, 3, 8)
ENDS = (4, 8, 9)
BF = jnp.bfloat16
F32 = jnp.float32
MESH = pl.DeviceIdType.MESH
VMEM_LIMIT = 67_000_000


def trig(modes, points):
    order = np.arange(modes)
    freq = ((order + 1) // 2).astype(np.float32)
    step = np.float32(2.0 * math.pi / points)
    angle = (step * freq)[:, None] * np.arange(points, dtype=np.float32)[None, :]
    angle = angle.astype(np.float64)
    values = np.where((order % 2 == 0)[:, None], np.cos(angle), np.sin(angle))
    return order, values.astype(np.float32)


def fourier_eval(modes, points):
    _, values = trig(modes, points)
    return (values * np.float32(math.sqrt(2.0 / modes))).astype(BF)


def fourier_proj(modes, points):
    order, values = trig(modes, points)
    weight = np.where(order == 0, 1.0 / points, 2.0 / points).astype(np.float32)
    return (values * weight[:, None] * np.float32(math.sqrt(modes / 2.0))).T.astype(BF)


def cheb_tables(degree, points):
    order = np.arange(degree, dtype=np.float32)
    theta = np.float32(math.pi) * (np.arange(points, dtype=np.float32) + np.float32(0.5))
    theta = theta / np.float32(points)
    angle = (order[:, None] * theta[None, :]).astype(np.float64)
    cos, sin = np.cos(angle).astype(np.float32), np.sin(angle).astype(np.float32)
    norm = np.float32(math.sqrt(2.0 / degree))
    weight = np.where(order == 0, 1.0 / points, 2.0 / points).astype(np.float32)
    levels = cos * norm
    slopes = -(order[:, None] / np.float32(degree)) * sin * norm
    projector = (cos * weight[:, None] * np.float32(math.sqrt(degree / 2.0))).T
    return levels.astype(BF), slopes.astype(BF), projector.astype(BF)


def tables():
    levels, slopes, projector = cheb_tables(NZ, ZG)

    def by_chunk(rows):
        return np.asarray(rows).reshape(COLS, ZC, G, NZ).transpose(2, 0, 1, 3).reshape(ZG, NZ)

    lift, slope = (
        by_chunk(np.asarray(t).T).reshape(G, -1, NZ)[list(ORDER)].reshape(PASSES, -1, NZ) for t in (levels, slopes)
    )
    return lift, slope, by_chunk(projector), fourier_eval(KY, YG), np.ascontiguousarray(fourier_proj(KY, YG))


def mm(left, right, dims=((1,), (0,))):
    return lax.dot_general(left, right, (dims, ((), ())), preferred_element_type=F32)


def kernel(
    vel, buoy, lift, slope, drop_in, evals_in, projs_in, strat, eig_val, left_in, right_in,
    out_buoy, out_vel,
    lifted, arrived, planes, passed, folded, tall, wide_eval, wide_proj, eval_x, proj_x, middle, flux, partial,
    inverses, done, done_s, strat_in, drop, evals, projs, eig_left, eig_right, load_s,
    turn_s, turn_r, hop_s, hop_r, colf_s, colf_r, rowf_s, rowf_r, rowb_s, rowb_r, colb_s, colb_r, strat_s, strat_r,
):
    row, col = lax.axis_index("row"), lax.axis_index("col")
    high = row // (ROWS // 2)
    base, low = (col // 2) * 2, col % 2
    part = base + (low + high) % 2

    def col_of(q):
        return (row, (q // 2) * 2 + (q % 2 + high) % 2)

    def row_of(t):
        return (t, base + (low + high + t // (ROWS // 2)) % 2)

    barrier = pltpu.get_barrier_semaphore()

    @pl.loop(1, COLS)
    def _(i):
        pl.semaphore_signal(barrier, inc=1, device_id=col_of((part + i) % COLS), device_id_type=MESH)

    @pl.loop(1, ROWS)
    def _(i):
        pl.semaphore_signal(barrier, inc=1, device_id=row_of((row + i) % ROWS), device_id_type=MESH)

    loads = [
        pltpu.make_async_copy(src, dst, load_s.at[n])
        for n, (src, dst) in enumerate(
            ((evals_in, evals), (projs_in, projs), (drop_in, drop), (left_in, eig_left), (right_in, eig_right))
        )
    ]
    for load in loads:
        load.start()

    def remote(src, dst, send, recv, device):
        return pltpu.make_async_remote_copy(
            src_ref=src, dst_ref=dst, send_sem=send, recv_sem=recv, device_id=device, device_id_type=MESH
        )

    chip, core = row // 2, row % 2

    def col_fwd(g, q):
        return remote(lifted.at[g, q], arrived.at[g, :, col], colf_s.at[g, q], colf_r.at[g, col], col_of(q))

    def col_fwd_in(g, s):
        block = arrived.at[g, :, s]
        return remote(block, block, colf_s.at[g, s], colf_r.at[g, s], col_of(0))

    def col_fwd_own(g):
        return pltpu.make_async_copy(lifted.at[g, part], arrived.at[g, :, col], colf_r.at[g, col])

    def col_back(g, s):
        return remote(passed.at[g, :, s], folded.at[g, part], colb_s.at[g, s], colb_r.at[g, part], (row, s))

    def col_back_in(g, q):
        block = folded.at[g, q]
        return remote(block, block, colb_s.at[g, q], colb_r.at[g, q], col_of(q))

    def col_back_own(g):
        return pltpu.make_async_copy(passed.at[g, :, col], folded.at[g, part], colb_r.at[g, part])

    def others(first, count, do):
        @pl.loop(1, count)
        def _(i):
            do((first + i) % count)

    def row_fwd(g, t):
        m = g // 2
        return remote(arrived.at[g, t // 2], planes.at[m, row], rowf_s.at[m, t], rowf_r.at[m, row], row_of(t))

    def row_fwd_in(m, t):
        block = planes.at[m, t]
        return remote(block, block, rowf_s.at[m, t], rowf_r.at[m, t], row_of(t))

    def row_fwd_own(g):
        m = g // 2
        return pltpu.make_async_copy(arrived.at[g, chip], planes.at[m, row], rowf_r.at[m, row])

    def row_back(m, g, t):
        return remote(planes.at[m, t], passed.at[g, chip], rowb_s.at[m, t], rowb_r.at[g, chip], row_of(t))

    def row_back_in(g, t):
        block = passed.at[g, t // 2]
        return remote(block, block, rowb_s.at[0, t], rowb_r.at[g, t // 2], row_of(t))

    def row_back_own(m, g):
        return pltpu.make_async_copy(planes.at[m, row], passed.at[g, chip], rowb_r.at[g, chip])

    def chips(side, here, there):
        @pl.loop(0, ZC)
        def _(i):
            t = ((chip + i) % ZC) * 2 + side
            pl.when(t == row)(lambda: here())
            pl.when(t != row)(lambda: there(t))

    def members(here, there):
        chips(core, here, there)
        chips(1 - core, here, there)

    def turn_out(g, t):
        m = g // 2
        return remote(
            lifted.at[g, t // 2], arrived.at[2 * m + high, row % 8], turn_s.at[g - 4, t // 2], turn_r.at[m - 2, row], row_of(t)
        )

    def turn_own(g):
        m = g // 2
        return pltpu.make_async_copy(lifted.at[g, chip], arrived.at[2 * m + high, row % 8], turn_r.at[m - 2, row])

    def turn_in(m, t):
        block = arrived.at[2 * m + t // 8, t % 8]
        return remote(block, block, turn_s.at[0, 0], turn_r.at[m - 2, t], row_of(t))

    def landing(m, h, s):
        return planes.at[m, h * 8 : (h + 1) * 8, (s // 2) * 2 + (s % 2 + high + h) % 2]

    def hop(m, h, q):
        return remote(
            arrived.at[2 * m + h, :, q], landing(m, h, col), hop_s.at[m - 2, h, q], hop_r.at[m - 2, h, col], col_of(q)
        )

    def hop_in(m, h, s):
        return remote(landing(m, h, s), landing(m, h, s), hop_s.at[m - 2, h, s], hop_r.at[m - 2, h, s], col_of(0))

    def hop_own(m, h):
        return pltpu.make_async_copy(arrived.at[2 * m + h, :, part], landing(m, h, col), hop_r.at[m - 2, h, col])

    def relay_turned(m):
        members(lambda: turn_own(2 * m).wait(), lambda t: turn_in(m, t).wait_recv())
        for h in range(2):
            others(part, COLS, lambda q: hop(m, h, q).start())
            hop_own(m, h).start()

    def relay_fwd(g):
        others(col, COLS, lambda s: col_fwd_in(g, s).wait_recv())
        col_fwd_own(g).wait()

        chips(g % 2, lambda: row_fwd_own(g).start(), lambda t: row_fwd(g, t).start())

    def relay_back(g):
        chips(g % 2, lambda: row_back_own(0, g).wait(), lambda t: row_back_in(g, t).wait_recv())
        others(col, COLS, lambda s: col_back(g, s).start())
        col_back_own(g).start()

    count = ZG // PASSES
    chunks = G // PASSES

    def chunk_at(i):
        late = jnp.where(i < 6, i + 2, jnp.where(i < 8, i - 4, 8))
        return jnp.where(i == 0, 0, jnp.where(i < 3, i + 3, jnp.where(i == 3, 1, late)))

    def to_points(u):
        for f, (table, field) in enumerate(((lift, vel), (slope, buoy))):

            @pl.loop(0, PAIRS // 2)
            def _(p):
                rows = pl.ds(pl.multiple_of(p * TWO, TWO), TWO)
                values = mm(table[u], field[rows, :], ((1,), (1,)))
                tall[pl.ds(2 * p, count, stride=PAIRS), :] = values[:, :LANES]
                tall[pl.ds(2 * p + 1, count, stride=PAIRS), :] = values[:, LANES:]

            @pl.loop(0, COLS * chunks)
            def _(i):
                rows = pl.ds(pl.multiple_of(i * SIZE, SIZE), SIZE)
                block = tall[rows, :].astype(BF).reshape(ZC, PAIRS, LANES)
                g, q = chunk_at(u * chunks + i // COLS), i % COLS

                @pl.when(g // 4 != 1)
                def _():
                    lifted[g, q, :, f] = block

                @pl.when(g // 4 == 1)
                def _():
                    lifted[g, :, q, f] = block

    def send_points(u):
        @pl.loop(u * chunks, (u + 1) * chunks)
        def _(i):
            g = chunk_at(i)

            @pl.when(g // 4 != 1)
            def _():
                others(part, COLS, lambda q: col_fwd(g, q).start())
                col_fwd_own(g).start()

            @pl.when(g // 4 == 1)
            def _():
                chips(g % 2, lambda: turn_own(g).start(), lambda t: turn_out(g, t).start())

    to_points(0)
    pl.semaphore_wait(barrier, COLS + ROWS - 2)
    send_points(0)
    swap = remote(strat, strat_in, strat_s, strat_r, (row, base + 1 - low))
    swap.start()

    @pl.loop(1, PASSES)
    def _(u):
        to_points(u)
        send_points(u)

    for load in loads:
        load.wait()

    @pl.loop(0, COLS)
    def _(s):
        for a in range(2):
            own = pl.ds(pl.multiple_of(s * LANES + a * K, K), K)
            other = pl.ds(pl.multiple_of(s * LANES + (1 - a) * K, K), K)
            wide_eval[a, own, :] = evals[pl.ds(pl.multiple_of(s * K, K), K), :]
            wide_eval[a, other, :] = jnp.zeros((K, YG), BF)

    relay_fwd(0)

    lane = lax.broadcasted_iota(jnp.int32, (LANES, LANES), 1)

    @pl.loop(0, YG // LANES)
    def _(i):
        for j in range(COLS // 2):
            rows = pl.ds(pl.multiple_of(i * LANES, LANES), LANES)
            tile = projs[rows, j * LANES : (j + 1) * LANES].astype(F32)
            turned = pltpu.roll(tile, K, 1)
            for s in (2 * j, 2 * j + 1):
                straight, moved = (tile, turned) if s % 2 == 0 else (turned, tile)
                for a in range(2):
                    keep = jnp.where((lane < K) == (a == 0), straight if a == 0 else moved, 0.0).astype(BF)
                    to = pl.ds(pl.multiple_of(a * YG + i * LANES, LANES), LANES)
                    wide_proj[to, s * LANES : (s + 1) * LANES] = keep

    relay_fwd(1)

    @pl.loop(0, XG // LANES)
    def _(j):
        points = pl.ds(pl.multiple_of(j * LANES, LANES), LANES)

        def ordered(values):
            tall[:KX, :] = values
            return jnp.concatenate([tall[pl.ds(a, KX // 2, stride=2), :] for a in range(2)], axis=0)

        eval_x[points, :] = ordered(evals[:, points].astype(F32)).T.astype(BF)
        proj_x[:, points] = ordered(projs[points, :].astype(F32).T).astype(BF)

    relay_fwd(2)

    def diagonals(p):
        place = p * TWO + lax.broadcasted_iota(jnp.int32, (TWO, LANES), 0)
        freq_x = ((row * A + (place >> 6) + 1) >> 1).astype(F32) * (2.0 / KX)
        freq_y = ((col * K + (place & (K - 1)) + 1) >> 1).astype(F32) * (2.0 / KY)
        wave = 4.0 * (freq_x * freq_x + freq_y * freq_y)
        lapl = jnp.concatenate([wave] * (NZ // LANES), axis=1) + eig_val[...].reshape(1, NZ)
        return 1.0 + diffuse_buoy * lapl, 1.0 + diffuse_vel * lapl

    @pl.loop(0, PAIRS // 2)
    def _(p):
        rows = pl.ds(pl.multiple_of(p * TWO, TWO), TWO)
        diag_buoy, diag_vel = diagonals(p)
        inverses[rows, :] = 1.0 / (diag_buoy * diag_vel + couple_buoy * couple_vel)

    def result(f, p):
        rows = pl.ds(pl.multiple_of(p * TWO, TWO), TWO)
        return pltpu.make_async_copy(done.at[f, rows, :], (out_buoy, out_vel)[f].at[rows, :], done_s.at[f, p])

    @pl.loop(2, 4)
    def _(m):
        relay_turned(m)
        pl.when(m == 2)(lambda: relay_fwd(3))

    swap.wait()
    strata = jnp.where(high == 0, strat[...], strat_in[...]).reshape(1, ZPART)
    level_of = lax.broadcasted_iota(jnp.int32, (1, ZPART), 1)

    half = KX // 2
    last = G // 2

    @pl.loop(0, last + 1 - core)
    def _(m):
        chunk = 2 * m + core

        pl.when(m == last - 1)(lambda: pl.loop(0, 2)(relay_back))

        @pl.when(m // 2 != 1)
        def _():
            members(lambda: row_fwd_own(2 * m).wait(), lambda t: row_fwd_in(m, t).wait_recv())

        @pl.when(m // 2 == 1)
        def _():
            for h in range(2):
                others(col, COLS, lambda s: hop_in(m, h, s).wait_recv())
                hop_own(m, h).wait()

        for f in range(2):
            left = jnp.concatenate([planes[m, :, s, f].reshape(half, LANES) for s in range(COLS)], axis=1)
            for a in range(2):
                middle[a * half : (a + 1) * half, f * YG : (f + 1) * YG] = mm(left, wide_eval[a]).astype(BF)

        pl.when(m == 0)(lambda: relay_fwd(G - 1))

        level = jnp.sum(jnp.where(level_of == chip * G + chunk, strata, 0.0), axis=1, keepdims=True)
        tile = XG // 3

        @pl.loop(0, 3)
        def _(x):
            rows = pl.ds(pl.multiple_of(x * tile, tile), tile)
            velocity = mm(eval_x[rows, :], middle[:, :YG]).astype(BF).astype(F32)
            gradient = mm(eval_x[rows, :], middle[:, YG:]).astype(BF).astype(F32)
            flux[rows, :YG] = (-(velocity * gradient) - level * velocity).astype(BF)
            flux[rows, YG:] = (-(velocity * jnp.abs(velocity))).astype(BF)


        @pl.loop(0, 2)
        def _(a):
            rows = pl.ds(pl.multiple_of(a * half, half), half)
            for f in range(2):
                middle[rows, f * YG : (f + 1) * YG] = mm(proj_x[rows, :], flux[:, f * YG : (f + 1) * YG]).astype(BF)
        for f in range(2):
            left = jnp.concatenate(
                [middle[a * half : (a + 1) * half, f * YG : (f + 1) * YG] for a in range(2)], axis=1
            )
            values = mm(left, wide_proj[...]).astype(BF)
            for s in range(COLS):
                planes[m, :, s, f] = values[:, s * LANES : (s + 1) * LANES].reshape(ROWS, PAIRS, LANES)

        members(lambda: row_back_own(m, chunk).start(), lambda t: row_back(m, chunk, t).start())

        @pl.when(m == last - 1)
        def _():
            pl.loop(2, 4)(relay_back)

    def gather(first, last, f, start):
        @pl.loop(first, last)
        def _(g):
            for q in range(COLS):
                place = pl.multiple_of(start + ((g - first) * COLS + q) * SIZE, SIZE)
                tall[pl.ds(place, SIZE), :] = folded[g, q, :, f].reshape(SIZE, LANES).astype(F32)

    def tendency(first, last, p, start):
        count = (last - first) * COLS * ZC
        columns = [tall[pl.ds(start + 2 * p + a, count, stride=PAIRS), :].astype(BF) for a in range(2)]
        rows = slice(first * COLS * ZC, last * COLS * ZC)
        return mm(jnp.concatenate(columns, axis=1), drop[rows, :], ((0,), (0,)))

    def wait_modes(first, last):
        @pl.loop(first, last)
        def _(g):
            others(part, COLS, lambda q: col_back_in(g, q).wait_recv())
            col_back_own(g).wait()

    pl.loop(4, G - 1)(relay_back)
    wait_modes(0, ENDS[0])
    for f in range(2):
        gather(0, ENDS[0], f, 0)

        @pl.loop(0, PAIRS // 2)
        def _(p):
            rows = pl.ds(pl.multiple_of(p * TWO, TWO), TWO)
            partial[f, rows, :] = tendency(0, ENDS[0], p, 0)

    relay_back(G - 1)
    wait_modes(ENDS[0], ENDS[1])
    for f in range(2):
        gather(ENDS[0], ENDS[1], f, 0)

        @pl.loop(0, PAIRS // 2)
        def _(p):
            rows = pl.ds(pl.multiple_of(p * TWO, TWO), TWO)
            partial[f, rows, :] += tendency(ENDS[0], ENDS[1], p, 0)

    wait_modes(ENDS[1], G)
    start = (G - ENDS[1]) * COLS * SIZE
    for f in range(2):
        gather(ENDS[1], G, f, f * start)

    @pl.loop(0, PAIRS // 2)
    def _(p):
        rows = pl.ds(pl.multiple_of(p * TWO, TWO), TWO)
        modal = []
        for f, field in enumerate((buoy, vel)):
            tend = partial[f, rows, :] + tendency(ENDS[1], G, p, f * start)
            rhs = (field[rows, :].astype(F32) + explicit_step * tend).astype(BF)
            modal.append(mm(rhs, eig_left[...]))
        modal_buoy, modal_vel = modal
        diag_buoy, diag_vel = diagonals(p)
        inverse = inverses[rows, :]
        solved_buoy = ((diag_vel * modal_buoy - couple_buoy * modal_vel) * inverse).astype(BF)
        solved_vel = ((diag_buoy * modal_vel + couple_vel * modal_buoy) * inverse).astype(BF)
        done[0, rows, :] = mm(solved_buoy, eig_right[...]).astype(BF)
        done[1, rows, :] = mm(solved_vel, eig_right[...]).astype(BF)
        result(0, p).start()
        result(1, p).start()

    @pl.loop(0, PAIRS // 2)
    def _(p):
        result(0, p).wait()
        result(1, p).wait()

    def nothing():
        pass

    @pl.loop(2, 4)
    def _(m):
        for h in range(2):
            others(part, COLS, lambda q: hop(m, h, q).wait_send())

    @pl.loop(0, G)
    def _(g):
        @pl.when(g // 4 != 1)
        def _():
            others(part, COLS, lambda q: col_fwd(g, q).wait_send())

        @pl.when(g // 4 == 1)
        def _():
            chips(g % 2, nothing, lambda t: turn_out(g, t).wait_send())

        others(col, COLS, lambda s: col_back(g, s).wait_send())

    @pl.loop(0, last)
    def _(m):
        pl.when(m // 2 != 1)(lambda: members(nothing, lambda t: row_fwd(2 * m, t).wait_send()))

    @pl.loop(0, last + 1 - core)
    def _(m):
        members(nothing, lambda t: row_back(m, 2 * m, t).wait_send())

    chips(0, nothing, lambda t: row_fwd(G - 1, t).wait_send())


def per_device(buoy, vel_w, strat, eig_val, eig_left, eig_right):
    modes = A * K
    dma = pltpu.SemaphoreType.DMA
    vmem = pl.BlockSpec(memory_space=pltpu.VMEM)
    hbm = pl.BlockSpec(memory_space=pl.ANY)
    shape = jax.ShapeDtypeStruct((modes, NZ), BF)
    consts = [jnp.asarray(t) for t in tables()]
    new_buoy, new_vel = pl.pallas_call(
        kernel,
        out_shape=(shape, shape),
        in_specs=[vmem] * 4 + [hbm] * 3 + [vmem] * 2 + [hbm] * 2,
        out_specs=(hbm, hbm),
        scratch_shapes=[
            pltpu.VMEM((G, COLS, ZC, 2, PAIRS, LANES), BF),
            pltpu.VMEM((G, ZC, COLS, 2, PAIRS, LANES), BF),
            pltpu.VMEM((G // 2 + 1, ROWS, COLS, 2, PAIRS, LANES), BF),
            pltpu.VMEM((G, ZC, COLS, 2, PAIRS, LANES), BF),
            pltpu.VMEM((G, COLS, ZC, 2, PAIRS, LANES), BF),
            pltpu.VMEM((TALL, LANES), F32),
            pltpu.VMEM((2, COLS * LANES, YG), BF),
            pltpu.VMEM((2 * YG, COLS * LANES), BF),
            pltpu.VMEM((XG, KX), BF),
            pltpu.VMEM((KX, XG), BF),
            pltpu.VMEM((KX, 2 * YG), BF),
            pltpu.VMEM((XG, 2 * YG), BF),
            pltpu.VMEM((2, modes, NZ), F32),
            pltpu.VMEM((modes, NZ), F32),
            pltpu.VMEM((2, modes, NZ), BF),
            dma((2, PAIRS // 2)),
            pltpu.VMEM((ZPART,), F32),
            pltpu.VMEM((ZG, NZ), BF),
            pltpu.VMEM((KY, YG), BF),
            pltpu.VMEM((YG, KY), BF),
            pltpu.VMEM((NZ, NZ), BF),
            pltpu.VMEM((NZ, NZ), BF),
            dma((5,)), dma((4, ZC)), dma((2, ROWS)), dma((2, 2, COLS)), dma((2, 2, COLS)),
            dma((G, COLS)), dma((G, COLS)), dma((G // 2 + 1, ROWS)), dma((G // 2 + 1, ROWS)),
            dma((G // 2 + 1, ROWS)), dma((G, ZC)), dma((G, COLS)), dma((G, COLS)),
            dma, dma,
        ],
        compiler_params=pltpu.CompilerParams(
            collective_id=0, has_side_effects=True, vmem_limit_bytes=VMEM_LIMIT
        ),
        name="section",
    )(
        vel_w.reshape(modes, NZ), buoy.reshape(modes, NZ), *consts, strat, eig_val, eig_left, eig_right
    )
    return new_buoy.reshape(buoy.shape), new_vel.reshape(buoy.shape)


def solution(mesh):
    in_specs = (P("row", "col", None), P("row", "col", None), P("col"), P(), P(), P())
    out_specs = (P("row", "col", None), P("row", "col", None))
    return jax.shard_map(
        per_device, mesh=mesh, in_specs=in_specs, out_specs=out_specs, check_vma=False
    )
```
